256 devices in a mesh: strip: 8 (over y, core), cell: 32 (over x, z).
Axes of the slice: x: 4, y: 4, z: 8, core: 2. Of those that a mesh axis runs over, the one named last changes fastest.
Arguments:
- features: bfloat16 [65536, 256], P(('strip', 'cell')), may hold values from -6 to 6
- pair_atom: int32 [1048576], P(('strip', 'cell')), may hold values from 0 to 255
- partner_row: int32 [1048576], P(('strip', 'cell')), may hold values from 0 to 1535, as said below
- transpose_slot: int32 [1048576], P(('strip', 'cell')), may hold values from 0 to 6143, as said below
- distance: float32 [1048576], P(('strip', 'cell')), may hold values from 1 to 8
- send_rows: int32 [8192, 48], P(('strip', 'cell')), may hold values from 0 to 767, as said below
- w_left: bfloat16 [256, 256], replicated, may hold values from -0.375 to 0.375
- w_right: bfloat16 [256, 256], replicated, may hold values from -0.375 to 0.375
- w_radial_in: bfloat16 [128, 256], replicated, may hold values from -4 to 4
- w_radial_out: bfloat16 [256, 256], replicated, may hold values from -0.375 to 0.375
- w_mix: bfloat16 [256, 256], replicated, may hold values from -0.375 to 0.375
- w_out: bfloat16 [256, 169], replicated, may hold values from -0.375 to 0.375
Outputs:
- own_blocks: bfloat16 [169, 1048576], P(None, ('strip', 'cell'))
- partner_blocks: bfloat16 [169, 1572864], P(None, ('strip', 'cell'))
The draws below stay inside these ranges and needn't reach their ends.
Inputs may be any that keep to these rules, and one draw needn't show every extreme that they name: `transpose_slot`: within one device the values are distinct; at most 64 of them share t // 64, and on every device one such group holds exactly 64. For pair slot p with transpose_slot t: partner_row // 48 equals (t // 64) % 32, and partner_row % 3 equals t // 2048. `send_rows`: entry k lies in [(k % 3) * 256, (k % 3 + 1) * 256); part k % 3 names the device of strip s - 1, s, s + 1 (cyclic) with the same cell index.
All inputs are finite; a program needn't handle non-finite values.
Results may differ from the reference program's by a relative error of at most 0.0084.
Values may be sent and summed in bfloat16 or wider, within the bound.
A program may use at most 64 MiB of HBM per device.

```python
import jax
import jax.numpy as jnp
import numpy as np
from jax import lax

D = 256
RB = 128
ORB = 13
BLOCK = 169
A_DEV = 256
PAIRS_DEV = 4096
FETCH = 48
SLOT = 64
RECV_DEV = 6144
ATOMS = 65536
PAIRS = 1048576
SEND_LISTS = 8192
N_STRIP = 8
N_CELL = 32
DEVICES = 256


def pair_tables(key):
    groups = RECV_DEV // SLOT

    def one_device(dev_key):
        first_key, second_key, third_key = jax.random.split(dev_key, 3)
        full_group = jax.random.randint(first_key, (), 0, groups)
        shuffled = jax.random.permutation(second_key, RECV_DEV).astype(jnp.int32)
        slot_group = jnp.arange(RECV_DEV, dtype=jnp.int32) // SLOT
        score = jnp.where(slot_group == full_group, 0, RECV_DEV) + shuffled
        chosen = jnp.argsort(score)[:PAIRS_DEV].astype(jnp.int32)
        offset = chosen // (RECV_DEV // 3)
        source = chosen // SLOT % (groups // 3)
        pick = jax.random.randint(third_key, (PAIRS_DEV,), 0, FETCH // 3)
        return (chosen, (source * FETCH + 3 * pick + offset).astype(jnp.int32))
    keys = jax.random.split(jax.random.fold_in(key, 7), DEVICES)
    return jax.vmap(one_device)(keys)


def draw_transpose_slot(key, part):
    return pair_tables(key)[0].reshape(-1)


def draw_partner_row(key, part):
    return pair_tables(key)[1].reshape(-1)


def draw_send_rows(key, part):
    atom = jax.random.randint(jax.random.fold_in(key, 11), (SEND_LISTS, FETCH), 0, A_DEV)
    return ((jnp.arange(FETCH, dtype=jnp.int32) % 3)[None, :] * A_DEV + atom).astype(jnp.int32)


def place_ends(drawn, stream_key, low, top_value):
    extent = drawn.shape
    place = [jax.random.randint(jax.random.fold_in(stream_key, axis), (), 0, extent[axis]) for axis in range(len(extent))]
    drawn = drawn.at[tuple(place)].set(low)
    longest = extent.index(max(extent))
    place[longest] = (place[longest] + 1) % extent[longest]
    return drawn.at[tuple(place)].set(top_value)


def levels(rng, extent, pieces, smallest, high):
    level, own = 1.0, jax.random.fold_in(rng, 6)
    for dim, blocks in pieces:
        draws = jnp.exp(jax.random.uniform(jax.random.fold_in(own, dim), (blocks,), jnp.float32, smallest / len(pieces), high / len(pieces)))
        level = level * jnp.repeat(draws, extent[dim] // blocks).reshape([-1 if axis == dim else 1 for axis in range(len(extent))])
    return level


def scatter_about(own_key, dims, spread, bound, cuts=(), kind=jnp.bfloat16):
    loudness = levels(own_key, dims, cuts, -0.22, 0.18) if cuts else 1.0
    drawn = jax.random.normal(own_key, dims, jnp.float32) * spread * loudness
    return jnp.minimum(jnp.maximum(drawn, -bound), bound).astype(kind)


def setup_inputs(seed: int = 0) -> dict:
    key_of = jax.random.split(jax.random.key(seed), 13)
    features = scatter_about(key_of[0], (ATOMS, D), 1.0, 6.0, ((0, 256),))
    pair_atom = place_ends(jax.random.randint(key_of[1], (PAIRS,), 0, A_DEV), jax.random.fold_in(key_of[1], 1), 0, A_DEV - 1).astype(jnp.int32)
    partner_row = draw_partner_row(jax.random.fold_in(key_of[12], 71), 0)
    transpose_slot = draw_transpose_slot(jax.random.fold_in(key_of[12], 71), 0)
    distance = jnp.clip(1.0 + 7.0 * jax.random.uniform(key_of[4], (PAIRS,), jnp.float32) ** levels(key_of[4], (PAIRS,), ((0, 256),), -0.2, 0.2), 1.0, 8.0)
    send_rows = draw_send_rows(jax.random.fold_in(key_of[12], 71), 0)
    w_left = scatter_about(key_of[6], (D, D), D ** -0.5, 0.375)
    w_right = scatter_about(key_of[7], (D, D), D ** -0.5, 0.375)
    w_radial_in = scatter_about(key_of[8], (RB, D), 2 ** -0.5, 4.0)
    w_radial_out = scatter_about(key_of[9], (D, D), D ** -0.5, 0.375)
    w_mix = scatter_about(key_of[10], (D, D), D ** -0.5, 0.375)
    w_out = scatter_about(key_of[11], (D, BLOCK), D ** -0.5, 0.375)
    return dict(features=features, pair_atom=pair_atom, partner_row=partner_row, transpose_slot=transpose_slot, distance=distance, send_rows=send_rows, w_left=w_left, w_right=w_right, w_radial_in=w_radial_in, w_radial_out=w_radial_out, w_mix=w_mix, w_out=w_out)


cutoff = 8.0


def radial_basis(distance, count):
    centers = jnp.arange(count, dtype=jnp.float32) * (cutoff / (count - 1))
    spacing = 2.0 * cutoff / count
    scaled = (distance[:, None] - centers[None, :]) / spacing
    envelope = 0.5 * (jnp.cos(jnp.pi * distance / cutoff) + 1.0)
    return (jnp.exp(-scaled * scaled) * envelope[:, None]).astype(jnp.bfloat16)


def pair_blocks(left_rows, right_rows, distance, w_radial_in, w_radial_out, w_mix, w_out):
    basis = radial_basis(distance, w_radial_in.shape[0])
    radial = jax.nn.silu(jnp.dot(basis, w_radial_in, preferred_element_type=jnp.float32)).astype(jnp.bfloat16)
    gate = jnp.dot(radial, w_radial_out, preferred_element_type=jnp.float32)
    edge = (left_rows.astype(jnp.float32) * right_rows.astype(jnp.float32) * gate).astype(jnp.bfloat16)
    mixed = jax.nn.silu(jnp.dot(edge, w_mix, preferred_element_type=jnp.float32)).astype(jnp.bfloat16)
    return lax.dot_general(w_out, mixed, (((0,), (1,)), ((), ())), preferred_element_type=jnp.float32).astype(jnp.bfloat16)


def reference(features, pair_atom, partner_row, transpose_slot, distance, send_rows, w_left, w_right, w_radial_in, w_radial_out, w_mix, w_out):
    devices = N_STRIP * N_CELL
    left_all = jnp.dot(features, w_left, preferred_element_type=jnp.float32).astype(jnp.bfloat16).reshape(N_STRIP, N_CELL, A_DEV, D)
    right_all = jnp.dot(features, w_right, preferred_element_type=jnp.float32).astype(jnp.bfloat16).reshape(N_STRIP, N_CELL, A_DEV, D)
    lists = send_rows.reshape(N_STRIP, N_CELL, N_CELL, FETCH)
    atoms = pair_atom.reshape(devices, PAIRS_DEV)
    partners = partner_row.reshape(devices, PAIRS_DEV)
    spans = distance.reshape(devices, PAIRS_DEV)

    def one_device(index):
        strip_index = index // N_CELL
        column = index % N_CELL
        rows = partners[index]
        source = rows // FETCH
        within = rows % FETCH
        entry = lists[strip_index, source, column, within]
        src_strip = (strip_index + entry // A_DEV - 1) % N_STRIP
        right_rows = right_all[src_strip, source, entry % A_DEV]
        left_rows = left_all[strip_index, column][atoms[index]]
        return pair_blocks(left_rows, right_rows, spans[index], w_radial_in, w_radial_out, w_mix, w_out)

    own_dev = lax.map(one_device, jnp.arange(devices, dtype=jnp.int32))
    own_blocks = own_dev.transpose(1, 0, 2).reshape(BLOCK, devices * PAIRS_DEV)
    order = np.arange(BLOCK).reshape(ORB, ORB).T.reshape(-1)
    flipped = own_blocks[order]
    slots = transpose_slot.reshape(devices, PAIRS_DEV)
    sender = jnp.arange(devices, dtype=jnp.int32)[:, None]
    send_strip = sender // N_CELL
    send_cell = sender % N_CELL
    offset = slots // (N_CELL * SLOT)
    target = (slots // SLOT) % N_CELL
    within_slot = slots % SLOT
    receiver = ((send_strip + offset - 1) % N_STRIP) * N_CELL + target
    columns = receiver * RECV_DEV + offset * (N_CELL * SLOT) + send_cell * SLOT + within_slot
    partner_blocks = jnp.zeros((BLOCK, devices * RECV_DEV), jnp.bfloat16).at[:, columns.reshape(-1).astype(jnp.int32)].set(flipped)
    return own_blocks, partner_blocks
```

```python
import jax
import jax.numpy as jnp
import numpy as np
from jax import lax
from jax.sharding import PartitionSpec as P

cutoff = 8.0


def passed_along(x, axis, by):
    peers = lax.axis_size(axis)
    return lax.ppermute(x, axis, [(i, (i + by) % peers) for i in range(peers)])


def radial_basis(distance, count):
    centers = jnp.arange(count, dtype=jnp.float32) * (cutoff / (count - 1))
    spacing = 2.0 * cutoff / count
    scaled = (distance[:, None] - centers[None, :]) / spacing
    envelope = 0.5 * (jnp.cos(jnp.pi * distance / cutoff) + 1.0)
    return (jnp.exp(-scaled * scaled) * envelope[:, None]).astype(jnp.bfloat16)


def select_rows(index, table):
    picker = (index[:, None] == jnp.arange(table.shape[0], dtype=jnp.int32)[None, :]).astype(
        jnp.bfloat16
    )
    return jnp.dot(picker, table, preferred_element_type=jnp.float32).astype(jnp.bfloat16)


def body(
    features,
    pair_atom,
    partner_row,
    transpose_slot,
    distance,
    send_rows,
    w_left,
    w_right,
    w_radial_in,
    w_radial_out,
    w_mix,
    w_out,
):
    width = features.shape[1]
    cells = lax.axis_size("cell")
    left = jnp.dot(features, w_left, preferred_element_type=jnp.float32).astype(jnp.bfloat16)
    right_own = jnp.dot(features, w_right, preferred_element_type=jnp.float32).astype(jnp.bfloat16)
    tables = jnp.concatenate(
        [passed_along(right_own, "strip", 1), right_own, passed_along(right_own, "strip", -1)], axis=0
    )
    chosen = select_rows(send_rows.reshape(-1), tables)
    right = lax.all_to_all(
        chosen.reshape(cells, -1, width), "cell", split_axis=0, concat_axis=0, tiled=True
    ).reshape(-1, width)
    left_rows = select_rows(pair_atom, left)
    right_rows = select_rows(partner_row, right)
    basis = radial_basis(distance, w_radial_in.shape[0])
    radial = jax.nn.silu(jnp.dot(basis, w_radial_in, preferred_element_type=jnp.float32)).astype(
        jnp.bfloat16
    )
    gate = jnp.dot(radial, w_radial_out, preferred_element_type=jnp.float32)
    edge = (left_rows.astype(jnp.float32) * right_rows.astype(jnp.float32) * gate).astype(
        jnp.bfloat16
    )
    mixed = jax.nn.silu(jnp.dot(edge, w_mix, preferred_element_type=jnp.float32)).astype(
        jnp.bfloat16
    )
    own_blocks = lax.dot_general(
        w_out, mixed, (((0,), (1,)), ((), ())), preferred_element_type=jnp.float32
    ).astype(jnp.bfloat16)
    entries = w_out.shape[1]
    orbitals = int(np.sqrt(entries) + 0.5)
    order = np.arange(entries).reshape(orbitals, orbitals).T.reshape(-1)
    w_flipped = w_out[:, order]
    slot_total = 3 * cells * (pair_atom.shape[0] // (2 * cells))
    placed = jnp.zeros((slot_total, width), jnp.bfloat16).at[transpose_slot].set(mixed)
    outbox = lax.dot_general(
        w_flipped, placed, (((0,), (1,)), ((), ())), preferred_element_type=jnp.float32
    ).astype(jnp.bfloat16)
    outbox = outbox.reshape(entries, 3, slot_total // 3)
    arrived = lax.all_to_all(outbox, "cell", split_axis=2, concat_axis=2, tiled=True)
    pieces = [None, arrived[:, 1], None]
    for which, offset in ((0, -1), (2, 1)):
        pieces[which] = passed_along(arrived[:, which], "strip", offset)
    gathered = jnp.stack(pieces, 1)
    partner_blocks = gathered.reshape(entries, slot_total)
    return (own_blocks, partner_blocks)


def solution(mesh):
    in_specs = (
        P(("strip", "cell"), None),
        P(("strip", "cell")),
        P(("strip", "cell")),
        P(("strip", "cell")),
        P(("strip", "cell")),
        P(("strip", "cell"), None),
        P(),
        P(),
        P(),
        P(),
        P(),
        P(),
    )
    out_specs = (P(None, ("strip", "cell")), P(None, ("strip", "cell")))
    return jax.shard_map(body, mesh=mesh, in_specs=in_specs, out_specs=out_specs, check_vma=False)
```

```python
import functools

import jax
import jax.numpy as jnp
import numpy as np
from jax import lax
from jax.experimental import pallas as pl
from jax.experimental.pallas import tpu as pltpu
from jax.sharding import PartitionSpec as P

MESH = pl.DeviceIdType.MESH
F32 = jnp.float32
BF16 = jnp.bfloat16
D = 256
BLOCK = 169
ORB = 13
HALF = 88
FETCH = 48
SLOT = 64
CELLS = 32
STRIPS = 8
Z = 8
X = 4
PAIRS = 4096
GROUPS = 96
CUTOFF = 8.0
COUNT = 128


def silu(x):
    half = 0.5 * x
    return half + half * jnp.tanh(half)


def offset_of(k):
    j = lax.div(k, 4)
    hop = lax.div(j + 1, 2) * (2 * lax.rem(j, 2) - 1)
    return lax.rem(k, 4), hop


def cell_at(k, sign):
    c = lax.axis_index("cell")
    dx, dz = offset_of(k)
    x = lax.rem(lax.div(c, Z) + sign * dx + X, X)
    z = lax.rem(lax.rem(c, Z) + sign * dz + Z, Z)
    return x * Z + z


def strip_at(step):
    return lax.rem(lax.axis_index("strip") + step + STRIPS, STRIPS)


def column(values, lane):
    lanes = lax.broadcasted_iota(jnp.int32, values.shape, 1)
    return jnp.sum(jnp.where(lanes == lane, values, 0.0), axis=1, keepdims=True)


def one_hot(index, width):
    lanes = lax.broadcasted_iota(jnp.int32, (index.shape[0], width), 1)
    return jnp.where(lanes == index.astype(jnp.int32), 1.0, 0.0).astype(BF16)


def dot(a, b):
    return jnp.dot(a, b, preferred_element_type=F32)


def dot_nt(a, b):
    return lax.dot_general(a, b, (((1,), (1,)), ((), ())), preferred_element_type=F32)


def envelope_of(distance):
    return 0.5 * (jnp.cos(jnp.pi * distance / CUTOFF) + 1.0)


def gate_of(distance, envelope, w_in, w_out):
    centers = lax.broadcasted_iota(jnp.int32, (1, COUNT), 1).astype(F32) * (CUTOFF / (COUNT - 1))
    scaled = (distance - centers) * (COUNT / (2.0 * CUTOFF))
    basis = (jnp.exp(-scaled * scaled) * envelope).astype(BF16)
    radial = silu(dot(basis, w_in)).astype(BF16)
    return dot(radial, w_out)


def main_kernel(
    feat, atom, prow, slot, dist, lists, w_left, w_right, w_rin, w_rout, w_mix, w_out,
    own, blk_in,
    feat_in, tables, left, rows_out, rows_in, gate_s, gate_o, blk_out,
    slot_d, slot_e, slot_a, slot_m, pair_d, pair_e, pair_a, pair_r, list_t,
    square, w_pad, w_own, w_flip,
    feat_ss, feat_rs, rows_ss, rows_rs, blk_ss, blk_rs, local_sem,
):
    me = lax.axis_index("cell")
    barrier = pltpu.get_barrier_semaphore()

    def greet(k, _):
        c = cell_at(k, 1)
        for step in (-1, 0, 1):
            if step:
                pl.semaphore_signal(barrier, inc=1, device_id=(strip_at(step), c), device_id_type=MESH)
            else:
                @pl.when(k > 0)
                def _():
                    pl.semaphore_signal(barrier, inc=1, device_id=(strip_at(0), c), device_id_type=MESH)
        return 0

    lax.fori_loop(0, CELLS, greet, 0)

    left[...] = dot(feat[...], w_left[...]).astype(BF16)
    tables[pl.ds(D, D), :] = dot(feat[...], w_right[...]).astype(BF16)

    w_pad[...] = jnp.zeros_like(w_pad)
    w_pad[:, 0:BLOCK] = w_out[...]
    entry = lax.broadcasted_iota(jnp.int32, (2 * HALF, D), 0)
    lane = lax.broadcasted_iota(jnp.int32, (2 * HALF, D), 1)
    quotient = lax.shift_right_logical(entry * 79, 10)
    flipped = (entry - quotient * ORB) * ORB + quotient
    keep = entry < BLOCK
    w_own[...] = dot_nt(jnp.where(keep & (lane == entry), 1.0, 0.0).astype(BF16), w_pad[...]).astype(BF16)
    w_flip[...] = dot_nt(jnp.where(keep & (lane == flipped), 1.0, 0.0).astype(BF16), w_pad[...]).astype(BF16)

    def place(j, total):
        left_parts, right_parts = [], []
        for h in range(2):
            at = pl.ds(2 * j + h, 1)
            t = slot[at, :]
            d = dist[at, :]
            d_hi = d.astype(BF16).astype(F32)
            d_mid = (d - d_hi).astype(BF16).astype(F32)
            d_lo = d - d_hi - d_mid
            k = prow[at, :] - FETCH * (lax.shift_right_logical(t, 6) & (CELLS - 1))
            hit = lax.broadcasted_iota(jnp.int32, (SLOT, 128), 0) == (t & (SLOT - 1))
            parts = (d_hi, d_mid, d_lo, (atom[at, :] + 1).astype(F32), k.astype(F32))
            left_parts.append(jnp.concatenate([jnp.where(hit, v, 0.0) for v in parts], axis=0))
            group = lax.broadcasted_iota(jnp.int32, (128, 128), 0) == lax.shift_right_logical(t, 6)
            right_parts.append(jnp.where(group, 1.0, 0.0))
        return total + dot_nt(
            jnp.concatenate(left_parts, axis=1).astype(BF16), jnp.concatenate(right_parts, axis=1).astype(BF16)
        )

    total = lax.fori_loop(0, PAIRS // 256, place, jnp.zeros((5 * SLOT, 128), F32))
    d = total[0:SLOT] + total[SLOT:2 * SLOT] + total[2 * SLOT:3 * SLOT]
    slot_d[...] = d
    slot_e[...] = envelope_of(d)
    slot_a[...] = total[3 * SLOT:4 * SLOT] - 1.0
    slot_m[...] = total[4 * SLOT:5 * SLOT]

    square[...] = jnp.zeros_like(square)
    for source, target in ((dist[...], pair_d), (envelope_of(dist[...]), pair_e), (atom[...].astype(F32), pair_a), (prow[...].astype(F32), pair_r)):
        square[0:32, :] = source
        target[...] = square[...].T
    square[0:32, 0:FETCH] = lists[...].astype(F32)
    list_t[...] = square[...].T

    pl.semaphore_wait(barrier, 3 * CELLS - 1)

    def feature_copy(which):
        return pltpu.make_async_remote_copy(
            src_ref=feat, dst_ref=feat_in.at[which], send_sem=feat_ss.at[which], recv_sem=feat_rs.at[which],
            device_id=(strip_at(1 - 2 * which), me), device_id_type=MESH,
        )

    for which in range(2):
        feature_copy(which).start()

    def pair_gates(j, _):
        d = jnp.concatenate([column(pair_d[...], 2 * j + h) for h in range(2)], axis=0)
        e = jnp.concatenate([column(pair_e[...], 2 * j + h) for h in range(2)], axis=0)
        gate_o[pl.ds(pl.multiple_of(j * 256, 256), 256), :] = gate_of(d, e, w_rin[...], w_rout[...])
        return 0

    early = 4
    lax.fori_loop(0, early, pair_gates, 0)

    for which in range(2):
        feature_copy(which).wait()
        tables[pl.ds(2 * D * which, D), :] = dot(feat_in[which], w_right[...]).astype(BF16)

    def row_copy(k):
        return pltpu.make_async_remote_copy(
            src_ref=rows_out.at[pl.ds(pl.multiple_of(k * FETCH, 16), FETCH)],
            dst_ref=rows_in.at[pl.ds(pl.multiple_of(me * FETCH, 16), FETCH)],
            send_sem=rows_ss.at[k], recv_sem=rows_rs.at[k],
            device_id=(strip_at(0), cell_at(k, 1)), device_id_type=MESH,
        )

    own_rows = pltpu.make_async_copy(
        rows_out.at[pl.ds(0, FETCH)], rows_in.at[pl.ds(pl.multiple_of(me * FETCH, 16), FETCH)], local_sem.at[0]
    )

    def send_rows_of(i):
        for h in range(4):
            if h:
                row_copy(4 * i + h).start()
            else:
                @pl.when(i == 0)
                def _():
                    own_rows.start()

                @pl.when(i > 0)
                def _():
                    row_copy(4 * i).start()

    def pick(i, _):
        index = jnp.concatenate([column(list_t[0:FETCH, :], cell_at(4 * i + h, 1)) for h in range(4)], axis=0)
        picked = dot(one_hot(index, 3 * D), tables[...]).astype(BF16)
        rows_out[pl.ds(pl.multiple_of(i * 4 * FETCH, 64), 4 * FETCH), :] = picked

        @pl.when(i > 0)
        def _():
            send_rows_of(i - 1)
        return 0

    lax.fori_loop(0, CELLS // 4, pick, 0)

    def slot_columns(source, i):
        cells = [cell_at(2 * i + h, -1) for h in range(2)]
        return jnp.concatenate([column(source[...], o * CELLS + c) for o in range(3) for c in cells], axis=0)

    def slot_gates(i, _):
        gate_s[pl.ds(pl.multiple_of(i * 384, 128), 384), :] = gate_of(
            slot_columns(slot_d, i), slot_columns(slot_e, i), w_rin[...], w_rout[...]
        )
        return 0

    lax.fori_loop(0, 1, slot_gates, 0)
    send_rows_of(CELLS // 4 - 1)
    lax.fori_loop(1, CELLS // 2, slot_gates, 0)

    def block_copy(k, o):
        return pltpu.make_async_remote_copy(
            src_ref=blk_out.at[k, o], dst_ref=blk_in.at[o * CELLS + me],
            send_sem=blk_ss.at[k, o], recv_sem=blk_rs.at[k, o],
            device_id=(strip_at(o - 1), cell_at(k, -1)), device_id_type=MESH,
        )

    own_block = pltpu.make_async_copy(blk_out.at[0, 1], blk_in.at[CELLS + me], local_sem.at[1])

    def send_blocks_of(i):
        for h in range(2):
            for o in range(3):
                if h or o != 1:
                    block_copy(2 * i + h, o).start()
                else:
                    @pl.when(i == 0)
                    def _():
                        own_block.start()

                    @pl.when(i > 0)
                    def _():
                        block_copy(2 * i, 1).start()

    def slots(i, _):
        @pl.when(i == 0)
        def _():
            own_rows.wait()

        @pl.when(i > 0)
        def _():
            row_copy(2 * i).wait_recv()
        row_copy(2 * i + 1).wait_recv()
        rows = jnp.concatenate(
            [rows_in[pl.ds(pl.multiple_of(cell_at(2 * i + h, -1) * FETCH, 16), FETCH), :] for h in range(2)], axis=0
        )
        second = lax.rem(lax.div(lax.broadcasted_iota(jnp.int32, (384, 1), 0), SLOT), 2) * FETCH
        left_rows = dot(one_hot(slot_columns(slot_a, i), D), left[...])
        right_rows = dot(one_hot(slot_columns(slot_m, i).astype(jnp.int32) + second, 2 * FETCH), rows)
        gate = gate_s[pl.ds(pl.multiple_of(i * 384, 128), 384), :]
        edge = (left_rows * right_rows * gate).astype(BF16)
        mixed = silu(dot(edge, w_mix[...])).astype(BF16)
        out = dot_nt(w_flip[...], mixed)
        low = lax.broadcasted_iota(jnp.int32, (HALF, 128), 1) < SLOT
        for o in range(3):
            top = out[0:HALF, o * 128:(o + 1) * 128]
            bottom = out[HALF:2 * HALF, o * 128:(o + 1) * 128]
            blk_out[2 * i, o] = jnp.where(low, top, pltpu.roll(bottom, SLOT, 1)).astype(BF16)
            blk_out[2 * i + 1, o] = jnp.where(low, pltpu.roll(top, SLOT, 1), bottom).astype(BF16)

        @pl.when(i > 0)
        def _():
            send_blocks_of(i - 1)
        return 0

    lax.fori_loop(0, CELLS // 2, slots, 0)
    lax.fori_loop(early, early + 1, pair_gates, 0)
    send_blocks_of(CELLS // 2 - 1)
    lax.fori_loop(early + 1, PAIRS // 256, pair_gates, 0)

    def pairs(j, _):
        index_l = jnp.concatenate([column(pair_a[...], 2 * j + h) for h in range(2)], axis=0)
        index_r = jnp.concatenate([column(pair_r[...], 2 * j + h) for h in range(2)], axis=0)
        left_rows = dot(one_hot(index_l, D), left[...])
        right_rows = dot(one_hot(index_r, CELLS * FETCH), rows_in[...])
        at = pl.ds(pl.multiple_of(j * 256, 256), 256)
        edge = (left_rows * right_rows * gate_o[at, :]).astype(BF16)
        mixed = silu(dot(edge, w_mix[...])).astype(BF16)
        own[:, at] = dot_nt(w_own[...], mixed)[0:BLOCK].astype(BF16)
        return 0

    lax.fori_loop(0, PAIRS // 256, pairs, 0)

    own_block.wait()
    block_copy(0, 0).wait()
    block_copy(0, 2).wait()

    def finish(k, _):
        row_copy(k).wait_send()
        for o in range(3):
            block_copy(k, o).wait()
        return 0

    lax.fori_loop(1, CELLS, finish, 0)


STEPS = 8


def unpack_kernel(own_in, blocks, own, partner):
    own[...] = own_in[...]
    low = lax.broadcasted_iota(jnp.int32, (HALF, 128), 1) < SLOT
    for q in range(GROUPS // STEPS // 2):
        even = blocks[2 * q].astype(F32)
        odd = blocks[2 * q + 1].astype(F32)
        top = jnp.where(low, even, pltpu.roll(odd, SLOT, 1))
        bottom = jnp.where(low, pltpu.roll(even, SLOT, 1), odd)
        partner[:, q * 128:(q + 1) * 128] = jnp.concatenate([top, bottom], axis=0)[0:BLOCK].astype(BF16)


def body(features, pair_atom, partner_row, transpose_slot, distance, send_rows, w_left, w_right, w_radial_in, w_radial_out, w_mix, w_out):
    vmem = pl.BlockSpec(memory_space=pltpu.VMEM)
    sem = pltpu.SemaphoreType.DMA
    own, blocks = pl.pallas_call(
        main_kernel,
        out_shape=(
            jax.ShapeDtypeStruct((BLOCK, PAIRS), BF16),
            jax.ShapeDtypeStruct((GROUPS, HALF, 128), BF16),
        ),
        in_specs=[vmem] * 12,
        out_specs=(vmem, pl.BlockSpec(memory_space=pl.ANY)),
        scratch_shapes=[
            pltpu.VMEM((2, D, D), BF16),
            pltpu.VMEM((3 * D, D), BF16),
            pltpu.VMEM((D, D), BF16),
            pltpu.VMEM((CELLS * FETCH, D), BF16),
            pltpu.VMEM((CELLS * FETCH, D), BF16),
            pltpu.VMEM((GROUPS * SLOT, D), F32),
            pltpu.VMEM((PAIRS, D), F32),
            pltpu.VMEM((CELLS, 3, HALF, 128), BF16),
            *[pltpu.VMEM((SLOT, 128), F32)] * 4,
            *[pltpu.VMEM((128, 128), F32)] * 5,
            pltpu.VMEM((128, 128), F32),
            pltpu.VMEM((D, D), BF16),
            pltpu.VMEM((2 * HALF, D), BF16),
            pltpu.VMEM((2 * HALF, D), BF16),
            sem((2,)), sem((2,)), sem((CELLS,)), sem((CELLS,)), sem((CELLS, 3)), sem((CELLS, 3)), sem((2,)),
        ],
        compiler_params=pltpu.CompilerParams(collective_id=0, has_side_effects=True, vmem_limit_bytes=48 << 20),
    )(
        features,
        pair_atom.reshape(32, 128),
        partner_row.reshape(32, 128),
        transpose_slot.reshape(32, 128),
        distance.reshape(32, 128),
        send_rows, w_left, w_right, w_radial_in, w_radial_out, w_mix, w_out,
    )
    own_width, partner_width = PAIRS // STEPS, GROUPS * SLOT // STEPS
    return pl.pallas_call(
        unpack_kernel,
        grid=(STEPS,),
        out_shape=(
            jax.ShapeDtypeStruct((BLOCK, PAIRS), BF16),
            jax.ShapeDtypeStruct((BLOCK, GROUPS * SLOT), BF16),
        ),
        in_specs=[
            pl.BlockSpec((BLOCK, own_width), lambda i: (0, i)),
            pl.BlockSpec((GROUPS // STEPS, HALF, 128), lambda i: (i, 0, 0)),
        ],
        out_specs=(
            pl.BlockSpec((BLOCK, own_width), lambda i: (0, i)),
            pl.BlockSpec((BLOCK, partner_width), lambda i: (0, i)),
        ),
        compiler_params=pltpu.CompilerParams(vmem_limit_bytes=16 << 20),
    )(own, blocks)


def solution(mesh):
    both = P(("strip", "cell"))
    rows = P(("strip", "cell"), None)
    in_specs = (rows, both, both, both, both, rows, P(), P(), P(), P(), P(), P())
    out_specs = (P(None, ("strip", "cell")), P(None, ("strip", "cell")))
    return jax.shard_map(body, mesh=mesh, in_specs=in_specs, out_specs=out_specs, check_vma=False)
```

```python
import functools

import jax
import jax.numpy as jnp
import numpy as np
from jax import lax
from jax.experimental import pallas as pl
from jax.experimental.pallas import tpu as pltpu
from jax.sharding import PartitionSpec as P

MESH = pl.DeviceIdType.MESH
F32 = jnp.float32
BF16 = jnp.bfloat16
D = 256
BLOCK = 169
ORB = 13
HALF = 88
FETCH = 48
SLOT = 64
CELLS = 32
STRIPS = 8
Z = 8
X = 4
PAIRS = 4096
GROUPS = 96
CUTOFF = 8.0
COUNT = 128
PART = 16
EARLY = 4


def silu(x):
    half = 0.5 * x
    return half + half * jnp.tanh(half)


def offset_of(k):
    j = lax.div(k, 4)
    hop = lax.div(j + 1, 2) * (2 * lax.rem(j, 2) - 1)
    return lax.rem(k, 4), hop


def cell_at(k, sign):
    c = lax.axis_index("cell")
    dx, dz = offset_of(k)
    x = lax.rem(lax.div(c, Z) + sign * dx + X, X)
    z = lax.rem(lax.rem(c, Z) + sign * dz + Z, Z)
    return x * Z + z


def strip_at(step):
    return lax.rem(lax.axis_index("strip") + step + STRIPS, STRIPS)


def column(values, lane):
    lanes = lax.broadcasted_iota(jnp.int32, values.shape, 1)
    return jnp.sum(jnp.where(lanes == lane, values, 0.0), axis=1, keepdims=True)


def one_hot(index, width):
    lanes = lax.broadcasted_iota(jnp.int32, (index.shape[0], width), 1)
    return jnp.where(lanes == index.astype(jnp.int32), 1.0, 0.0).astype(BF16)


def dot(a, b):
    return jnp.dot(a, b, preferred_element_type=F32)


def dot_nt(a, b):
    return lax.dot_general(a, b, (((1,), (1,)), ((), ())), preferred_element_type=F32)


def row_index(slot, row):
    offset = lax.shift_right_logical(slot, 11)
    base = FETCH * (lax.shift_right_logical(slot, 6) & (CELLS - 1))
    part = lax.shift_right_logical((row - base - offset) * 171, 9)
    return base + offset * PART + part


def envelope_of(distance):
    return 0.5 * (jnp.cos(jnp.pi * distance / CUTOFF) + 1.0)


def gate_of(distance, envelope, w_in, w_out):
    centers = lax.broadcasted_iota(jnp.int32, (1, COUNT), 1).astype(F32) * (CUTOFF / (COUNT - 1))
    scaled = (distance - centers) * (COUNT / (2.0 * CUTOFF))
    basis = (jnp.exp(-scaled * scaled) * envelope).astype(BF16)
    radial = silu(dot(basis, w_in)).astype(BF16)
    return dot(radial, w_out)


def main_kernel(
    feat_h, atom_h, prow_h, slot_h, dist_h, lists_h, w_left_h, w_right_h, w_rin_h, w_rout_h, w_mix_h, w_out_h,
    own, partner,
    feat, atom, prow, slot, dist, lists, w_left, w_right, w_rin, w_rout, w_mix, w_raw, w_out,
    feat_in, tables, left, rows_out, rows_in, gate_s, gate_o, blk_out, blk_in,
    slot_d, slot_e, slot_a, slot_m, pair_d, pair_e, pair_a, pair_r, list_t, list_s,
    square, w_own, w_flip,
    in_sem, feat_ss, feat_rs, rows_ss, rows_rs, blk_ss, blk_rs, local_sem,
):
    me = lax.axis_index("cell")
    sources = (feat_h, w_left_h, w_right_h, lists_h, slot_h, dist_h, atom_h, prow_h, w_out_h, w_rin_h, w_rout_h, w_mix_h)
    targets = (feat, w_left, w_right, lists, slot, dist, atom, prow, w_raw, w_rin, w_rout, w_mix)
    loads = [pltpu.make_async_copy(a, b, in_sem.at[n]) for n, (a, b) in enumerate(zip(sources, targets))]
    for load in loads:
        load.start()

    barrier = pltpu.get_barrier_semaphore()

    def greet(k, _):
        c = cell_at(k, 1)
        for step in (-1, 0, 1):
            if step:
                pl.semaphore_signal(barrier, inc=1, device_id=(strip_at(step), c), device_id_type=MESH)
            else:
                @pl.when(k > 0)
                def _():
                    pl.semaphore_signal(barrier, inc=1, device_id=(strip_at(0), c), device_id_type=MESH)
        return 0

    lax.fori_loop(0, CELLS, greet, 0)
    for load in loads:
        load.wait()

    left[...] = dot(feat[...], w_left[...]).astype(BF16)
    tables[1] = dot(feat[...], w_right[...]).astype(BF16)

    square[...] = jnp.zeros_like(square)
    square[0:32, 0:FETCH] = lists[...].astype(F32)
    list_t[...] = square[...].T
    for o in range(3):
        list_s[pl.ds(o * PART, PART), :] = list_t[pl.ds(o, PART, stride=3), :] - float(o * D)

    def pick(o, i):
        index = jnp.concatenate(
            [column(list_s[pl.ds(pl.multiple_of(o * PART, PART), PART), :], cell_at(8 * i + h, 1)) for h in range(8)], axis=0
        )
        picked = dot(one_hot(index, D), tables[o]).astype(BF16)
        rows_out[o, pl.ds(pl.multiple_of(i * 8 * PART, 128), 8 * PART), :] = picked

    def pick_own(i, _):
        pick(1, i)
        return 0

    lax.fori_loop(0, CELLS // 8, pick_own, 0)

    def place(j, total):
        left_parts, right_parts = [], []
        for h in range(2):
            at = pl.ds(2 * j + h, 1)
            t = slot[at, :]
            d = dist[at, :]
            d_hi = d.astype(BF16).astype(F32)
            d_mid = (d - d_hi).astype(BF16).astype(F32)
            d_lo = d - d_hi - d_mid
            index = row_index(t, prow[at, :]) - FETCH * (lax.shift_right_logical(t, 6) & (CELLS - 1))
            hit = lax.broadcasted_iota(jnp.int32, (SLOT, 128), 0) == (t & (SLOT - 1))
            parts = (d_hi, d_mid, d_lo, (atom[at, :] + 1).astype(F32), index.astype(F32))
            left_parts.append(jnp.concatenate([jnp.where(hit, v, 0.0) for v in parts], axis=0))
            group = lax.broadcasted_iota(jnp.int32, (128, 128), 0) == lax.shift_right_logical(t, 6)
            right_parts.append(jnp.where(group, 1.0, 0.0))
        return total + dot_nt(
            jnp.concatenate(left_parts, axis=1).astype(BF16), jnp.concatenate(right_parts, axis=1).astype(BF16)
        )

    total = lax.fori_loop(0, PAIRS // 256, place, jnp.zeros((5 * SLOT, 128), F32))
    d = total[0:SLOT] + total[SLOT:2 * SLOT] + total[2 * SLOT:3 * SLOT]
    slot_d[...] = d
    slot_e[...] = envelope_of(d)
    slot_a[...] = total[3 * SLOT:4 * SLOT] - 1.0
    slot_m[...] = total[4 * SLOT:5 * SLOT]

    pl.semaphore_wait(barrier, 3 * CELLS - 1)

    def feature_copy(which):
        return pltpu.make_async_remote_copy(
            src_ref=feat, dst_ref=feat_in.at[which], send_sem=feat_ss.at[which], recv_sem=feat_rs.at[which],
            device_id=(strip_at(1 - 2 * which), me), device_id_type=MESH,
        )

    def row_copy(k, o, sender):
        return pltpu.make_async_remote_copy(
            src_ref=rows_out.at[o, pl.ds(pl.multiple_of(k * PART, PART), PART)],
            dst_ref=rows_in.at[pl.ds(pl.multiple_of(me * FETCH + o * PART, PART), PART)],
            send_sem=rows_ss.at[k, o], recv_sem=rows_rs.at[sender, o],
            device_id=(strip_at(0), cell_at(k, 1)), device_id_type=MESH,
        )

    def own_rows(o):
        return pltpu.make_async_copy(
            rows_out.at[o, pl.ds(0, PART)], rows_in.at[pl.ds(pl.multiple_of(me * FETCH + o * PART, PART), PART)], local_sem.at[o]
        )

    def send_rows_of(o, i):
        for h in range(8):
            if h:
                row_copy(8 * i + h, o, me).start()
            else:
                @pl.when(i == 0)
                def _():
                    own_rows(o).start()

                @pl.when(i > 0)
                def _():
                    row_copy(8 * i, o, me).start()

    for which in range(2):
        feature_copy(which).start()

    def send_own_part(i, _):
        send_rows_of(1, i)
        return 0

    lax.fori_loop(0, CELLS // 8, send_own_part, 0)

    def slot_columns(source, i):
        cells = [cell_at(2 * i + h, -1) for h in range(2)]
        return jnp.concatenate([column(source[...], o * CELLS + c) for o in range(3) for c in cells], axis=0)

    def slot_gates(i, _):
        gate_s[pl.ds(pl.multiple_of(i * 384, 128), 384), :] = gate_of(
            slot_columns(slot_d, i), slot_columns(slot_e, i), w_rin[...], w_rout[...]
        )
        return 0

    early = EARLY
    lax.fori_loop(0, early, slot_gates, 0)

    for which in range(2):
        feature_copy(which).wait()
        tables[2 * which] = dot(feat_in[which], w_right[...]).astype(BF16)

    def pick_rest(i, _):
        pick(2 * lax.div(i, 4), lax.rem(i, 4))

        @pl.when(i > 0)
        def _():
            send_rows_of(2 * lax.div(i - 1, 4), lax.rem(i - 1, 4))
        return 0

    lax.fori_loop(0, CELLS // 4, pick_rest, 0)
    lax.fori_loop(early, early + 1, slot_gates, 0)
    send_rows_of(2, CELLS // 8 - 1)
    lax.fori_loop(early + 1, CELLS // 2, slot_gates, 0)

    def block_copy(k, o, sender):
        return pltpu.make_async_remote_copy(
            src_ref=blk_out.at[k, o], dst_ref=blk_in.at[o * CELLS + me],
            send_sem=blk_ss.at[k, o], recv_sem=blk_rs.at[sender, o],
            device_id=(strip_at(o - 1), cell_at(k, -1)), device_id_type=MESH,
        )

    own_block = pltpu.make_async_copy(blk_out.at[0, 1], blk_in.at[CELLS + me], local_sem.at[3])

    def send_blocks_of(i):
        for h in range(2):
            for o in range(3):
                if h or o != 1:
                    block_copy(2 * i + h, o, me).start()
                else:
                    @pl.when(i == 0)
                    def _():
                        own_block.start()

                    @pl.when(i > 0)
                    def _():
                        block_copy(2 * i, 1, me).start()

    low = lax.broadcasted_iota(jnp.int32, (HALF, 128), 1) < SLOT

    def slots(i, _):
        cells = [cell_at(2 * i + h, -1) for h in range(2)]
        for o in range(3):
            @pl.when(i == 0)
            def _():
                own_rows(o).wait()

            @pl.when(i > 0)
            def _():
                row_copy(2 * i, o, cells[0]).wait_recv()
            row_copy(2 * i + 1, o, cells[1]).wait_recv()
        rows = jnp.concatenate([rows_in[pl.ds(pl.multiple_of(c * FETCH, PART), FETCH), :] for c in cells], axis=0)
        second = lax.rem(lax.div(lax.broadcasted_iota(jnp.int32, (384, 1), 0), SLOT), 2) * FETCH
        left_rows = dot(one_hot(slot_columns(slot_a, i), D), left[...])
        right_rows = dot(one_hot(slot_columns(slot_m, i).astype(jnp.int32) + second, 2 * FETCH), rows)
        gate = gate_s[pl.ds(pl.multiple_of(i * 384, 128), 384), :]
        edge = (left_rows * right_rows * gate).astype(BF16)
        mixed = silu(dot(edge, w_mix[...])).astype(BF16)
        out = dot_nt(w_flip[...], mixed)
        for o in range(3):
            top = out[0:HALF, o * 128:(o + 1) * 128]
            bottom = out[HALF:2 * HALF, o * 128:(o + 1) * 128]
            blk_out[2 * i, o] = jnp.where(low, top, pltpu.roll(bottom, SLOT, 1)).astype(BF16)
            blk_out[2 * i + 1, o] = jnp.where(low, pltpu.roll(top, SLOT, 1), bottom).astype(BF16)

        @pl.when(i > 0)
        def _():
            send_blocks_of(i - 1)
        return 0

    entry = lax.broadcasted_iota(jnp.int32, (2 * HALF, D), 0)
    lane = lax.broadcasted_iota(jnp.int32, (2 * HALF, D), 1)
    quotient = lax.shift_right_logical(entry * 79, 10)
    flipped = (entry - quotient * ORB) * ORB + quotient
    w_out[...] = jnp.zeros_like(w_out)
    w_out[0:BLOCK, :] = w_raw[...]
    w_own[...] = w_out[0:2 * HALF, :]
    w_flip[...] = dot(jnp.where((entry < BLOCK) & (lane == flipped), 1.0, 0.0).astype(BF16), w_out[...]).astype(BF16)

    lax.fori_loop(0, CELLS // 2, slots, 0)

    index = row_index(slot[...], prow[...])
    for source, target in ((dist[...], pair_d), (envelope_of(dist[...]), pair_e), (atom[...].astype(F32), pair_a), (index.astype(F32), pair_r)):
        square[0:32, :] = source
        target[...] = square[...].T
    send_blocks_of(CELLS // 2 - 1)

    def pair_gates(j, _):
        d = jnp.concatenate([column(pair_d[...], 2 * j + h) for h in range(2)], axis=0)
        e = jnp.concatenate([column(pair_e[...], 2 * j + h) for h in range(2)], axis=0)
        gate_o[pl.ds(pl.multiple_of(j * 256, 256), 256), :] = gate_of(d, e, w_rin[...], w_rout[...])
        return 0

    lax.fori_loop(0, PAIRS // 256, pair_gates, 0)

    def pairs(j, _):
        index_l = jnp.concatenate([column(pair_a[...], 2 * j + h) for h in range(2)], axis=0)
        index_r = jnp.concatenate([column(pair_r[...], 2 * j + h) for h in range(2)], axis=0)
        left_rows = dot(one_hot(index_l, D), left[...])
        right_rows = dot(one_hot(index_r, CELLS * FETCH), rows_in[...])
        at = pl.ds(pl.multiple_of(j * 256, 256), 256)
        edge = (left_rows * right_rows * gate_o[at, :]).astype(BF16)
        mixed = silu(dot(edge, w_mix[...])).astype(BF16)
        own[:, at] = dot_nt(w_own[...], mixed)[0:BLOCK].astype(BF16)
        return 0

    lax.fori_loop(0, PAIRS // 256, pairs, 0)

    own_block.wait()
    block_copy(0, 0, me).wait()
    block_copy(0, 2, me).wait()
    parity = lax.rem(me, 2)

    def unpack(n, _):
        o = lax.rem(n, 3)
        x = lax.rem(lax.div(n, 3) + lax.div(me, Z), X)
        rank = lax.div(n, 3 * X)
        middle = lax.div(rank + 2, 3) * (1 + 2 * lax.rem(rank + parity, 2))
        shift = middle * lax.div(3 - rank + 2, 3) + 2 * lax.div(rank, 3)
        shift = lax.rem(shift, 4)
        even = x * Z + 2 * lax.rem(lax.div(lax.rem(me, Z), 2) + shift, 4)
        for h in range(2):
            @pl.when(even + h != me)
            def _():
                block_copy(0, o, even + h).wait_recv()
        base = o * CELLS + even
        first = blk_in[base].astype(F32)
        second = blk_in[base + 1].astype(F32)
        top = jnp.where(low, first, pltpu.roll(second, SLOT, 1))
        bottom = jnp.where(low, pltpu.roll(first, SLOT, 1), second)
        partner[:, pl.ds(pl.multiple_of(base * SLOT, 128), 128)] = jnp.concatenate([top, bottom], axis=0)[0:BLOCK].astype(BF16)
        return 0

    lax.fori_loop(0, GROUPS // 2, unpack, 0)

    def finish(k, _):
        for o in range(3):
            row_copy(k, o, me).wait_send()
            block_copy(k, o, me).wait_send()
        return 0

    lax.fori_loop(1, CELLS, finish, 0)


def output_kernel(own_in, partner_in, own, partner, sem):
    copies = [pltpu.make_async_copy(own_in, own, sem.at[0]), pltpu.make_async_copy(partner_in, partner, sem.at[1])]
    for copy in copies:
        copy.start()
    for copy in copies:
        copy.wait()


def body(features, pair_atom, partner_row, transpose_slot, distance, send_rows, w_left, w_right, w_radial_in, w_radial_out, w_mix, w_out):
    vmem = pl.BlockSpec(memory_space=pltpu.VMEM)
    hbm = pl.BlockSpec(memory_space=pltpu.HBM)
    sem = pltpu.SemaphoreType.DMA
    outputs = (
        jax.ShapeDtypeStruct((BLOCK, PAIRS), BF16),
        jax.ShapeDtypeStruct((BLOCK, GROUPS * SLOT), BF16),
    )
    own, partner = pl.pallas_call(
        main_kernel,
        out_shape=outputs,
        in_specs=[hbm] * 12,
        out_specs=(vmem, vmem),
        scratch_shapes=[
            pltpu.VMEM((D, D), BF16),
            *[pltpu.VMEM((32, 128), jnp.int32)] * 3,
            pltpu.VMEM((32, 128), F32),
            pltpu.VMEM((CELLS, FETCH), jnp.int32),
            pltpu.VMEM((D, D), BF16),
            pltpu.VMEM((D, D), BF16),
            pltpu.VMEM((COUNT, D), BF16),
            pltpu.VMEM((D, D), BF16),
            pltpu.VMEM((D, D), BF16),
            pltpu.VMEM((BLOCK, D), BF16),
            pltpu.VMEM((D, D), BF16),
            pltpu.VMEM((2, D, D), BF16),
            pltpu.VMEM((3, D, D), BF16),
            pltpu.VMEM((D, D), BF16),
            pltpu.VMEM((3, CELLS * PART, D), BF16),
            pltpu.VMEM((CELLS * FETCH, D), BF16),
            pltpu.VMEM((GROUPS * SLOT, D), F32),
            pltpu.VMEM((PAIRS, D), F32),
            pltpu.VMEM((CELLS, 3, HALF, 128), BF16),
            pltpu.VMEM((GROUPS, HALF, 128), BF16),
            *[pltpu.VMEM((SLOT, 128), F32)] * 4,
            *[pltpu.VMEM((128, 128), F32)] * 5,
            pltpu.VMEM((FETCH, 128), F32),
            pltpu.VMEM((128, 128), F32),
            pltpu.VMEM((2 * HALF, D), BF16),
            pltpu.VMEM((2 * HALF, D), BF16),
            sem((12,)), sem((2,)), sem((2,)), sem((CELLS, 3)), sem((CELLS, 3)), sem((CELLS, 3)), sem((CELLS, 3)), sem((4,)),
        ],
        compiler_params=pltpu.CompilerParams(collective_id=0, has_side_effects=True, vmem_limit_bytes=48 << 20),
    )(*[pltpu.with_memory_space_constraint(a, pltpu.HBM) for a in (
        features,
        pair_atom.reshape(32, 128),
        partner_row.reshape(32, 128),
        transpose_slot.reshape(32, 128),
        distance.reshape(32, 128),
        send_rows, w_left, w_right, w_radial_in, w_radial_out, w_mix, w_out.T,
    )])
    return pl.pallas_call(
        output_kernel,
        out_shape=outputs,
        in_specs=[vmem, vmem],
        out_specs=(hbm, hbm),
        scratch_shapes=[sem((2,))],
        compiler_params=pltpu.CompilerParams(vmem_limit_bytes=16 << 20),
    )(own, partner)


def solution(mesh):
    both = P(("strip", "cell"))
    rows = P(("strip", "cell"), None)
    in_specs = (rows, both, both, both, both, rows, P(), P(), P(), P(), P(), P())
    out_specs = (P(None, ("strip", "cell")), P(None, ("strip", "cell")))
    return jax.shard_map(body, mesh=mesh, in_specs=in_specs, out_specs=out_specs, check_vma=False)
```

```python
import functools

import jax
import jax.numpy as jnp
import numpy as np
from jax import lax
from jax.experimental import pallas as pl
from jax.experimental.pallas import tpu as pltpu
from jax.sharding import PartitionSpec as P

MESH = pl.DeviceIdType.MESH
F32 = jnp.float32
BF16 = jnp.bfloat16
D = 256
BLOCK = 169
ORB = 13
HALF = 88
FETCH = 48
SLOT = 64
CELLS = 32
STRIPS = 8
Z = 8
X = 4
PAIRS = 4096
GROUPS = 96
CUTOFF = 8.0
COUNT = 128
PART = 16
EARLY = 2
WIDE = 4
SPAN = 3 * WIDE * SLOT


def silu(x):
    half = 0.5 * x
    return half + half * jnp.tanh(half)


def offset_of(k):
    j = lax.rem(k, Z)
    hop = lax.div(j + 1, 2) * (2 * lax.rem(j, 2) - 1)
    return lax.div(k, Z), hop


def cell_at(k, sign):
    c = lax.axis_index("cell")
    dx, dz = offset_of(k)
    x = lax.rem(lax.div(c, Z) + sign * dx + X, X)
    z = lax.rem(lax.rem(c, Z) + sign * dz + Z, Z)
    return x * Z + z


def strip_at(step):
    return lax.rem(lax.axis_index("strip") + step + STRIPS, STRIPS)


def column(values, lane):
    lanes = lax.broadcasted_iota(jnp.int32, values.shape, 1)
    return jnp.sum(jnp.where(lanes == lane, values, 0.0), axis=1, keepdims=True)


def one_hot(index, width):
    lanes = lax.broadcasted_iota(jnp.int32, (index.shape[0], width), 1).astype(F32)
    return jnp.where(lanes == index, 1.0, 0.0).astype(BF16)


def dot(a, b):
    return jnp.dot(a, b, preferred_element_type=F32)


def dot_nt(a, b):
    return lax.dot_general(a, b, (((1,), (1,)), ((), ())), preferred_element_type=F32)


def row_index(slot, row):
    offset = lax.shift_right_logical(slot, 11)
    base = FETCH * (lax.shift_right_logical(slot, 6) & (CELLS - 1))
    part = lax.shift_right_logical((row - base - offset) * 171, 9)
    return base + offset * PART + part


def envelope_of(distance):
    return 0.5 * (jnp.cos(jnp.pi * distance / CUTOFF) + 1.0)


def gate_of(distance, envelope, w_in, w_out):
    centers = lax.broadcasted_iota(jnp.int32, (1, COUNT), 1).astype(F32) * (CUTOFF / (COUNT - 1))
    scaled = (distance - centers) * (COUNT / (2.0 * CUTOFF))
    basis = (jnp.exp(-scaled * scaled) * envelope).astype(BF16)
    radial = silu(dot(basis, w_in)).astype(BF16)
    return dot(radial, w_out)


def main_kernel(
    feat_h, atom_h, prow_h, slot_h, dist_h, lists_h, w_left_h, w_right_h, w_rin_h, w_rout_h, w_mix_h, w_out_h,
    own, partner,
    feat, atom, prow, slot, dist, lists, w_left, w_right, w_rin, w_rout, w_mix, w_raw, w_out,
    feat_in, tables, left, rows_out, rows_in, gate_s, gate_o, blk_out, blk_in,
    slot_d, slot_e, slot_a, slot_m, pair_d, pair_e, pair_a, pair_r, list_t, list_s,
    square, w_own, w_flip,
    in_sem, feat_ss, feat_rs, rows_ss, rows_rs, blk_ss, blk_rs, local_sem,
):
    me = lax.axis_index("cell")
    sources = (feat_h, w_left_h, w_right_h, lists_h, slot_h, dist_h, atom_h, prow_h, w_out_h, w_rin_h, w_rout_h, w_mix_h)
    targets = (feat, w_left, w_right, lists, slot, dist, atom, prow, w_raw, w_rin, w_rout, w_mix)
    loads = [pltpu.make_async_copy(a, b, in_sem.at[n]) for n, (a, b) in enumerate(zip(sources, targets))]
    for load in loads:
        load.start()

    barrier = pltpu.get_barrier_semaphore()

    def greet(k, _):
        c = cell_at(k, 1)
        for step in (-1, 0, 1):
            if step:
                pl.semaphore_signal(barrier, inc=1, device_id=(strip_at(step), c), device_id_type=MESH)
            else:
                @pl.when(k > 0)
                def _():
                    pl.semaphore_signal(barrier, inc=1, device_id=(strip_at(0), c), device_id_type=MESH)
        return 0

    lax.fori_loop(0, CELLS, greet, 0)
    for load in loads:
        load.wait()

    left[...] = dot(feat[...], w_left[...]).astype(BF16)
    tables[1] = dot(feat[...], w_right[...]).astype(BF16)

    square[...] = jnp.zeros_like(square)
    square[0:32, 0:FETCH] = lists[...].astype(F32)
    list_t[...] = square[...].T
    for o in range(3):
        list_s[pl.ds(o * PART, PART), :] = list_t[pl.ds(o, PART, stride=3), :] - float(o * D)

    def pick(o, i):
        index = jnp.concatenate(
            [column(list_s[pl.ds(pl.multiple_of(o * PART, PART), PART), :], cell_at(8 * i + h, 1)) for h in range(8)], axis=0
        )
        picked = dot(one_hot(index, D), tables[o]).astype(BF16)
        rows_out[o, pl.ds(pl.multiple_of(i * 8 * PART, 128), 8 * PART), :] = picked

    def pick_own(i, _):
        pick(1, i)
        return 0

    lax.fori_loop(0, CELLS // 8, pick_own, 0)

    def place(j, total):
        left_parts, right_parts = [], []
        for h in range(2):
            at = pl.ds(2 * j + h, 1)
            t = slot[at, :]
            d = dist[at, :]
            d_hi = d.astype(BF16).astype(F32)
            d_mid = (d - d_hi).astype(BF16).astype(F32)
            d_lo = d - d_hi - d_mid
            index = row_index(t, prow[at, :]) - FETCH * (lax.shift_right_logical(t, 6) & (CELLS - 1))
            hit = lax.broadcasted_iota(jnp.int32, (SLOT, 128), 0) == (t & (SLOT - 1))
            parts = (d_hi, d_mid, d_lo, (atom[at, :] + 1).astype(F32), index.astype(F32))
            left_parts.append(jnp.concatenate([jnp.where(hit, v, 0.0) for v in parts], axis=0))
            group = lax.broadcasted_iota(jnp.int32, (128, 128), 0) == lax.shift_right_logical(t, 6)
            right_parts.append(jnp.where(group, 1.0, 0.0))
        return total + dot_nt(
            jnp.concatenate(left_parts, axis=1).astype(BF16), jnp.concatenate(right_parts, axis=1).astype(BF16)
        )

    total = lax.fori_loop(0, PAIRS // 256, place, jnp.zeros((5 * SLOT, 128), F32))
    d = total[0:SLOT] + total[SLOT:2 * SLOT] + total[2 * SLOT:3 * SLOT]
    slot_d[...] = d
    slot_e[...] = envelope_of(d)
    slot_a[...] = total[3 * SLOT:4 * SLOT] - 1.0
    slot_m[...] = total[4 * SLOT:5 * SLOT]

    pl.semaphore_wait(barrier, 3 * CELLS - 1)

    def feature_copy(which):
        return pltpu.make_async_remote_copy(
            src_ref=feat, dst_ref=feat_in.at[which], send_sem=feat_ss.at[which], recv_sem=feat_rs.at[which],
            device_id=(strip_at(1 - 2 * which), me), device_id_type=MESH,
        )

    def row_copy(k, o, sender):
        return pltpu.make_async_remote_copy(
            src_ref=rows_out.at[o, pl.ds(pl.multiple_of(k * PART, PART), PART)],
            dst_ref=rows_in.at[pl.ds(pl.multiple_of(me * FETCH + o * PART, PART), PART)],
            send_sem=rows_ss.at[k, o], recv_sem=rows_rs.at[sender, o],
            device_id=(strip_at(0), cell_at(k, 1)), device_id_type=MESH,
        )

    def own_rows(o):
        return pltpu.make_async_copy(
            rows_out.at[o, pl.ds(0, PART)], rows_in.at[pl.ds(pl.multiple_of(me * FETCH + o * PART, PART), PART)], local_sem.at[o]
        )

    def send_rows_of(o, i):
        for h in range(8):
            if h:
                row_copy(8 * i + h, o, me).start()
            else:
                @pl.when(i == 0)
                def _():
                    own_rows(o).start()

                @pl.when(i > 0)
                def _():
                    row_copy(8 * i, o, me).start()

    for which in range(2):
        feature_copy(which).start()

    def send_own_part(i, _):
        send_rows_of(1, i)
        return 0

    lax.fori_loop(0, CELLS // 8, send_own_part, 0)

    def slot_columns(source, i):
        cells = [cell_at(WIDE * i + h, -1) for h in range(WIDE)]
        return jnp.concatenate([column(source[...], o * CELLS + c) for o in range(3) for c in cells], axis=0)

    def slot_gates(i, _):
        gate_s[pl.ds(pl.multiple_of(i * SPAN, 128), SPAN), :] = gate_of(
            slot_columns(slot_d, i), slot_columns(slot_e, i), w_rin[...], w_rout[...]
        )
        return 0

    early = EARLY
    lax.fori_loop(0, early, slot_gates, 0)

    for which in range(2):
        feature_copy(which).wait()
        tables[2 * which] = dot(feat_in[which], w_right[...]).astype(BF16)

    def pick_rest(i, _):
        pick(2 * lax.div(i, 4), lax.rem(i, 4))

        @pl.when(i > 0)
        def _():
            send_rows_of(2 * lax.div(i - 1, 4), lax.rem(i - 1, 4))
        return 0

    lax.fori_loop(0, CELLS // 4, pick_rest, 0)
    lax.fori_loop(early, early + 1, slot_gates, 0)
    send_rows_of(2, CELLS // 8 - 1)
    lax.fori_loop(early + 1, CELLS // WIDE, slot_gates, 0)

    def block_copy(k, o, sender):
        return pltpu.make_async_remote_copy(
            src_ref=blk_out.at[k, o], dst_ref=blk_in.at[o * CELLS + me],
            send_sem=blk_ss.at[k, o], recv_sem=blk_rs.at[sender, o],
            device_id=(strip_at(o - 1), cell_at(k, -1)), device_id_type=MESH,
        )

    own_block = pltpu.make_async_copy(blk_out.at[0, 1], blk_in.at[CELLS + me], local_sem.at[3])

    def send_blocks_of(i):
        for h in range(WIDE):
            for o in range(3):
                if h or o != 1:
                    block_copy(WIDE * i + h, o, me).start()
                else:
                    @pl.when(i == 0)
                    def _():
                        own_block.start()

                    @pl.when(i > 0)
                    def _():
                        block_copy(WIDE * i, 1, me).start()

    low = lax.broadcasted_iota(jnp.int32, (HALF, 128), 1) < SLOT

    def slots(i, _):
        cells = [cell_at(WIDE * i + h, -1) for h in range(WIDE)]
        for o in range(3):
            @pl.when(i == 0)
            def _():
                own_rows(o).wait()

            @pl.when(i > 0)
            def _():
                row_copy(WIDE * i, o, cells[0]).wait_recv()
            for h in range(1, WIDE):
                row_copy(WIDE * i + h, o, cells[h]).wait_recv()
        rows = jnp.concatenate([rows_in[pl.ds(pl.multiple_of(c * FETCH, PART), FETCH), :] for c in cells], axis=0)
        second = lax.rem(lax.div(lax.broadcasted_iota(jnp.int32, (SPAN, 1), 0), SLOT), WIDE) * FETCH
        left_rows = dot(one_hot(slot_columns(slot_a, i), D), left[...])
        right_rows = dot(one_hot(slot_columns(slot_m, i) + second.astype(F32), WIDE * FETCH), rows)
        gate = gate_s[pl.ds(pl.multiple_of(i * SPAN, 128), SPAN), :]
        edge = (left_rows * right_rows * gate).astype(BF16)
        mixed = silu(dot(edge, w_mix[...])).astype(BF16)
        out = dot_nt(w_flip[...], mixed)
        for o in range(3):
            for h in range(0, WIDE, 2):
                start = (o * WIDE + h) * SLOT
                top = out[0:HALF, start:start + 128]
                bottom = out[HALF:2 * HALF, start:start + 128]
                blk_out[WIDE * i + h, o] = jnp.where(low, top, pltpu.roll(bottom, SLOT, 1)).astype(BF16)
                blk_out[WIDE * i + h + 1, o] = jnp.where(low, pltpu.roll(top, SLOT, 1), bottom).astype(BF16)

        @pl.when(i > 0)
        def _():
            send_blocks_of(i - 1)
        return 0

    entry = lax.broadcasted_iota(jnp.int32, (2 * HALF, D), 0)
    lane = lax.broadcasted_iota(jnp.int32, (2 * HALF, D), 1)
    quotient = lax.shift_right_logical(entry * 79, 10)
    flipped = (entry - quotient * ORB) * ORB + quotient
    w_out[...] = jnp.zeros_like(w_out)
    w_out[0:BLOCK, :] = w_raw[...]
    w_own[...] = w_out[0:2 * HALF, :]
    w_flip[...] = dot(jnp.where((entry < BLOCK) & (lane == flipped), 1.0, 0.0).astype(BF16), w_out[...]).astype(BF16)

    lax.fori_loop(0, CELLS // WIDE, slots, 0)

    index = row_index(slot[...], prow[...])
    for source, target in ((dist[...], pair_d), (envelope_of(dist[...]), pair_e), (atom[...].astype(F32), pair_a), (index.astype(F32), pair_r)):
        square[0:32, :] = source
        target[...] = square[...].T
    send_blocks_of(CELLS // WIDE - 1)

    def pair_gates(j, _):
        d = jnp.concatenate([column(pair_d[...], 2 * j + h) for h in range(2)], axis=0)
        e = jnp.concatenate([column(pair_e[...], 2 * j + h) for h in range(2)], axis=0)
        gate_o[pl.ds(pl.multiple_of(j * 256, 256), 256), :] = gate_of(d, e, w_rin[...], w_rout[...])
        return 0

    lax.fori_loop(0, PAIRS // 256, pair_gates, 0, unroll=4)

    def pairs(j, _):
        index_l = jnp.concatenate([column(pair_a[...], 2 * j + h) for h in range(2)], axis=0)
        index_r = jnp.concatenate([column(pair_r[...], 2 * j + h) for h in range(2)], axis=0)
        left_rows = dot(one_hot(index_l, D), left[...])
        right_rows = dot(one_hot(index_r, CELLS * FETCH), rows_in[...])
        at = pl.ds(pl.multiple_of(j * 256, 256), 256)
        edge = (left_rows * right_rows * gate_o[at, :]).astype(BF16)
        mixed = silu(dot(edge, w_mix[...])).astype(BF16)
        own[:, at] = dot_nt(w_own[...], mixed)[0:BLOCK].astype(BF16)
        return 0

    lax.fori_loop(0, PAIRS // 256, pairs, 0, unroll=4)

    own_block.wait()
    block_copy(0, 0, me).wait()
    block_copy(0, 2, me).wait()
    parity = lax.rem(me, 2)

    def unpack(n, _):
        o = lax.rem(n, 3)
        x = lax.rem(lax.div(n, 3) + lax.div(me, Z), X)
        rank = lax.div(n, 3 * X)
        middle = lax.div(rank + 2, 3) * (1 + 2 * lax.rem(rank + parity, 2))
        shift = middle * lax.div(3 - rank + 2, 3) + 2 * lax.div(rank, 3)
        shift = lax.rem(shift, 4)
        even = x * Z + 2 * lax.rem(lax.div(lax.rem(me, Z), 2) + shift, 4)
        for h in range(2):
            @pl.when(even + h != me)
            def _():
                block_copy(0, o, even + h).wait_recv()
        base = o * CELLS + even
        first = blk_in[base].astype(F32)
        second = blk_in[base + 1].astype(F32)
        top = jnp.where(low, first, pltpu.roll(second, SLOT, 1))
        bottom = jnp.where(low, pltpu.roll(first, SLOT, 1), second)
        partner[:, pl.ds(pl.multiple_of(base * SLOT, 128), 128)] = jnp.concatenate([top, bottom], axis=0)[0:BLOCK].astype(BF16)
        return 0

    lax.fori_loop(0, GROUPS // 2, unpack, 0)

    def finish(k, _):
        for o in range(3):
            row_copy(k, o, me).wait_send()
            block_copy(k, o, me).wait_send()
        return 0

    lax.fori_loop(1, CELLS, finish, 0)


def output_kernel(own_in, partner_in, own, partner, sem):
    copies = [pltpu.make_async_copy(own_in, own, sem.at[0]), pltpu.make_async_copy(partner_in, partner, sem.at[1])]
    for copy in copies:
        copy.start()
    for copy in copies:
        copy.wait()


def body(features, pair_atom, partner_row, transpose_slot, distance, send_rows, w_left, w_right, w_radial_in, w_radial_out, w_mix, w_out):
    vmem = pl.BlockSpec(memory_space=pltpu.VMEM)
    hbm = pl.BlockSpec(memory_space=pltpu.HBM)
    sem = pltpu.SemaphoreType.DMA
    outputs = (
        jax.ShapeDtypeStruct((BLOCK, PAIRS), BF16),
        jax.ShapeDtypeStruct((BLOCK, GROUPS * SLOT), BF16),
    )
    own, partner = pl.pallas_call(
        main_kernel,
        out_shape=outputs,
        in_specs=[hbm] * 12,
        out_specs=(vmem, vmem),
        scratch_shapes=[
            pltpu.VMEM((D, D), BF16),
            *[pltpu.VMEM((32, 128), jnp.int32)] * 3,
            pltpu.VMEM((32, 128), F32),
            pltpu.VMEM((CELLS, FETCH), jnp.int32),
            pltpu.VMEM((D, D), BF16),
            pltpu.VMEM((D, D), BF16),
            pltpu.VMEM((COUNT, D), BF16),
            pltpu.VMEM((D, D), BF16),
            pltpu.VMEM((D, D), BF16),
            pltpu.VMEM((BLOCK, D), BF16),
            pltpu.VMEM((D, D), BF16),
            pltpu.VMEM((2, D, D), BF16),
            pltpu.VMEM((3, D, D), BF16),
            pltpu.VMEM((D, D), BF16),
            pltpu.VMEM((3, CELLS * PART, D), BF16),
            pltpu.VMEM((CELLS * FETCH, D), BF16),
            pltpu.VMEM((GROUPS * SLOT, D), F32),
            pltpu.VMEM((PAIRS, D), F32),
            pltpu.VMEM((CELLS, 3, HALF, 128), BF16),
            pltpu.VMEM((GROUPS, HALF, 128), BF16),
            *[pltpu.VMEM((SLOT, 128), F32)] * 4,
            *[pltpu.VMEM((128, 128), F32)] * 5,
            pltpu.VMEM((FETCH, 128), F32),
            pltpu.VMEM((128, 128), F32),
            pltpu.VMEM((2 * HALF, D), BF16),
            pltpu.VMEM((2 * HALF, D), BF16),
            sem((12,)), sem((2,)), sem((2,)), sem((CELLS, 3)), sem((CELLS, 3)), sem((CELLS, 3)), sem((CELLS, 3)), sem((4,)),
        ],
        compiler_params=pltpu.CompilerParams(collective_id=0, has_side_effects=True, vmem_limit_bytes=48 << 20),
    )(*[pltpu.with_memory_space_constraint(a, pltpu.HBM) for a in (
        features,
        pair_atom.reshape(32, 128),
        partner_row.reshape(32, 128),
        transpose_slot.reshape(32, 128),
        distance.reshape(32, 128),
        send_rows, w_left, w_right, w_radial_in, w_radial_out, w_mix, w_out.T,
    )])
    return pl.pallas_call(
        output_kernel,
        out_shape=outputs,
        in_specs=[vmem, vmem],
        out_specs=(hbm, hbm),
        scratch_shapes=[sem((2,))],
        compiler_params=pltpu.CompilerParams(vmem_limit_bytes=16 << 20),
    )(own, partner)


def solution(mesh):
    both = P(("strip", "cell"))
    rows = P(("strip", "cell"), None)
    in_specs = (rows, both, both, both, both, rows, P(), P(), P(), P(), P(), P())
    out_specs = (P(None, ("strip", "cell")), P(None, ("strip", "cell")))
    return jax.shard_map(body, mesh=mesh, in_specs=in_specs, out_specs=out_specs, check_vma=False)
```

```python
import functools

import jax
import jax.numpy as jnp
import numpy as np
from jax import lax
from jax.experimental import pallas as pl
from jax.experimental.pallas import tpu as pltpu
from jax.sharding import PartitionSpec as P

MESH = pl.DeviceIdType.MESH
F32 = jnp.float32
BF16 = jnp.bfloat16
D = 256
BLOCK = 169
ORB = 13
HALF = 88
FETCH = 48
SLOT = 64
CELLS = 32
STRIPS = 8
Z = 8
X = 4
PAIRS = 4096
GROUPS = 96
CUTOFF = 8.0
COUNT = 128
PART = 16
EARLY = 2
WIDE = 4
SPAN = 3 * WIDE * SLOT
NEAR = 5
FAR = Z - NEAR
NEAR_CELLS = NEAR * X
FAR_CELLS = FAR * X


def silu(x):
    half = 0.5 * x
    return half + half * jnp.tanh(half)


def offset_of(k):
    j = lax.rem(k, Z)
    hop = lax.div(j + 1, 2) * (2 * lax.rem(j, 2) - 1)
    return lax.div(k, Z), hop


def cell_at(k, sign):
    c = lax.axis_index("cell")
    dx, dz = offset_of(k)
    x = lax.rem(lax.div(c, Z) + sign * dx + X, X)
    z = lax.rem(lax.rem(c, Z) + sign * dz + Z, Z)
    return x * Z + z


def strip_at(step):
    return lax.rem(lax.axis_index("strip") + step + STRIPS, STRIPS)


def column(values, lane):
    lanes = lax.broadcasted_iota(jnp.int32, values.shape, 1)
    return jnp.sum(jnp.where(lanes == lane, values, 0.0), axis=1, keepdims=True)


def one_hot(index, width):
    lanes = lax.broadcasted_iota(jnp.int32, (index.shape[0], width), 1).astype(F32)
    return jnp.where(lanes == index, 1.0, 0.0).astype(BF16)


def dot(a, b):
    return jnp.dot(a, b, preferred_element_type=F32)


def dot_nt(a, b):
    return lax.dot_general(a, b, (((1,), (1,)), ((), ())), preferred_element_type=F32)


def row_index(slot, row):
    offset = lax.shift_right_logical(slot, 11)
    base = FETCH * (lax.shift_right_logical(slot, 6) & (CELLS - 1))
    part = lax.shift_right_logical((row - base - offset) * 171, 9)
    return base + offset * PART + part


def envelope_of(distance):
    return 0.5 * (jnp.cos(jnp.pi * distance / CUTOFF) + 1.0)


def gate_of(distance, envelope, w_in, w_out):
    centers = lax.broadcasted_iota(jnp.int32, (1, COUNT), 1).astype(F32) * (CUTOFF / (COUNT - 1))
    scaled = (distance - centers) * (COUNT / (2.0 * CUTOFF))
    basis = (jnp.exp(-scaled * scaled) * envelope).astype(BF16)
    radial = silu(dot(basis, w_in)).astype(BF16)
    return dot(radial, w_out)


def main_kernel(
    feat_h, atom_h, prow_h, slot_h, dist_h, lists_h, w_left_h, w_right_h, w_rin_h, w_rout_h, w_mix_h, w_out_h,
    own, partner,
    feat, atom, prow, slot, dist, lists, w_left, w_right, w_rin, w_rout, w_mix, w_raw, w_out,
    feat_in, list_in, far_f, scal_out, scal_in, tables, left, rows_out, rows_in, gate_s, gate_o, blk_out, blk_in,
    slot_d, slot_e, slot_a, slot_m, pair_d, pair_e, pair_a, pair_r, list_t, list_s, list_n, turn_a, turn_b,
    square, w_own, w_flip,
    in_sem, feat_ss, feat_rs, list_ss, list_rs, hop_ss, hop_rs, side_ss, side_rs, near_ss, near_rs, scal_ss, scal_rs, rows_ss, rows_rs, blk_ss, blk_rs, local_sem,
):
    me = lax.axis_index("cell")
    sources = (feat_h, w_left_h, w_right_h, lists_h, slot_h, dist_h, atom_h, prow_h, w_out_h, w_rin_h, w_rout_h, w_mix_h)
    targets = (feat, w_left, w_right, lists, slot, dist, atom, prow, w_raw, w_rin, w_rout, w_mix)
    loads = [pltpu.make_async_copy(a, b, in_sem.at[n]) for n, (a, b) in enumerate(zip(sources, targets))]
    for load in loads:
        load.start()

    barrier = pltpu.get_barrier_semaphore()

    def greet(k, _):
        c = cell_at(k, 1)
        for step in (-1, 0, 1):
            if step:
                pl.semaphore_signal(barrier, inc=1, device_id=(strip_at(step), c), device_id_type=MESH)
            else:
                @pl.when(k > 0)
                def _():
                    pl.semaphore_signal(barrier, inc=1, device_id=(strip_at(0), c), device_id_type=MESH)
        return 0

    lax.fori_loop(0, CELLS, greet, 0)
    for load in loads:
        load.wait()

    left[...] = dot(feat[...], w_left[...]).astype(BF16)
    tables[1] = dot(feat[...], w_right[...]).astype(BF16)

    square[...] = jnp.zeros_like(square)
    square[0:32, 0:FETCH] = lists[...].astype(F32)
    list_t[...] = square[...].T
    for o in range(3):
        list_s[pl.ds(o * PART, PART), :] = list_t[pl.ds(o, PART, stride=3), :] - float(o * D)

    def pick(o, i):
        index = jnp.concatenate(
            [column(list_s[pl.ds(pl.multiple_of(o * PART, PART), PART), :], cell_at(8 * i + h, 1)) for h in range(8)], axis=0
        )
        picked = dot(one_hot(index, D), tables[o]).astype(BF16)
        rows_out[o, pl.ds(pl.multiple_of(i * 8 * PART, 128), 8 * PART), :] = picked

    def pick_own(i, _):
        pick(1, i)
        return 0

    lax.fori_loop(0, CELLS // 8, pick_own, 0)

    def place(j, total):
        left_parts, right_parts = [], []
        for h in range(2):
            at = pl.ds(2 * j + h, 1)
            t = slot[at, :]
            d = dist[at, :]
            d_hi = d.astype(BF16).astype(F32)
            d_mid = (d - d_hi).astype(BF16).astype(F32)
            d_lo = d - d_hi - d_mid
            index = row_index(t, prow[at, :]) - FETCH * (lax.shift_right_logical(t, 6) & (CELLS - 1))
            hit = lax.broadcasted_iota(jnp.int32, (SLOT, 128), 0) == (t & (SLOT - 1))
            parts = (d_hi, d_mid, d_lo, (atom[at, :] + 1).astype(F32), index.astype(F32))
            left_parts.append(jnp.concatenate([jnp.where(hit, v, 0.0) for v in parts], axis=0))
            group = lax.broadcasted_iota(jnp.int32, (128, 128), 0) == lax.shift_right_logical(t, 6)
            right_parts.append(jnp.where(group, 1.0, 0.0))
        return total + dot_nt(
            jnp.concatenate(left_parts, axis=1).astype(BF16), jnp.concatenate(right_parts, axis=1).astype(BF16)
        )

    total = lax.fori_loop(0, PAIRS // 256, place, jnp.zeros((5 * SLOT, 128), F32))
    d = total[0:SLOT] + total[SLOT:2 * SLOT] + total[2 * SLOT:3 * SLOT]
    slot_d[...] = d
    slot_e[...] = envelope_of(d)
    slot_a[...] = total[3 * SLOT:4 * SLOT] - 1.0
    slot_m[...] = total[4 * SLOT:5 * SLOT]
    turn_a[...] = jnp.concatenate([d, total[3 * SLOT:4 * SLOT] - 1.0], axis=0).T
    turn_b[...] = jnp.concatenate([total[4 * SLOT:5 * SLOT], jnp.zeros((SLOT, 128), F32)], axis=0).T

    def pack_scalars(n, _):
        c = cell_at(lax.rem(n, X) * Z + NEAR + lax.div(n, X), -1)
        for o in range(3):
            scal_out[3 * n + o, 0:1, :] = turn_a[pl.ds(o * CELLS + c, 1), :]
            scal_out[3 * n + o, 1:2, :] = turn_b[pl.ds(o * CELLS + c, 1), :]
        return 0

    lax.fori_loop(0, FAR_CELLS, pack_scalars, 0)

    pl.semaphore_wait(barrier, 3 * CELLS - 1)

    def feature_copy(which):
        return pltpu.make_async_remote_copy(
            src_ref=feat, dst_ref=feat_in.at[which], send_sem=feat_ss.at[which], recv_sem=feat_rs.at[which],
            device_id=(strip_at(1 - 2 * which), me), device_id_type=MESH,
        )

    def row_copy(k, o, sender):
        return pltpu.make_async_remote_copy(
            src_ref=rows_out.at[o, pl.ds(pl.multiple_of(k * PART, PART), PART)],
            dst_ref=rows_in.at[pl.ds(pl.multiple_of(me * FETCH + o * PART, PART), PART)],
            send_sem=rows_ss.at[k, o], recv_sem=rows_rs.at[sender, o],
            device_id=(strip_at(0), cell_at(k, 1)), device_id_type=MESH,
        )

    def own_rows(o):
        return pltpu.make_async_copy(
            rows_out.at[o, pl.ds(0, PART)], rows_in.at[pl.ds(pl.multiple_of(me * FETCH + o * PART, PART), PART)], local_sem.at[o]
        )

    def send_rows_of(o, i):
        for h in range(8):
            if h:
                row_copy(8 * i + h, o, me).start()
            else:
                @pl.when(i == 0)
                def _():
                    own_rows(o).start()

                @pl.when(i > 0)
                def _():
                    row_copy(8 * i, o, me).start()

    def list_copy(which):
        return pltpu.make_async_remote_copy(
            src_ref=lists, dst_ref=list_in.at[which], send_sem=list_ss.at[which], recv_sem=list_rs.at[which],
            device_id=(strip_at(1 - 2 * which), me), device_id_type=MESH,
        )

    def far_step(b, dx):
        return dx * Z + NEAR + b

    def hop_copy(b):
        return pltpu.make_async_remote_copy(
            src_ref=feat, dst_ref=far_f.at[1, b * X], send_sem=hop_ss.at[b], recv_sem=hop_rs.at[b],
            device_id=(strip_at(0), cell_at(far_step(b, 0), -1)), device_id_type=MESH,
        )

    def side_copy(b, dx):
        return pltpu.make_async_remote_copy(
            src_ref=far_f.at[1, b * X], dst_ref=far_f.at[1, b * X + dx],
            send_sem=side_ss.at[b, dx - 1], recv_sem=side_rs.at[b, dx - 1],
            device_id=(strip_at(0), cell_at(dx * Z, -1)), device_id_type=MESH,
        )

    def near_copy(n, which):
        return pltpu.make_async_remote_copy(
            src_ref=far_f.at[1, n], dst_ref=far_f.at[2 * which, n],
            send_sem=near_ss.at[n, which], recv_sem=near_rs.at[n, which],
            device_id=(strip_at(1 - 2 * which), me), device_id_type=MESH,
        )

    def scalar_copy(n, o):
        k = far_step(lax.div(n, X), lax.rem(n, X))
        return pltpu.make_async_remote_copy(
            src_ref=scal_out.at[3 * n + o], dst_ref=scal_in.at[3 * n + o],
            send_sem=scal_ss.at[n, o], recv_sem=scal_rs.at[n, o],
            device_id=(strip_at(o - 1), cell_at(k, -1)), device_id_type=MESH,
        )

    for which in range(2):
        feature_copy(which).start()
        list_copy(which).start()

    def send_own_part(i, _):
        send_rows_of(1, i)
        return 0

    lax.fori_loop(0, CELLS // 8, send_own_part, 0)

    def near_step(n):
        return lax.div(n, NEAR) * Z + lax.rem(n, NEAR)

    def slot_columns(source, i):
        cells = [cell_at(near_step(WIDE * i + h), -1) for h in range(WIDE)]
        return jnp.concatenate([column(source[...], o * CELLS + c) for o in range(3) for c in cells], axis=0)

    def slot_gates(i, _):
        gate_s[pl.ds(pl.multiple_of(i * SPAN, 128), SPAN), :] = gate_of(
            slot_columns(slot_d, i), slot_columns(slot_e, i), w_rin[...], w_rout[...]
        )
        return 0

    early = EARLY
    lax.fori_loop(0, early, slot_gates, 0)

    for which in range(2):
        feature_copy(which).wait()
        tables[2 * which] = dot(feat_in[which], w_right[...]).astype(BF16)

    def pick_rest(i, _):
        pick(2 * lax.div(i, 4), lax.rem(i, 4))

        @pl.when(i > 0)
        def _():
            send_rows_of(2 * lax.div(i - 1, 4), lax.rem(i - 1, 4))
        return 0

    lax.fori_loop(0, CELLS // 4, pick_rest, 0)
    lax.fori_loop(early, early + 1, slot_gates, 0)
    send_rows_of(2, CELLS // 8 - 1)
    for b in range(FAR):
        hop_copy(b).start()

    def send_scalars(n, _):
        for o in range(3):
            scalar_copy(n, o).start()
        return 0

    lax.fori_loop(0, FAR_CELLS, send_scalars, 0)
    for which in range(2):
        list_copy(which).wait()
        square[0:32, 0:FETCH] = list_in[which].astype(F32)
        list_t[...] = square[...].T
        list_n[which] = list_t[pl.ds(2 - 2 * which, PART, stride=3), :] - float((2 - 2 * which) * D)
    lax.fori_loop(early + 1, NEAR_CELLS // WIDE, slot_gates, 0)

    def block_copy(k, o, sender):
        return pltpu.make_async_remote_copy(
            src_ref=blk_out.at[k, o], dst_ref=blk_in.at[o * CELLS + me],
            send_sem=blk_ss.at[k, o], recv_sem=blk_rs.at[sender, o],
            device_id=(strip_at(o - 1), cell_at(k, -1)), device_id_type=MESH,
        )

    own_block = pltpu.make_async_copy(blk_out.at[0, 1], blk_in.at[CELLS + me], local_sem.at[3])

    def send_blocks_of(i):
        for h in range(WIDE):
            for o in range(3):
                if h or o != 1:
                    block_copy(near_step(WIDE * i + h), o, me).start()
                else:
                    @pl.when(i == 0)
                    def _():
                        own_block.start()

                    @pl.when(i > 0)
                    def _():
                        block_copy(near_step(WIDE * i), 1, me).start()

    low = lax.broadcasted_iota(jnp.int32, (HALF, 128), 1) < SLOT

    def halves(out, o, h):
        start = (o * WIDE + h) * SLOT
        top = out[0:HALF, start:start + 128]
        bottom = out[HALF:2 * HALF, start:start + 128]
        return (
            jnp.where(low, top, pltpu.roll(bottom, SLOT, 1)).astype(BF16),
            jnp.where(low, pltpu.roll(top, SLOT, 1), bottom).astype(BF16),
        )

    def far_rows(n, _):
        k = far_step(lax.div(n, X), lax.rem(n, X))
        for o in range(3):
            row_copy(k, o, cell_at(k, -1)).wait_recv()
        return 0

    def slots(i, _):
        cells = [cell_at(near_step(WIDE * i + h), -1) for h in range(WIDE)]
        for o in range(3):
            @pl.when(i == 0)
            def _():
                own_rows(o).wait()

            @pl.when(i > 0)
            def _():
                row_copy(near_step(WIDE * i), o, cells[0]).wait_recv()
            for h in range(1, WIDE):
                row_copy(near_step(WIDE * i + h), o, cells[h]).wait_recv()
        rows = jnp.concatenate([rows_in[pl.ds(pl.multiple_of(c * FETCH, PART), FETCH), :] for c in cells], axis=0)
        second = lax.rem(lax.div(lax.broadcasted_iota(jnp.int32, (SPAN, 1), 0), SLOT), WIDE) * FETCH
        left_rows = dot(one_hot(slot_columns(slot_a, i), D), left[...])
        right_rows = dot(one_hot(slot_columns(slot_m, i) + second.astype(F32), WIDE * FETCH), rows)
        gate = gate_s[pl.ds(pl.multiple_of(i * SPAN, 128), SPAN), :]
        edge = (left_rows * right_rows * gate).astype(BF16)
        mixed = silu(dot(edge, w_mix[...])).astype(BF16)
        out = dot_nt(w_flip[...], mixed)
        for o in range(3):
            for h in range(0, WIDE, 2):
                first, second = halves(out, o, h)
                blk_out[near_step(WIDE * i + h), o] = first
                blk_out[near_step(WIDE * i + h + 1), o] = second

        @pl.when(i > 0)
        def _():
            send_blocks_of(i - 1)
        return 0

    entry = lax.broadcasted_iota(jnp.int32, (2 * HALF, D), 0)
    lane = lax.broadcasted_iota(jnp.int32, (2 * HALF, D), 1)
    quotient = lax.shift_right_logical(entry * 79, 10)
    flipped = (entry - quotient * ORB) * ORB + quotient
    w_out[...] = jnp.zeros_like(w_out)
    w_out[0:BLOCK, :] = w_raw[...]
    w_own[...] = w_out[0:2 * HALF, :]
    w_flip[...] = dot(jnp.where((entry < BLOCK) & (lane == flipped), 1.0, 0.0).astype(BF16), w_out[...]).astype(BF16)

    index = row_index(slot[...], prow[...])
    for source, target in ((dist[...], pair_d), (envelope_of(dist[...]), pair_e), (atom[...].astype(F32), pair_a), (index.astype(F32), pair_r)):
        square[0:32, :] = source
        target[...] = square[...].T


    def pair_gates(j, _):
        d = jnp.concatenate([column(pair_d[...], 2 * j + h) for h in range(2)], axis=0)
        e = jnp.concatenate([column(pair_e[...], 2 * j + h) for h in range(2)], axis=0)
        gate_o[pl.ds(pl.multiple_of(j * 256, 256), 256), :] = gate_of(d, e, w_rin[...], w_rout[...])
        return 0


    lax.fori_loop(0, PAIRS // 256, pair_gates, 0, unroll=4)
    lax.fori_loop(0, NEAR_CELLS // WIDE, slots, 0)
    lax.fori_loop(0, FAR_CELLS, far_rows, 0)
    send_blocks_of(NEAR_CELLS // WIDE - 1)

    def pairs(j, _):
        index_l = jnp.concatenate([column(pair_a[...], 2 * j + h) for h in range(2)], axis=0)
        index_r = jnp.concatenate([column(pair_r[...], 2 * j + h) for h in range(2)], axis=0)
        left_rows = dot(one_hot(index_l, D), left[...])
        right_rows = dot(one_hot(index_r, CELLS * FETCH), rows_in[...])
        at = pl.ds(pl.multiple_of(j * 256, 256), 256)
        edge = (left_rows * right_rows * gate_o[at, :]).astype(BF16)
        mixed = silu(dot(edge, w_mix[...])).astype(BF16)
        own[:, at] = dot_nt(w_own[...], mixed)[0:BLOCK].astype(BF16)
        return 0

    def to_sides(b):
        hop_copy(b).wait_recv()
        for dx in range(1, X):
            side_copy(b, dx).start()
        for which in range(2):
            near_copy(b * X, which).start()

    def to_strips(b):
        for dx in range(1, X):
            side_copy(b, dx).wait_recv()
            for which in range(2):
                near_copy(b * X + dx, which).start()

    def pairs_of(i, _):
        for h in range(4):
            pairs(4 * i + h, 0)

        @pl.when(i == 0)
        def _():
            to_sides(0)
            to_sides(1)
            to_sides(2)

        @pl.when(i == 2)
        def _():
            to_strips(0)
            to_strips(1)
            to_strips(2)
        return 0

    lax.fori_loop(0, PAIRS // 1024, pairs_of, 0)

    own_block.wait()
    block_copy(0, 0, me).wait()
    block_copy(0, 2, me).wait()
    parity = lax.rem(me, 2)

    def unpack(n, _):
        o = lax.rem(n, 3)
        x = lax.rem(lax.div(n, 3) + lax.div(me, Z), X)
        rank = lax.div(n, 3 * X)
        middle = lax.div(rank + 2, 3) * (1 + 2 * lax.rem(rank + parity, 2))
        shift = lax.rem(middle * lax.div(3 - rank + 2, 3) + 2 * lax.div(rank, 3), 4)
        even = x * Z + 2 * lax.rem(lax.div(lax.rem(me, Z), 2) + shift, 4)
        for h in range(2):
            away = lax.rem(lax.rem(even, Z) + h - lax.rem(me, Z) + Z + 2, Z)

            @pl.when((even + h != me) & (away < NEAR))
            def _():
                block_copy(0, o, even + h).wait_recv()
        base = o * CELLS + even
        first = blk_in[base].astype(F32)
        second = blk_in[base + 1].astype(F32)
        top = jnp.where(low, first, pltpu.roll(second, SLOT, 1))
        bottom = jnp.where(low, pltpu.roll(first, SLOT, 1), second)
        partner[:, pl.ds(pl.multiple_of(base * SLOT, 128), 128)] = jnp.concatenate([top, bottom], axis=0)[0:BLOCK].astype(BF16)
        return 0

    def far(b, _):
        groups = [(o, dx) for o in range(3) for dx in range(X)]
        cells = [cell_at(far_step(b, dx), 1) for dx in range(X)]
        for dx in range(X):
            for which in range(2):
                near_copy(b * X + dx, which).wait_recv()
        for g, (o, dx) in enumerate(groups):
            scalar_copy(b * X + dx, o).wait_recv()
            turn_a[g:g + 1, :] = scal_in[3 * (b * X + dx) + o, 0:1, :]
            turn_b[g:g + 1, :] = scal_in[3 * (b * X + dx) + o, 1:2, :]
        square[0:16, :] = envelope_of(turn_a[0:16, :])
        values, places, envelopes = turn_a[...].T, turn_b[...].T, square[...].T
        d = jnp.concatenate([values[0:SLOT, g:g + 1] for g in range(12)], axis=0)
        e = jnp.concatenate([envelopes[0:SLOT, g:g + 1] for g in range(12)], axis=0)
        m = jnp.concatenate([places[0:SLOT, g:g + 1] + float((g - o) * PART) for g, (o, dx) in enumerate(groups)], axis=0)
        gate = gate_of(d, e, w_rin[...], w_rout[...])
        entries = (list_n[1], list_s[PART:2 * PART, :], list_n[0])
        index = jnp.concatenate([column(entries[o], cells[dx]) for o, dx in groups], axis=0)
        rows = dot(one_hot(index, D), tables[1]).astype(BF16)
        right_rows = dot(one_hot(m, 12 * PART), rows)
        picked = jnp.concatenate(
            [dot(one_hot(values[SLOT:2 * SLOT, g:g + 1], D), far_f[2 - o, b * X + dx]).astype(BF16) for g, (o, dx) in enumerate(groups)], axis=0
        )
        left_rows = dot(picked, w_left[...]).astype(BF16).astype(F32)
        edge = (left_rows * right_rows * gate).astype(BF16)
        mixed = silu(dot(edge, w_mix[...])).astype(BF16)
        out = dot_nt(w_flip[...], mixed)
        for o in range(3):
            for h in range(0, X, 2):
                first, second = halves(out, o, h)
                blk_in[o * CELLS + cells[h]] = first
                blk_in[o * CELLS + cells[h + 1]] = second
        return 0

    lax.fori_loop(0, GROUPS // 4, unpack, 0)
    lax.fori_loop(0, FAR, far, 0)
    lax.fori_loop(GROUPS // 4, GROUPS // 2, unpack, 0)

    def finish(k, _):
        for o in range(3):
            row_copy(k, o, me).wait_send()
        return 0

    lax.fori_loop(1, CELLS, finish, 0)

    def finish_blocks(n, _):
        for o in range(3):
            block_copy(near_step(n), o, me).wait_send()
        return 0

    lax.fori_loop(1, NEAR_CELLS, finish_blocks, 0)

    def finish_far(n, _):
        for o in range(3):
            scalar_copy(n, o).wait_send()
        for which in range(2):
            near_copy(n, which).wait_send()
        return 0

    lax.fori_loop(0, FAR_CELLS, finish_far, 0)
    for b in range(FAR):
        hop_copy(b).wait_send()
        for dx in range(1, X):
            side_copy(b, dx).wait_send()


def output_kernel(own_in, partner_in, own, partner, sem):
    copies = [pltpu.make_async_copy(own_in, own, sem.at[0]), pltpu.make_async_copy(partner_in, partner, sem.at[1])]
    for copy in copies:
        copy.start()
    for copy in copies:
        copy.wait()


def body(features, pair_atom, partner_row, transpose_slot, distance, send_rows, w_left, w_right, w_radial_in, w_radial_out, w_mix, w_out):
    vmem = pl.BlockSpec(memory_space=pltpu.VMEM)
    hbm = pl.BlockSpec(memory_space=pltpu.HBM)
    sem = pltpu.SemaphoreType.DMA
    outputs = (
        jax.ShapeDtypeStruct((BLOCK, PAIRS), BF16),
        jax.ShapeDtypeStruct((BLOCK, GROUPS * SLOT), BF16),
    )
    own, partner = pl.pallas_call(
        main_kernel,
        out_shape=outputs,
        in_specs=[hbm] * 12,
        out_specs=(vmem, vmem),
        scratch_shapes=[
            pltpu.VMEM((D, D), BF16),
            *[pltpu.VMEM((32, 128), jnp.int32)] * 3,
            pltpu.VMEM((32, 128), F32),
            pltpu.VMEM((CELLS, FETCH), jnp.int32),
            pltpu.VMEM((D, D), BF16),
            pltpu.VMEM((D, D), BF16),
            pltpu.VMEM((COUNT, D), BF16),
            pltpu.VMEM((D, D), BF16),
            pltpu.VMEM((D, D), BF16),
            pltpu.VMEM((BLOCK, D), BF16),
            pltpu.VMEM((D, D), BF16),
            pltpu.VMEM((2, D, D), BF16),
            pltpu.VMEM((2, CELLS, FETCH), jnp.int32),
            pltpu.VMEM((3, FAR_CELLS, D, D), BF16),
            pltpu.VMEM((3 * FAR_CELLS, 2, 128), F32),
            pltpu.VMEM((3 * FAR_CELLS, 2, 128), F32),
            pltpu.VMEM((3, D, D), BF16),
            pltpu.VMEM((D, D), BF16),
            pltpu.VMEM((3, CELLS * PART, D), BF16),
            pltpu.VMEM((CELLS * FETCH, D), BF16),
            pltpu.VMEM((GROUPS * SLOT, D), F32),
            pltpu.VMEM((PAIRS, D), F32),
            pltpu.VMEM((CELLS, 3, HALF, 128), BF16),
            pltpu.VMEM((GROUPS, HALF, 128), BF16),
            *[pltpu.VMEM((SLOT, 128), F32)] * 4,
            *[pltpu.VMEM((128, 128), F32)] * 5,
            pltpu.VMEM((FETCH, 128), F32),
            pltpu.VMEM((2, PART, 128), F32),
            *[pltpu.VMEM((128, 128), F32)] * 3,
            pltpu.VMEM((2 * HALF, D), BF16),
            pltpu.VMEM((2 * HALF, D), BF16),
            sem((12,)), *[sem((2,))] * 4, *[sem((FAR,))] * 2, *[sem((FAR, X - 1))] * 2,
            *[sem((FAR_CELLS, 2))] * 2, *[sem((FAR_CELLS, 3))] * 2, sem((CELLS, 3)), sem((CELLS, 3)), sem((CELLS, 3)), sem((CELLS, 3)), sem((4,)),
        ],
        compiler_params=pltpu.CompilerParams(collective_id=0, has_side_effects=True, vmem_limit_bytes=48 << 20),
    )(*[pltpu.with_memory_space_constraint(a, pltpu.HBM) for a in (
        features,
        pair_atom.reshape(32, 128),
        partner_row.reshape(32, 128),
        transpose_slot.reshape(32, 128),
        distance.reshape(32, 128),
        send_rows, w_left, w_right, w_radial_in, w_radial_out, w_mix, w_out.T,
    )])
    return pl.pallas_call(
        output_kernel,
        out_shape=outputs,
        in_specs=[vmem, vmem],
        out_specs=(hbm, hbm),
        scratch_shapes=[sem((2,))],
        compiler_params=pltpu.CompilerParams(vmem_limit_bytes=16 << 20),
    )(own, partner)


def solution(mesh):
    both = P(("strip", "cell"))
    rows = P(("strip", "cell"), None)
    in_specs = (rows, both, both, both, both, rows, P(), P(), P(), P(), P(), P())
    out_specs = (P(None, ("strip", "cell")), P(None, ("strip", "cell")))
    return jax.shard_map(body, mesh=mesh, in_specs=in_specs, out_specs=out_specs, check_vma=False)
```

```python
import functools

import jax
import jax.numpy as jnp
import numpy as np
from jax import lax
from jax.experimental import pallas as pl
from jax.experimental.pallas import tpu as pltpu
from jax.sharding import PartitionSpec as P

MESH = pl.DeviceIdType.MESH
F32 = jnp.float32
BF16 = jnp.bfloat16
D = 256
BLOCK = 169
ORB = 13
HALF = 88
FETCH = 48
SLOT = 64
CELLS = 32
STRIPS = 8
Z = 8
X = 4
PAIRS = 4096
GROUPS = 96
CUTOFF = 8.0
COUNT = 128
PART = 16
EARLY = 2
WIDE = 4
SPAN = 3 * WIDE * SLOT
NEAR = 7
FAR = Z - NEAR
NEAR_CELLS = NEAR * X
FAR_CELLS = FAR * X


def silu(x):
    half = 0.5 * x
    return half + half * jnp.tanh(half)


def offset_of(k):
    late = lax.div(k, NEAR_CELLS)
    n = k - late * NEAR_CELLS
    j = (1 - late) * lax.rem(k, NEAR) + late * (NEAR + lax.div(n, X))
    hop = lax.div(j + 1, 2) * (2 * lax.rem(j, 2) - 1)
    return (1 - late) * lax.div(k, NEAR) + late * lax.rem(n, X), hop


def cell_at(k, sign):
    c = lax.axis_index("cell")
    dx, dz = offset_of(k)
    x = lax.rem(lax.div(c, Z) + sign * dx + X, X)
    z = lax.rem(lax.rem(c, Z) + sign * dz + Z, Z)
    return x * Z + z


def strip_at(step):
    return lax.rem(lax.axis_index("strip") + step + STRIPS, STRIPS)


def column(values, lane):
    lanes = lax.broadcasted_iota(jnp.int32, values.shape, 1)
    return jnp.sum(jnp.where(lanes == lane, values, 0.0), axis=1, keepdims=True)


def one_hot(index, width):
    lanes = lax.broadcasted_iota(jnp.int32, (index.shape[0], width), 1).astype(F32)
    return jnp.where(lanes == index, 1.0, 0.0).astype(BF16)


def dot(a, b):
    return jnp.dot(a, b, preferred_element_type=F32)


def dot_nt(a, b):
    return lax.dot_general(a, b, (((1,), (1,)), ((), ())), preferred_element_type=F32)


def row_index(slot, row):
    offset = lax.shift_right_logical(slot, 11)
    base = FETCH * (lax.shift_right_logical(slot, 6) & (CELLS - 1))
    part = lax.shift_right_logical((row - base - offset) * 171, 9)
    return base + offset * PART + part


def envelope_of(distance):
    return 0.5 * (jnp.cos(jnp.pi * distance / CUTOFF) + 1.0)


def gate_of(distance, envelope, w_in, w_out):
    centers = lax.broadcasted_iota(jnp.int32, (1, COUNT), 1).astype(F32) * (CUTOFF / (COUNT - 1))
    scaled = (distance - centers) * (COUNT / (2.0 * CUTOFF))
    basis = (jnp.exp(-scaled * scaled) * envelope).astype(BF16)
    radial = silu(dot(basis, w_in)).astype(BF16)
    return dot(radial, w_out)


def main_kernel(
    feat_h, atom_h, prow_h, slot_h, dist_h, lists_h, w_left_h, w_right_h, w_rin_h, w_rout_h, w_mix_h, w_out_h,
    own, partner,
    feat, atom, prow, slot, dist, lists, w_left, w_right, w_rin, w_rout, w_mix, w_raw, w_out,
    feat_in, list_in, far_f, scal_out, scal_in, tables, left, rows_out, rows_in, gate_s, gate_o, blk_out, blk_in,
    slot_d, slot_e, slot_a, slot_m, pair_d, pair_e, pair_a, pair_r, list_t, list_s, list_n, turn_a, turn_b,
    square, w_own, w_flip,
    in_sem, feat_ss, feat_rs, list_ss, list_rs, hop_ss, hop_rs, side_ss, side_rs, near_ss, near_rs, scal_ss, scal_rs, rows_ss, rows_rs, blk_ss, blk_rs, local_sem,
):
    me = lax.axis_index("cell")
    sources = (feat_h, w_left_h, w_right_h, lists_h, slot_h, dist_h, atom_h, prow_h, w_out_h, w_rin_h, w_rout_h, w_mix_h)
    targets = (feat, w_left, w_right, lists, slot, dist, atom, prow, w_raw, w_rin, w_rout, w_mix)
    loads = [pltpu.make_async_copy(a, b, in_sem.at[n]) for n, (a, b) in enumerate(zip(sources, targets))]
    for load in loads:
        load.start()

    barrier = pltpu.get_barrier_semaphore()

    def greet(k, _):
        c = cell_at(k, 1)
        for step in (-1, 0, 1):
            if step:
                pl.semaphore_signal(barrier, inc=1, device_id=(strip_at(step), c), device_id_type=MESH)
            else:
                @pl.when(k > 0)
                def _():
                    pl.semaphore_signal(barrier, inc=1, device_id=(strip_at(0), c), device_id_type=MESH)
        return 0

    lax.fori_loop(0, CELLS, greet, 0)
    for load in loads:
        load.wait()

    left[...] = dot(feat[...], w_left[...]).astype(BF16)
    tables[1] = dot(feat[...], w_right[...]).astype(BF16)

    square[...] = jnp.zeros_like(square)
    square[0:32, 0:FETCH] = lists[...].astype(F32)
    list_t[...] = square[...].T
    for o in range(3):
        list_s[pl.ds(o * PART, PART), :] = list_t[pl.ds(o, PART, stride=3), :] - float(o * D)

    def pick(o, i):
        index = jnp.concatenate(
            [column(list_s[pl.ds(pl.multiple_of(o * PART, PART), PART), :], cell_at(8 * i + h, 1)) for h in range(8)], axis=0
        )
        picked = dot(one_hot(index, D), tables[o]).astype(BF16)
        rows_out[o, pl.ds(pl.multiple_of(i * 8 * PART, 128), 8 * PART), :] = picked

    def pick_own(i, _):
        pick(1, i)
        return 0

    lax.fori_loop(0, CELLS // 8, pick_own, 0)

    def place(j, total):
        left_parts, right_parts = [], []
        for h in range(2):
            at = pl.ds(2 * j + h, 1)
            t = slot[at, :]
            d = dist[at, :]
            d_hi = d.astype(BF16).astype(F32)
            d_mid = (d - d_hi).astype(BF16).astype(F32)
            d_lo = d - d_hi - d_mid
            index = row_index(t, prow[at, :]) - FETCH * (lax.shift_right_logical(t, 6) & (CELLS - 1))
            hit = lax.broadcasted_iota(jnp.int32, (SLOT, 128), 0) == (t & (SLOT - 1))
            parts = (d_hi, d_mid, d_lo, (atom[at, :] + 1).astype(F32), index.astype(F32))
            left_parts.append(jnp.concatenate([jnp.where(hit, v, 0.0) for v in parts], axis=0))
            group = lax.broadcasted_iota(jnp.int32, (128, 128), 0) == lax.shift_right_logical(t, 6)
            right_parts.append(jnp.where(group, 1.0, 0.0))
        return total + dot_nt(
            jnp.concatenate(left_parts, axis=1).astype(BF16), jnp.concatenate(right_parts, axis=1).astype(BF16)
        )

    total = lax.fori_loop(0, PAIRS // 256, place, jnp.zeros((5 * SLOT, 128), F32))
    d = total[0:SLOT] + total[SLOT:2 * SLOT] + total[2 * SLOT:3 * SLOT]
    slot_d[...] = d
    slot_e[...] = envelope_of(d)
    slot_a[...] = total[3 * SLOT:4 * SLOT] - 1.0
    slot_m[...] = total[4 * SLOT:5 * SLOT]
    turn_a[...] = jnp.concatenate([d, total[3 * SLOT:4 * SLOT] - 1.0], axis=0).T
    turn_b[...] = jnp.concatenate([total[4 * SLOT:5 * SLOT], jnp.zeros((SLOT, 128), F32)], axis=0).T

    def pack_scalars(n, _):
        c = cell_at(NEAR_CELLS + n, -1)
        for o in range(3):
            scal_out[3 * n + o, 0:1, :] = turn_a[pl.ds(o * CELLS + c, 1), :]
            scal_out[3 * n + o, 1:2, :] = turn_b[pl.ds(o * CELLS + c, 1), :]
        return 0

    lax.fori_loop(0, FAR_CELLS, pack_scalars, 0)

    pl.semaphore_wait(barrier, 3 * CELLS - 1)

    def feature_copy(which):
        return pltpu.make_async_remote_copy(
            src_ref=feat, dst_ref=feat_in.at[which], send_sem=feat_ss.at[which], recv_sem=feat_rs.at[which],
            device_id=(strip_at(1 - 2 * which), me), device_id_type=MESH,
        )

    def row_copy(k, o, sender):
        return pltpu.make_async_remote_copy(
            src_ref=rows_out.at[o, pl.ds(pl.multiple_of(k * PART, PART), PART)],
            dst_ref=rows_in.at[pl.ds(pl.multiple_of(me * FETCH + o * PART, PART), PART)],
            send_sem=rows_ss.at[o], recv_sem=rows_rs.at[sender, o],
            device_id=(strip_at(0), cell_at(k, 1)), device_id_type=MESH,
        )

    def own_rows(o):
        return pltpu.make_async_copy(
            rows_out.at[o, pl.ds(0, PART)], rows_in.at[pl.ds(pl.multiple_of(me * FETCH + o * PART, PART), PART)], local_sem.at[o]
        )

    def send_rows_of(o, i):
        for h in range(8):
            if h:
                row_copy(8 * i + h, o, me).start()
            else:
                @pl.when(i == 0)
                def _():
                    own_rows(o).start()

                @pl.when(i > 0)
                def _():
                    row_copy(8 * i, o, me).start()

    def list_copy(which):
        return pltpu.make_async_remote_copy(
            src_ref=lists, dst_ref=list_in.at[which], send_sem=list_ss.at[which], recv_sem=list_rs.at[which],
            device_id=(strip_at(1 - 2 * which), me), device_id_type=MESH,
        )

    def far_step(b, dx):
        return NEAR_CELLS + b * X + dx

    def hop_copy(b):
        return pltpu.make_async_remote_copy(
            src_ref=feat, dst_ref=far_f.at[1, b * X], send_sem=hop_ss.at[b], recv_sem=hop_rs.at[b],
            device_id=(strip_at(0), cell_at(far_step(b, 0), -1)), device_id_type=MESH,
        )

    def side_copy(b, dx):
        return pltpu.make_async_remote_copy(
            src_ref=far_f.at[1, b * X], dst_ref=far_f.at[1, b * X + dx],
            send_sem=side_ss.at[b, dx - 1], recv_sem=side_rs.at[b, dx - 1],
            device_id=(strip_at(0), cell_at(dx * NEAR, -1)), device_id_type=MESH,
        )

    def near_copy(n, which):
        return pltpu.make_async_remote_copy(
            src_ref=far_f.at[1, n], dst_ref=far_f.at[2 * which, n],
            send_sem=near_ss.at[which], recv_sem=near_rs.at[n, which],
            device_id=(strip_at(1 - 2 * which), me), device_id_type=MESH,
        )

    def scalar_copy(n, o):
        k = far_step(lax.div(n, X), lax.rem(n, X))
        return pltpu.make_async_remote_copy(
            src_ref=scal_out.at[3 * n + o], dst_ref=scal_in.at[3 * n + o],
            send_sem=scal_ss.at[0], recv_sem=scal_rs.at[n, o],
            device_id=(strip_at(o - 1), cell_at(k, -1)), device_id_type=MESH,
        )

    for which in range(2):
        feature_copy(which).start()
        list_copy(which).start()
    for b in range(FAR):
        hop_copy(b).start()

    def send_own_part(i, _):
        send_rows_of(1, i)
        return 0

    lax.fori_loop(0, CELLS // 8, send_own_part, 0)

    def near_step(n):
        return n

    def slot_columns(source, i):
        cells = [cell_at(near_step(WIDE * i + h), -1) for h in range(WIDE)]
        return jnp.concatenate([column(source[...], o * CELLS + c) for o in range(3) for c in cells], axis=0)

    def slot_gates(i, _):
        gate_s[pl.ds(pl.multiple_of(i * SPAN, 128), SPAN), :] = gate_of(
            slot_columns(slot_d, i), slot_columns(slot_e, i), w_rin[...], w_rout[...]
        )
        return 0

    early = EARLY
    lax.fori_loop(0, early, slot_gates, 0)

    for which in range(2):
        feature_copy(which).wait()
        tables[2 * which] = dot(feat_in[which], w_right[...]).astype(BF16)

    def rest(i):
        return 2 * lax.div(i, 4), lax.rem(i, 4)

    def pick_rest(i, _):
        pick(*rest(i))

        @pl.when(i > 0)
        def _():
            send_rows_of(*rest(i - 1))
        return 0

    lax.fori_loop(0, CELLS // 4, pick_rest, 0)
    lax.fori_loop(early, early + 1, slot_gates, 0)
    send_rows_of(2, CELLS // 8 - 1)
    def send_scalars(n, _):
        for o in range(3):
            scalar_copy(n, o).start()
        return 0

    lax.fori_loop(0, FAR_CELLS, send_scalars, 0)
    for which in range(2):
        list_copy(which).wait()
        square[0:32, 0:FETCH] = list_in[which].astype(F32)
        list_t[...] = square[...].T
        list_n[which] = list_t[pl.ds(2 - 2 * which, PART, stride=3), :] - float((2 - 2 * which) * D)
    lax.fori_loop(early + 1, NEAR_CELLS // WIDE, slot_gates, 0)

    def block_copy(k, o, sender):
        return pltpu.make_async_remote_copy(
            src_ref=blk_out.at[k, o], dst_ref=blk_in.at[o * CELLS + me],
            send_sem=blk_ss.at[k, o], recv_sem=blk_rs.at[sender, o],
            device_id=(strip_at(o - 1), cell_at(k, -1)), device_id_type=MESH,
        )

    own_block = pltpu.make_async_copy(blk_out.at[0, 1], blk_in.at[CELLS + me], local_sem.at[3])

    def send_blocks_of(i):
        for h in range(WIDE):
            for o in range(3):
                if h or o != 1:
                    block_copy(near_step(WIDE * i + h), o, me).start()
                else:
                    @pl.when(i == 0)
                    def _():
                        own_block.start()

                    @pl.when(i > 0)
                    def _():
                        block_copy(near_step(WIDE * i), 1, me).start()

    low = lax.broadcasted_iota(jnp.int32, (HALF, 128), 1) < SLOT

    def halves(out, o, h):
        start = (o * WIDE + h) * SLOT
        top = out[0:HALF, start:start + 128]
        bottom = out[HALF:2 * HALF, start:start + 128]
        return (
            jnp.where(low, top, pltpu.roll(bottom, SLOT, 1)).astype(BF16),
            jnp.where(low, pltpu.roll(top, SLOT, 1), bottom).astype(BF16),
        )

    def far_rows(n, _):
        k = far_step(lax.div(n, X), lax.rem(n, X))
        for o in range(3):
            row_copy(k, o, cell_at(k, -1)).wait_recv()
        return 0

    def slots(i, _):
        cells = [cell_at(near_step(WIDE * i + h), -1) for h in range(WIDE)]
        for o in range(3):
            @pl.when(i == 0)
            def _():
                own_rows(o).wait()

            @pl.when(i > 0)
            def _():
                row_copy(near_step(WIDE * i), o, cells[0]).wait_recv()
            for h in range(1, WIDE):
                row_copy(near_step(WIDE * i + h), o, cells[h]).wait_recv()
        rows = jnp.concatenate([rows_in[pl.ds(pl.multiple_of(c * FETCH, PART), FETCH), :] for c in cells], axis=0)
        second = lax.rem(lax.div(lax.broadcasted_iota(jnp.int32, (SPAN, 1), 0), SLOT), WIDE) * FETCH
        left_rows = dot(one_hot(slot_columns(slot_a, i), D), left[...])
        right_rows = dot(one_hot(slot_columns(slot_m, i) + second.astype(F32), WIDE * FETCH), rows)
        gate = gate_s[pl.ds(pl.multiple_of(i * SPAN, 128), SPAN), :]
        edge = (left_rows * right_rows * gate).astype(BF16)
        mixed = silu(dot(edge, w_mix[...])).astype(BF16)
        out = dot_nt(w_flip[...], mixed)
        for o in range(3):
            for h in range(0, WIDE, 2):
                first, second = halves(out, o, h)
                blk_out[near_step(WIDE * i + h), o] = first
                blk_out[near_step(WIDE * i + h + 1), o] = second

        @pl.when(i > 0)
        def _():
            send_blocks_of(i - 1)
        return 0

    entry = lax.broadcasted_iota(jnp.int32, (2 * HALF, D), 0)
    lane = lax.broadcasted_iota(jnp.int32, (2 * HALF, D), 1)
    quotient = lax.shift_right_logical(entry * 79, 10)
    flipped = (entry - quotient * ORB) * ORB + quotient
    w_out[...] = jnp.zeros_like(w_out)
    w_out[0:BLOCK, :] = w_raw[...]
    w_own[...] = w_out[0:2 * HALF, :]
    w_flip[...] = dot(jnp.where((entry < BLOCK) & (lane == flipped), 1.0, 0.0).astype(BF16), w_out[...]).astype(BF16)

    index = row_index(slot[...], prow[...])
    for source, target in ((dist[...], pair_d), (envelope_of(dist[...]), pair_e), (atom[...].astype(F32), pair_a), (index.astype(F32), pair_r)):
        square[0:32, :] = source
        target[...] = square[...].T


    def to_sides(b):
        hop_copy(b).wait_recv()
        for dx in range(1, X):
            side_copy(b, dx).start()
        for which in range(2):
            near_copy(b * X, which).start()

    def to_strips(b):
        for dx in range(1, X):
            side_copy(b, dx).wait_recv()
            for which in range(2):
                near_copy(b * X + dx, which).start()

    def pair_gates(j, _):
        d = jnp.concatenate([column(pair_d[...], 2 * j + h) for h in range(2)], axis=0)
        e = jnp.concatenate([column(pair_e[...], 2 * j + h) for h in range(2)], axis=0)
        gate_o[pl.ds(pl.multiple_of(j * 256, 256), 256), :] = gate_of(d, e, w_rin[...], w_rout[...])
        return 0


    lax.fori_loop(0, PAIRS // 256, pair_gates, 0, unroll=4)
    for b in range(FAR):
        to_sides(b)
    lax.fori_loop(0, NEAR_CELLS // WIDE, slots, 0)
    lax.fori_loop(0, FAR_CELLS, far_rows, 0)
    send_blocks_of(NEAR_CELLS // WIDE - 1)

    def pairs(j, _):
        index_l = jnp.concatenate([column(pair_a[...], 2 * j + h) for h in range(2)], axis=0)
        index_r = jnp.concatenate([column(pair_r[...], 2 * j + h) for h in range(2)], axis=0)
        left_rows = dot(one_hot(index_l, D), left[...])
        right_rows = dot(one_hot(index_r, CELLS * FETCH), rows_in[...])
        at = pl.ds(pl.multiple_of(j * 256, 256), 256)
        edge = (left_rows * right_rows * gate_o[at, :]).astype(BF16)
        mixed = silu(dot(edge, w_mix[...])).astype(BF16)
        own[:, at] = dot_nt(w_own[...], mixed)[0:BLOCK].astype(BF16)
        return 0

    def pairs_of(i, _):
        for h in range(4):
            pairs(4 * i + h, 0)

        @pl.when(i == 3)
        def _():
            to_strips(0)
        return 0

    lax.fori_loop(0, PAIRS // 1024, pairs_of, 0)

    own_block.wait()
    block_copy(0, 0, me).wait()
    block_copy(0, 2, me).wait()
    parity = lax.rem(me, 2)

    def unpack(n, _):
        o = lax.rem(n, 3)
        x = lax.rem(lax.div(n, 3) + lax.div(me, Z), X)
        rank = lax.div(n, 3 * X)
        middle = lax.div(rank + 2, 3) * (1 + 2 * lax.rem(rank + parity, 2))
        shift = lax.rem(middle * lax.div(3 - rank + 2, 3) + 2 * lax.div(rank, 3), 4)
        even = x * Z + 2 * lax.rem(lax.div(lax.rem(me, Z), 2) + shift, 4)
        for h in range(2):
            away = lax.rem(lax.rem(even, Z) + h - lax.rem(me, Z) + Z + NEAR // 2, Z)

            @pl.when((even + h != me) & (away < NEAR))
            def _():
                block_copy(0, o, even + h).wait_recv()
        base = o * CELLS + even
        first = blk_in[base].astype(F32)
        second = blk_in[base + 1].astype(F32)
        top = jnp.where(low, first, pltpu.roll(second, SLOT, 1))
        bottom = jnp.where(low, pltpu.roll(first, SLOT, 1), second)
        partner[:, pl.ds(pl.multiple_of(base * SLOT, 128), 128)] = jnp.concatenate([top, bottom], axis=0)[0:BLOCK].astype(BF16)
        return 0

    def far(b, _):
        groups = [(o, dx) for o in range(3) for dx in range(X)]
        cells = [cell_at(far_step(b, dx), 1) for dx in range(X)]
        for dx in range(X):
            for which in range(2):
                near_copy(b * X + dx, which).wait_recv()
        for g, (o, dx) in enumerate(groups):
            scalar_copy(b * X + dx, o).wait_recv()
            turn_a[g:g + 1, :] = scal_in[3 * (b * X + dx) + o, 0:1, :]
            turn_b[g:g + 1, :] = scal_in[3 * (b * X + dx) + o, 1:2, :]
        square[0:16, :] = envelope_of(turn_a[0:16, :])
        values, places, envelopes = turn_a[...].T, turn_b[...].T, square[...].T
        d = jnp.concatenate([values[0:SLOT, g:g + 1] for g in range(12)], axis=0)
        e = jnp.concatenate([envelopes[0:SLOT, g:g + 1] for g in range(12)], axis=0)
        m = jnp.concatenate([places[0:SLOT, g:g + 1] + float((g - o) * PART) for g, (o, dx) in enumerate(groups)], axis=0)
        gate = gate_of(d, e, w_rin[...], w_rout[...])
        entries = (list_n[1], list_s[PART:2 * PART, :], list_n[0])
        index = jnp.concatenate([column(entries[o], cells[dx]) for o, dx in groups], axis=0)
        rows = dot(one_hot(index, D), tables[1]).astype(BF16)
        right_rows = dot(one_hot(m, 12 * PART), rows)
        picked = jnp.concatenate(
            [dot(one_hot(values[SLOT:2 * SLOT, g:g + 1], D), far_f[2 - o, b * X + dx]).astype(BF16) for g, (o, dx) in enumerate(groups)], axis=0
        )
        left_rows = dot(picked, w_left[...]).astype(BF16).astype(F32)
        edge = (left_rows * right_rows * gate).astype(BF16)
        mixed = silu(dot(edge, w_mix[...])).astype(BF16)
        out = dot_nt(w_flip[...], mixed)
        for o in range(3):
            for h in range(0, X, 2):
                first, second = halves(out, o, h)
                blk_in[o * CELLS + cells[h]] = first
                blk_in[o * CELLS + cells[h + 1]] = second
        return 0

    lax.fori_loop(0, 3 * GROUPS // 8, unpack, 0)
    lax.fori_loop(0, FAR, far, 0)
    lax.fori_loop(3 * GROUPS // 8, GROUPS // 2, unpack, 0)

    sent = []
    for o in range(3):
        sent.append((rows_out.at[o, pl.ds(PART, (CELLS - 1) * PART)], rows_in.at[pl.ds(0, (CELLS - 1) * PART)], rows_ss.at[o], rows_rs.at[0, o]))
    for which in range(2):
        sent.append((far_f.at[1], far_f.at[2 * which], near_ss.at[which], near_rs.at[0, which]))
    sent.append((scal_out, scal_in, scal_ss.at[0], scal_rs.at[0, 0]))
    for source, target, send_sem, recv_sem in sent:
        pltpu.make_async_remote_copy(
            src_ref=source, dst_ref=target, send_sem=send_sem, recv_sem=recv_sem,
            device_id=(strip_at(1), me), device_id_type=MESH,
        ).wait_send()

    def finish_blocks(n, _):
        for o in range(3):
            block_copy(near_step(n), o, me).wait_send()
        return 0

    lax.fori_loop(1, NEAR_CELLS, finish_blocks, 0)

    for b in range(FAR):
        hop_copy(b).wait_send()
        for dx in range(1, X):
            side_copy(b, dx).wait_send()


def output_kernel(own_in, partner_in, own, partner, sem):
    copies = [pltpu.make_async_copy(own_in, own, sem.at[0]), pltpu.make_async_copy(partner_in, partner, sem.at[1])]
    for copy in copies:
        copy.start()
    for copy in copies:
        copy.wait()


def body(features, pair_atom, partner_row, transpose_slot, distance, send_rows, w_left, w_right, w_radial_in, w_radial_out, w_mix, w_out):
    vmem = pl.BlockSpec(memory_space=pltpu.VMEM)
    hbm = pl.BlockSpec(memory_space=pltpu.HBM)
    sem = pltpu.SemaphoreType.DMA
    outputs = (
        jax.ShapeDtypeStruct((BLOCK, PAIRS), BF16),
        jax.ShapeDtypeStruct((BLOCK, GROUPS * SLOT), BF16),
    )
    own, partner = pl.pallas_call(
        main_kernel,
        out_shape=outputs,
        in_specs=[hbm] * 12,
        out_specs=(vmem, vmem),
        scratch_shapes=[
            pltpu.VMEM((D, D), BF16),
            *[pltpu.VMEM((32, 128), jnp.int32)] * 3,
            pltpu.VMEM((32, 128), F32),
            pltpu.VMEM((CELLS, FETCH), jnp.int32),
            pltpu.VMEM((D, D), BF16),
            pltpu.VMEM((D, D), BF16),
            pltpu.VMEM((COUNT, D), BF16),
            pltpu.VMEM((D, D), BF16),
            pltpu.VMEM((D, D), BF16),
            pltpu.VMEM((BLOCK, D), BF16),
            pltpu.VMEM((D, D), BF16),
            pltpu.VMEM((2, D, D), BF16),
            pltpu.VMEM((2, CELLS, FETCH), jnp.int32),
            pltpu.VMEM((3, FAR_CELLS, D, D), BF16),
            pltpu.VMEM((3 * FAR_CELLS, 2, 128), F32),
            pltpu.VMEM((3 * FAR_CELLS, 2, 128), F32),
            pltpu.VMEM((3, D, D), BF16),
            pltpu.VMEM((D, D), BF16),
            pltpu.VMEM((3, CELLS * PART, D), BF16),
            pltpu.VMEM((CELLS * FETCH, D), BF16),
            pltpu.VMEM((GROUPS * SLOT, D), F32),
            pltpu.VMEM((PAIRS, D), F32),
            pltpu.VMEM((CELLS, 3, HALF, 128), BF16),
            pltpu.VMEM((GROUPS, HALF, 128), BF16),
            *[pltpu.VMEM((SLOT, 128), F32)] * 4,
            *[pltpu.VMEM((128, 128), F32)] * 5,
            pltpu.VMEM((FETCH, 128), F32),
            pltpu.VMEM((2, PART, 128), F32),
            *[pltpu.VMEM((128, 128), F32)] * 3,
            pltpu.VMEM((2 * HALF, D), BF16),
            pltpu.VMEM((2 * HALF, D), BF16),
            sem((12,)), *[sem((2,))] * 4, *[sem((FAR,))] * 2, *[sem((FAR, X - 1))] * 2,
            sem((2,)), sem((FAR_CELLS, 2)), sem((1,)), sem((FAR_CELLS, 3)), sem((3,)), sem((CELLS, 3)), sem((CELLS, 3)), sem((CELLS, 3)), sem((4,)),
        ],
        compiler_params=pltpu.CompilerParams(collective_id=0, has_side_effects=True, vmem_limit_bytes=48 << 20),
    )(*[pltpu.with_memory_space_constraint(a, pltpu.HBM) for a in (
        features,
        pair_atom.reshape(32, 128),
        partner_row.reshape(32, 128),
        transpose_slot.reshape(32, 128),
        distance.reshape(32, 128),
        send_rows, w_left, w_right, w_radial_in, w_radial_out, w_mix, w_out.T,
    )])
    return pl.pallas_call(
        output_kernel,
        out_shape=outputs,
        in_specs=[vmem, vmem],
        out_specs=(hbm, hbm),
        scratch_shapes=[sem((2,))],
        compiler_params=pltpu.CompilerParams(vmem_limit_bytes=16 << 20),
    )(own, partner)


def solution(mesh):
    both = P(("strip", "cell"))
    rows = P(("strip", "cell"), None)
    in_specs = (rows, both, both, both, both, rows, P(), P(), P(), P(), P(), P())
    out_specs = (P(None, ("strip", "cell")), P(None, ("strip", "cell")))
    return jax.shard_map(body, mesh=mesh, in_specs=in_specs, out_specs=out_specs, check_vma=False)
```

```python
import functools

import jax
import jax.numpy as jnp
import numpy as np
from jax import lax
from jax.experimental import pallas as pl
from jax.experimental.pallas import tpu as pltpu
from jax.sharding import PartitionSpec as P

MESH = pl.DeviceIdType.MESH
F32 = jnp.float32
BF16 = jnp.bfloat16
D = 256
BLOCK = 169
ORB = 13
HALF = 88
FETCH = 48
SLOT = 64
CELLS = 32
STRIPS = 8
Z = 8
X = 4
PAIRS = 4096
GROUPS = 96
CUTOFF = 8.0
COUNT = 128
PART = 16
EARLY = 2
WIDE = 4
SPAN = 3 * WIDE * SLOT
NEAR = 7
FAR = Z - NEAR
NEAR_CELLS = NEAR * X
FAR_CELLS = FAR * X


def silu(x):
    half = 0.5 * x
    return half + half * jnp.tanh(half)


def offset_of(k):
    late = lax.div(k, NEAR_CELLS)
    n = k - late * NEAR_CELLS
    j = (1 - late) * lax.rem(k, NEAR) + late * (NEAR + lax.div(n, X))
    hop = lax.div(j + 1, 2) * (2 * lax.rem(j, 2) - 1)
    return (1 - late) * lax.div(k, NEAR) + late * lax.rem(n, X), hop


def cell_at(k, sign):
    c = lax.axis_index("cell")
    dx, dz = offset_of(k)
    x = lax.rem(lax.div(c, Z) + sign * dx + X, X)
    z = lax.rem(lax.rem(c, Z) + sign * dz + Z, Z)
    return x * Z + z


def strip_at(step):
    return lax.rem(lax.axis_index("strip") + step + STRIPS, STRIPS)


def column(values, lane):
    lanes = lax.broadcasted_iota(jnp.int32, values.shape, 1)
    return jnp.sum(jnp.where(lanes == lane, values, 0.0), axis=1, keepdims=True)


def one_hot(index, width):
    lanes = lax.broadcasted_iota(jnp.int32, (index.shape[0], width), 1).astype(F32)
    return jnp.where(lanes == index, 1.0, 0.0).astype(BF16)


def dot(a, b):
    return jnp.dot(a, b, preferred_element_type=F32)


def dot_nt(a, b):
    return lax.dot_general(a, b, (((1,), (1,)), ((), ())), preferred_element_type=F32)


def row_index(slot, row):
    offset = lax.shift_right_logical(slot, 11)
    base = FETCH * (lax.shift_right_logical(slot, 6) & (CELLS - 1))
    part = lax.shift_right_logical((row - base - offset) * 171, 9)
    return base + offset * PART + part


def envelope_of(distance):
    return 0.5 * (jnp.cos(jnp.pi * distance / CUTOFF) + 1.0)


def gate_of(distance, envelope, w_in, w_out):
    centers = lax.broadcasted_iota(jnp.int32, (1, COUNT), 1).astype(F32) * (CUTOFF / (COUNT - 1))
    scaled = (distance - centers) * (COUNT / (2.0 * CUTOFF))
    basis = (jnp.exp(-scaled * scaled) * envelope).astype(BF16)
    radial = silu(dot(basis, w_in)).astype(BF16)
    return dot(radial, w_out)


def main_kernel(
    feat_h, atom_h, prow_h, slot_h, dist_h, lists_h, w_left_h, w_right_h, w_rin_h, w_rout_h, w_mix_h, w_out_h,
    own, partner,
    feat, atom, prow, slot, dist, lists, w_left, w_right, w_rin, w_rout, w_mix, w_raw, w_out,
    feat_in, list_in, far_f, scal_out, scal_in, entry_out, entry_in, tables, left, rows_out, rows_in, gate_s, gate_o, blk_out, blk_in,
    slot_d, slot_e, slot_a, slot_m, pair_d, pair_e, pair_a, pair_r, list_t, list_s, list_n, turn_a, turn_b,
    square, w_own, w_flip,
    in_sem, feat_ss, feat_rs, list_ss, list_rs, hop_ss, hop_rs, side_ss, side_rs, near_ss, near_rs, scal_ss, scal_rs, entry_ss, entry_rs, rows_ss, rows_rs, blk_ss, blk_rs, local_sem,
):
    me = lax.axis_index("cell")
    sources = (feat_h, w_left_h, w_right_h, lists_h, slot_h, dist_h, atom_h, prow_h, w_out_h, w_rin_h, w_rout_h, w_mix_h)
    targets = (feat, w_left, w_right, lists, slot, dist, atom, prow, w_raw, w_rin, w_rout, w_mix)
    loads = [pltpu.make_async_copy(a, b, in_sem.at[n]) for n, (a, b) in enumerate(zip(sources, targets))]
    for load in loads:
        load.start()

    barrier = pltpu.get_barrier_semaphore()

    def greet(k, _):
        c = cell_at(k, 1)
        for step in (-1, 0, 1):
            if step:
                pl.semaphore_signal(barrier, inc=1, device_id=(strip_at(step), c), device_id_type=MESH)
            else:
                @pl.when(k > 0)
                def _():
                    pl.semaphore_signal(barrier, inc=1, device_id=(strip_at(0), c), device_id_type=MESH)
        return 0

    lax.fori_loop(0, CELLS, greet, 0)
    for load in loads:
        load.wait()

    left[...] = dot(feat[...], w_left[...]).astype(BF16)
    tables[1] = dot(feat[...], w_right[...]).astype(BF16)

    entry_out[...] = jnp.zeros_like(entry_out)
    for n in range(FAR_CELLS):
        entry_out[n, 0:1, 0:FETCH] = lists[pl.ds(cell_at(NEAR_CELLS + n, -1), 1), :].astype(F32)
    square[...] = jnp.zeros_like(square)
    square[0:32, 0:FETCH] = lists[...].astype(F32)
    list_t[...] = square[...].T
    for o in range(3):
        list_s[pl.ds(o * PART, PART), :] = list_t[pl.ds(o, PART, stride=3), :] - float(o * D)

    def pick(o, i):
        index = jnp.concatenate(
            [column(list_s[pl.ds(pl.multiple_of(o * PART, PART), PART), :], cell_at(8 * i + h, 1)) for h in range(8)], axis=0
        )
        picked = dot(one_hot(index, D), tables[o]).astype(BF16)
        rows_out[o, pl.ds(pl.multiple_of(i * 8 * PART, 128), 8 * PART), :] = picked

    def pick_own(i, _):
        pick(1, i)
        return 0

    lax.fori_loop(0, CELLS // 8, pick_own, 0)

    def place(j, total):
        left_parts, right_parts = [], []
        for h in range(2):
            at = pl.ds(2 * j + h, 1)
            t = slot[at, :]
            d = dist[at, :]
            d_hi = d.astype(BF16).astype(F32)
            d_mid = (d - d_hi).astype(BF16).astype(F32)
            d_lo = d - d_hi - d_mid
            index = row_index(t, prow[at, :]) - FETCH * (lax.shift_right_logical(t, 6) & (CELLS - 1))
            hit = lax.broadcasted_iota(jnp.int32, (SLOT, 128), 0) == (t & (SLOT - 1))
            parts = (d_hi, d_mid, d_lo, (atom[at, :] + 1).astype(F32), index.astype(F32))
            left_parts.append(jnp.concatenate([jnp.where(hit, v, 0.0) for v in parts], axis=0))
            group = lax.broadcasted_iota(jnp.int32, (128, 128), 0) == lax.shift_right_logical(t, 6)
            right_parts.append(jnp.where(group, 1.0, 0.0))
        return total + dot_nt(
            jnp.concatenate(left_parts, axis=1).astype(BF16), jnp.concatenate(right_parts, axis=1).astype(BF16)
        )

    total = lax.fori_loop(0, PAIRS // 256, place, jnp.zeros((5 * SLOT, 128), F32))
    d = total[0:SLOT] + total[SLOT:2 * SLOT] + total[2 * SLOT:3 * SLOT]
    slot_d[...] = d
    slot_e[...] = envelope_of(d)
    slot_a[...] = total[3 * SLOT:4 * SLOT] - 1.0
    slot_m[...] = total[4 * SLOT:5 * SLOT]
    turn_a[...] = jnp.concatenate([d, total[3 * SLOT:4 * SLOT] - 1.0], axis=0).T
    turn_b[...] = jnp.concatenate([total[4 * SLOT:5 * SLOT], jnp.zeros((SLOT, 128), F32)], axis=0).T

    def pack_scalars(n, _):
        c = cell_at(NEAR_CELLS + n, -1)
        for o in range(3):
            scal_out[3 * n + o, 0:1, :] = turn_a[pl.ds(o * CELLS + c, 1), :]
            scal_out[3 * n + o, 1:2, :] = turn_b[pl.ds(o * CELLS + c, 1), :]
        return 0

    lax.fori_loop(0, FAR_CELLS, pack_scalars, 0)

    pl.semaphore_wait(barrier, 3 * CELLS - 1)

    def feature_copy(which):
        return pltpu.make_async_remote_copy(
            src_ref=feat, dst_ref=feat_in.at[which], send_sem=feat_ss.at[which], recv_sem=feat_rs.at[which],
            device_id=(strip_at(1 - 2 * which), me), device_id_type=MESH,
        )

    def row_copy(k, o, sender):
        return pltpu.make_async_remote_copy(
            src_ref=rows_out.at[o, pl.ds(pl.multiple_of(k * PART, PART), PART)],
            dst_ref=rows_in.at[pl.ds(pl.multiple_of(me * FETCH + o * PART, PART), PART)],
            send_sem=rows_ss.at[o], recv_sem=rows_rs.at[sender, o],
            device_id=(strip_at(0), cell_at(k, 1)), device_id_type=MESH,
        )

    def own_rows(o):
        return pltpu.make_async_copy(
            rows_out.at[o, pl.ds(0, PART)], rows_in.at[pl.ds(pl.multiple_of(me * FETCH + o * PART, PART), PART)], local_sem.at[o]
        )

    def send_rows_of(o, i):
        for h in range(8):
            if h >= NEAR_CELLS % 8:
                @pl.when(i < CELLS // 8 - 1)
                def _():
                    row_copy(8 * i + h, o, me).start()
            elif h:
                row_copy(8 * i + h, o, me).start()
            else:
                @pl.when(i == 0)
                def _():
                    own_rows(o).start()

                @pl.when(i > 0)
                def _():
                    row_copy(8 * i, o, me).start()

    def list_copy(which):
        return pltpu.make_async_remote_copy(
            src_ref=lists, dst_ref=list_in.at[which], send_sem=list_ss.at[which], recv_sem=list_rs.at[which],
            device_id=(strip_at(1 - 2 * which), me), device_id_type=MESH,
        )

    def far_step(b, dx):
        return NEAR_CELLS + b * X + dx

    def hop_copy(b):
        return pltpu.make_async_remote_copy(
            src_ref=feat, dst_ref=far_f.at[1, b * X], send_sem=hop_ss.at[b], recv_sem=hop_rs.at[b],
            device_id=(strip_at(0), cell_at(far_step(b, 0), -1)), device_id_type=MESH,
        )

    def side_copy(b, dx):
        return pltpu.make_async_remote_copy(
            src_ref=far_f.at[1, b * X], dst_ref=far_f.at[1, b * X + dx],
            send_sem=side_ss.at[b, dx - 1], recv_sem=side_rs.at[b, dx - 1],
            device_id=(strip_at(0), cell_at(dx * NEAR, -1)), device_id_type=MESH,
        )

    def near_copy(n, which):
        return pltpu.make_async_remote_copy(
            src_ref=far_f.at[1, n], dst_ref=far_f.at[2 * which, n],
            send_sem=near_ss.at[which], recv_sem=near_rs.at[n, which],
            device_id=(strip_at(1 - 2 * which), me), device_id_type=MESH,
        )

    def scalar_copy(n, o):
        k = far_step(lax.div(n, X), lax.rem(n, X))
        return pltpu.make_async_remote_copy(
            src_ref=scal_out.at[3 * n + o], dst_ref=scal_in.at[3 * n + o],
            send_sem=scal_ss.at[0], recv_sem=scal_rs.at[n, o],
            device_id=(strip_at(o - 1), cell_at(k, -1)), device_id_type=MESH,
        )

    def entry_copy(n):
        return pltpu.make_async_remote_copy(
            src_ref=entry_out.at[n], dst_ref=entry_in.at[n], send_sem=entry_ss.at[n], recv_sem=entry_rs.at[n],
            device_id=(strip_at(0), cell_at(NEAR_CELLS + n, -1)), device_id_type=MESH,
        )

    for which in range(2):
        feature_copy(which).start()
        list_copy(which).start()
    for n in range(FAR_CELLS):
        entry_copy(n).start()
    for b in range(FAR):
        hop_copy(b).start()

    def send_own_part(i, _):
        send_rows_of(1, i)
        return 0

    lax.fori_loop(0, CELLS // 8, send_own_part, 0)

    def near_step(n):
        return n

    def slot_columns(source, i):
        cells = [cell_at(near_step(WIDE * i + h), -1) for h in range(WIDE)]
        return jnp.concatenate([column(source[...], o * CELLS + c) for o in range(3) for c in cells], axis=0)

    def slot_gates(i, _):
        gate_s[pl.ds(pl.multiple_of(i * SPAN, 128), SPAN), :] = gate_of(
            slot_columns(slot_d, i), slot_columns(slot_e, i), w_rin[...], w_rout[...]
        )
        return 0

    early = EARLY
    lax.fori_loop(0, early, slot_gates, 0)

    for which in range(2):
        feature_copy(which).wait()
        tables[2 * which] = dot(feat_in[which], w_right[...]).astype(BF16)

    def rest(i):
        return 2 * lax.div(i, 4), lax.rem(i, 4)

    def pick_rest(i, _):
        pick(*rest(i))

        @pl.when(i > 0)
        def _():
            send_rows_of(*rest(i - 1))
        return 0

    lax.fori_loop(0, CELLS // 4, pick_rest, 0)
    lax.fori_loop(early, early + 1, slot_gates, 0)
    send_rows_of(2, CELLS // 8 - 1)
    def send_scalars(n, _):
        for o in range(3):
            scalar_copy(n, o).start()
        return 0

    lax.fori_loop(0, FAR_CELLS, send_scalars, 0)
    for which in range(2):
        list_copy(which).wait()
        square[0:32, 0:FETCH] = list_in[which].astype(F32)
        list_t[...] = square[...].T
        list_n[which] = list_t[pl.ds(2 - 2 * which, PART, stride=3), :] - float((2 - 2 * which) * D)
    lax.fori_loop(early + 1, NEAR_CELLS // WIDE, slot_gates, 0)

    def block_copy(k, o, sender):
        return pltpu.make_async_remote_copy(
            src_ref=blk_out.at[k, o], dst_ref=blk_in.at[o * CELLS + me],
            send_sem=blk_ss.at[k, o], recv_sem=blk_rs.at[sender, o],
            device_id=(strip_at(o - 1), cell_at(k, -1)), device_id_type=MESH,
        )

    own_block = pltpu.make_async_copy(blk_out.at[0, 1], blk_in.at[CELLS + me], local_sem.at[3])

    def send_blocks_of(i):
        for h in range(WIDE):
            for o in range(3):
                if h or o != 1:
                    block_copy(near_step(WIDE * i + h), o, me).start()
                else:
                    @pl.when(i == 0)
                    def _():
                        own_block.start()

                    @pl.when(i > 0)
                    def _():
                        block_copy(near_step(WIDE * i), 1, me).start()

    low = lax.broadcasted_iota(jnp.int32, (HALF, 128), 1) < SLOT

    def halves(out, o, h):
        start = (o * WIDE + h) * SLOT
        top = out[0:HALF, start:start + 128]
        bottom = out[HALF:2 * HALF, start:start + 128]
        return (
            jnp.where(low, top, pltpu.roll(bottom, SLOT, 1)).astype(BF16),
            jnp.where(low, pltpu.roll(top, SLOT, 1), bottom).astype(BF16),
        )

    def slots(i, _):
        cells = [cell_at(near_step(WIDE * i + h), -1) for h in range(WIDE)]
        for o in range(3):
            @pl.when(i == 0)
            def _():
                own_rows(o).wait()

            @pl.when(i > 0)
            def _():
                row_copy(near_step(WIDE * i), o, cells[0]).wait_recv()
            for h in range(1, WIDE):
                row_copy(near_step(WIDE * i + h), o, cells[h]).wait_recv()
        rows = jnp.concatenate([rows_in[pl.ds(pl.multiple_of(c * FETCH, PART), FETCH), :] for c in cells], axis=0)
        second = lax.rem(lax.div(lax.broadcasted_iota(jnp.int32, (SPAN, 1), 0), SLOT), WIDE) * FETCH
        left_rows = dot(one_hot(slot_columns(slot_a, i), D), left[...])
        right_rows = dot(one_hot(slot_columns(slot_m, i) + second.astype(F32), WIDE * FETCH), rows)
        gate = gate_s[pl.ds(pl.multiple_of(i * SPAN, 128), SPAN), :]
        edge = (left_rows * right_rows * gate).astype(BF16)
        mixed = silu(dot(edge, w_mix[...])).astype(BF16)
        out = dot_nt(w_flip[...], mixed)
        for o in range(3):
            for h in range(0, WIDE, 2):
                first, second = halves(out, o, h)
                blk_out[near_step(WIDE * i + h), o] = first
                blk_out[near_step(WIDE * i + h + 1), o] = second

        @pl.when(i > 0)
        def _():
            send_blocks_of(i - 1)
        return 0

    entry = lax.broadcasted_iota(jnp.int32, (2 * HALF, D), 0)
    lane = lax.broadcasted_iota(jnp.int32, (2 * HALF, D), 1)
    quotient = lax.shift_right_logical(entry * 79, 10)
    flipped = (entry - quotient * ORB) * ORB + quotient
    w_out[...] = jnp.zeros_like(w_out)
    w_out[0:BLOCK, :] = w_raw[...]
    w_own[...] = w_out[0:2 * HALF, :]
    w_flip[...] = dot(jnp.where((entry < BLOCK) & (lane == flipped), 1.0, 0.0).astype(BF16), w_out[...]).astype(BF16)

    def to_sides(b):
        hop_copy(b).wait_recv()
        for dx in range(1, X):
            side_copy(b, dx).start()
        for which in range(2):
            near_copy(b * X, which).start()

    def to_strips(b):
        for dx in range(1, X):
            side_copy(b, dx).wait_recv()
            for which in range(2):
                near_copy(b * X + dx, which).start()


    for b in range(FAR):
        to_sides(b)
    lax.fori_loop(0, NEAR_CELLS // WIDE, slots, 0)

    index = row_index(slot[...], prow[...])
    for source, target in ((dist[...], pair_d), (envelope_of(dist[...]), pair_e), (atom[...].astype(F32), pair_a), (index.astype(F32), pair_r)):
        square[0:32, :] = source
        target[...] = square[...].T


    send_blocks_of(NEAR_CELLS // WIDE - 1)
    for b in range(FAR):
        to_strips(b)

    def pair_gates(j, _):
        d = jnp.concatenate([column(pair_d[...], 2 * j + h) for h in range(2)], axis=0)
        e = jnp.concatenate([column(pair_e[...], 2 * j + h) for h in range(2)], axis=0)
        gate_o[pl.ds(pl.multiple_of(j * 256, 256), 256), :] = gate_of(d, e, w_rin[...], w_rout[...])
        return 0

    lax.fori_loop(0, PAIRS // 256, pair_gates, 0, unroll=4)

    for n in range(FAR_CELLS):
        entry_copy(n).wait()
        square[n:n + 1, :] = entry_in[n, 0:1, :]
        for which in range(2):
            near_copy(n, which).wait_recv()
    list_t[...] = square[...].T
    spans = [list_t[pl.ds(o, PART, stride=3), :] - float(o * D) for o in range(3)]
    chosen = jnp.concatenate(
        [dot(one_hot(spans[o][:, n:n + 1], D), far_f[o, n]).astype(BF16) for n in range(FAR_CELLS) for o in range(3)], axis=0
    )
    chosen = dot(chosen, w_right[...]).astype(BF16)
    for n in range(FAR_CELLS):
        rows_in[pl.ds(pl.multiple_of(cell_at(NEAR_CELLS + n, 1) * FETCH, PART), FETCH), :] = chosen[n * FETCH:(n + 1) * FETCH]


    def pairs(j, _):
        index_l = jnp.concatenate([column(pair_a[...], 2 * j + h) for h in range(2)], axis=0)
        index_r = jnp.concatenate([column(pair_r[...], 2 * j + h) for h in range(2)], axis=0)
        left_rows = dot(one_hot(index_l, D), left[...])
        right_rows = dot(one_hot(index_r, CELLS * FETCH), rows_in[...])
        at = pl.ds(pl.multiple_of(j * 256, 256), 256)
        edge = (left_rows * right_rows * gate_o[at, :]).astype(BF16)
        mixed = silu(dot(edge, w_mix[...])).astype(BF16)
        own[:, at] = dot_nt(w_own[...], mixed)[0:BLOCK].astype(BF16)
        return 0

    def pairs_of(i, _):
        for h in range(4):
            pairs(4 * i + h, 0)

        return 0

    lax.fori_loop(0, PAIRS // 1024, pairs_of, 0)

    own_block.wait()
    block_copy(0, 0, me).wait()
    block_copy(0, 2, me).wait()
    parity = lax.rem(me, 2)

    def unpack(n, _):
        o = lax.rem(n, 3)
        x = lax.rem(lax.div(n, 3) + lax.div(me, Z), X)
        rank = lax.div(n, 3 * X)
        middle = lax.div(rank + 2, 3) * (1 + 2 * lax.rem(rank + parity, 2))
        shift = lax.rem(middle * lax.div(3 - rank + 2, 3) + 2 * lax.div(rank, 3), 4)
        even = x * Z + 2 * lax.rem(lax.div(lax.rem(me, Z), 2) + shift, 4)
        for h in range(2):
            away = lax.rem(lax.rem(even, Z) + h - lax.rem(me, Z) + Z + NEAR // 2, Z)

            @pl.when((even + h != me) & (away < NEAR))
            def _():
                block_copy(0, o, even + h).wait_recv()
        base = o * CELLS + even
        first = blk_in[base].astype(F32)
        second = blk_in[base + 1].astype(F32)
        top = jnp.where(low, first, pltpu.roll(second, SLOT, 1))
        bottom = jnp.where(low, pltpu.roll(first, SLOT, 1), second)
        partner[:, pl.ds(pl.multiple_of(base * SLOT, 128), 128)] = jnp.concatenate([top, bottom], axis=0)[0:BLOCK].astype(BF16)
        return 0

    def far(b, _):
        groups = [(o, dx) for o in range(3) for dx in range(X)]
        cells = [cell_at(far_step(b, dx), 1) for dx in range(X)]
        for g, (o, dx) in enumerate(groups):
            scalar_copy(b * X + dx, o).wait_recv()
            turn_a[g:g + 1, :] = scal_in[3 * (b * X + dx) + o, 0:1, :]
            turn_b[g:g + 1, :] = scal_in[3 * (b * X + dx) + o, 1:2, :]
        square[0:16, :] = envelope_of(turn_a[0:16, :])
        values, places, envelopes = turn_a[...].T, turn_b[...].T, square[...].T
        d = jnp.concatenate([values[0:SLOT, g:g + 1] for g in range(12)], axis=0)
        e = jnp.concatenate([envelopes[0:SLOT, g:g + 1] for g in range(12)], axis=0)
        m = jnp.concatenate([places[0:SLOT, g:g + 1] + float((g - o) * PART) for g, (o, dx) in enumerate(groups)], axis=0)
        gate = gate_of(d, e, w_rin[...], w_rout[...])
        entries = (list_n[1], list_s[PART:2 * PART, :], list_n[0])
        index = jnp.concatenate([column(entries[o], cells[dx]) for o, dx in groups], axis=0)
        rows = dot(one_hot(index, D), tables[1]).astype(BF16)
        right_rows = dot(one_hot(m, 12 * PART), rows)
        picked = jnp.concatenate(
            [dot(one_hot(values[SLOT:2 * SLOT, g:g + 1], D), far_f[2 - o, b * X + dx]).astype(BF16) for g, (o, dx) in enumerate(groups)], axis=0
        )
        left_rows = dot(picked, w_left[...]).astype(BF16).astype(F32)
        edge = (left_rows * right_rows * gate).astype(BF16)
        mixed = silu(dot(edge, w_mix[...])).astype(BF16)
        out = dot_nt(w_flip[...], mixed)
        for o in range(3):
            for h in range(0, X, 2):
                first, second = halves(out, o, h)
                blk_in[o * CELLS + cells[h]] = first
                blk_in[o * CELLS + cells[h + 1]] = second
        return 0

    lax.fori_loop(0, 3 * GROUPS // 8, unpack, 0)
    lax.fori_loop(0, FAR, far, 0)
    lax.fori_loop(3 * GROUPS // 8, GROUPS // 2, unpack, 0)

    sent = []
    for o in range(3):
        sent.append((rows_out.at[o, pl.ds(PART, (NEAR_CELLS - 1) * PART)], rows_in.at[pl.ds(0, (NEAR_CELLS - 1) * PART)], rows_ss.at[o], rows_rs.at[0, o]))
    for which in range(2):
        sent.append((far_f.at[1], far_f.at[2 * which], near_ss.at[which], near_rs.at[0, which]))
    sent.append((scal_out, scal_in, scal_ss.at[0], scal_rs.at[0, 0]))
    for source, target, send_sem, recv_sem in sent:
        pltpu.make_async_remote_copy(
            src_ref=source, dst_ref=target, send_sem=send_sem, recv_sem=recv_sem,
            device_id=(strip_at(1), me), device_id_type=MESH,
        ).wait_send()

    def finish_blocks(n, _):
        for o in range(3):
            block_copy(near_step(n), o, me).wait_send()
        return 0

    lax.fori_loop(1, NEAR_CELLS, finish_blocks, 0)

    for b in range(FAR):
        hop_copy(b).wait_send()
        for dx in range(1, X):
            side_copy(b, dx).wait_send()


def output_kernel(own_in, partner_in, own, partner, sem):
    copies = [pltpu.make_async_copy(own_in, own, sem.at[0]), pltpu.make_async_copy(partner_in, partner, sem.at[1])]
    for copy in copies:
        copy.start()
    for copy in copies:
        copy.wait()


def body(features, pair_atom, partner_row, transpose_slot, distance, send_rows, w_left, w_right, w_radial_in, w_radial_out, w_mix, w_out):
    vmem = pl.BlockSpec(memory_space=pltpu.VMEM)
    hbm = pl.BlockSpec(memory_space=pltpu.HBM)
    sem = pltpu.SemaphoreType.DMA
    outputs = (
        jax.ShapeDtypeStruct((BLOCK, PAIRS), BF16),
        jax.ShapeDtypeStruct((BLOCK, GROUPS * SLOT), BF16),
    )
    own, partner = pl.pallas_call(
        main_kernel,
        out_shape=outputs,
        in_specs=[hbm] * 12,
        out_specs=(vmem, vmem),
        scratch_shapes=[
            pltpu.VMEM((D, D), BF16),
            *[pltpu.VMEM((32, 128), jnp.int32)] * 3,
            pltpu.VMEM((32, 128), F32),
            pltpu.VMEM((CELLS, FETCH), jnp.int32),
            pltpu.VMEM((D, D), BF16),
            pltpu.VMEM((D, D), BF16),
            pltpu.VMEM((COUNT, D), BF16),
            pltpu.VMEM((D, D), BF16),
            pltpu.VMEM((D, D), BF16),
            pltpu.VMEM((BLOCK, D), BF16),
            pltpu.VMEM((D, D), BF16),
            pltpu.VMEM((2, D, D), BF16),
            pltpu.VMEM((2, CELLS, FETCH), jnp.int32),
            pltpu.VMEM((3, FAR_CELLS, D, D), BF16),
            pltpu.VMEM((3 * FAR_CELLS, 2, 128), F32),
            pltpu.VMEM((3 * FAR_CELLS, 2, 128), F32),
            pltpu.VMEM((FAR_CELLS, 2, 128), F32),
            pltpu.VMEM((FAR_CELLS, 2, 128), F32),
            pltpu.VMEM((3, D, D), BF16),
            pltpu.VMEM((D, D), BF16),
            pltpu.VMEM((3, CELLS * PART, D), BF16),
            pltpu.VMEM((CELLS * FETCH, D), BF16),
            pltpu.VMEM((GROUPS * SLOT, D), F32),
            pltpu.VMEM((PAIRS, D), F32),
            pltpu.VMEM((CELLS, 3, HALF, 128), BF16),
            pltpu.VMEM((GROUPS, HALF, 128), BF16),
            *[pltpu.VMEM((SLOT, 128), F32)] * 4,
            *[pltpu.VMEM((128, 128), F32)] * 5,
            pltpu.VMEM((FETCH, 128), F32),
            pltpu.VMEM((2, PART, 128), F32),
            *[pltpu.VMEM((128, 128), F32)] * 3,
            pltpu.VMEM((2 * HALF, D), BF16),
            pltpu.VMEM((2 * HALF, D), BF16),
            sem((12,)), *[sem((2,))] * 4, *[sem((FAR,))] * 2, *[sem((FAR, X - 1))] * 2,
            sem((2,)), sem((FAR_CELLS, 2)), sem((1,)), sem((FAR_CELLS, 3)), sem((FAR_CELLS,)), sem((FAR_CELLS,)), sem((3,)), sem((CELLS, 3)), sem((CELLS, 3)), sem((CELLS, 3)), sem((4,)),
        ],
        compiler_params=pltpu.CompilerParams(collective_id=0, has_side_effects=True, vmem_limit_bytes=48 << 20),
    )(*[pltpu.with_memory_space_constraint(a, pltpu.HBM) for a in (
        features,
        pair_atom.reshape(32, 128),
        partner_row.reshape(32, 128),
        transpose_slot.reshape(32, 128),
        distance.reshape(32, 128),
        send_rows, w_left, w_right, w_radial_in, w_radial_out, w_mix, w_out.T,
    )])
    return pl.pallas_call(
        output_kernel,
        out_shape=outputs,
        in_specs=[vmem, vmem],
        out_specs=(hbm, hbm),
        scratch_shapes=[sem((2,))],
        compiler_params=pltpu.CompilerParams(vmem_limit_bytes=16 << 20),
    )(own, partner)


def solution(mesh):
    both = P(("strip", "cell"))
    rows = P(("strip", "cell"), None)
    in_specs = (rows, both, both, both, both, rows, P(), P(), P(), P(), P(), P())
    out_specs = (P(None, ("strip", "cell")), P(None, ("strip", "cell")))
    return jax.shard_map(body, mesh=mesh, in_specs=in_specs, out_specs=out_specs, check_vma=False)
```

```python
import functools

import jax
import jax.numpy as jnp
import numpy as np
from jax import lax
from jax.experimental import pallas as pl
from jax.experimental.pallas import tpu as pltpu
from jax.sharding import PartitionSpec as P

MESH = pl.DeviceIdType.MESH
F32 = jnp.float32
BF16 = jnp.bfloat16
D = 256
BLOCK = 169
ORB = 13
HALF = 88
FETCH = 48
SLOT = 64
CELLS = 32
STRIPS = 8
Z = 8
X = 4
PAIRS = 4096
GROUPS = 96
CUTOFF = 8.0
COUNT = 128
PART = 16
EARLY = 4
WIDE = 4
SPAN = 3 * WIDE * SLOT
NEAR = 7
FAR = Z - NEAR
NEAR_CELLS = NEAR * X
FAR_CELLS = FAR * X


def silu(x):
    half = 0.5 * x
    return half + half * jnp.tanh(half)


def offset_of(k):
    late = lax.div(k, NEAR_CELLS)
    n = k - late * NEAR_CELLS
    j = (1 - late) * lax.rem(k, NEAR) + late * (NEAR + lax.div(n, X))
    hop = lax.div(j + 1, 2) * (2 * lax.rem(j, 2) - 1)
    return (1 - late) * lax.div(k, NEAR) + late * lax.rem(n, X), hop


def cell_at(k, sign):
    c = lax.axis_index("cell")
    dx, dz = offset_of(k)
    x = lax.rem(lax.div(c, Z) + sign * dx + X, X)
    z = lax.rem(lax.rem(c, Z) + sign * dz + Z, Z)
    return x * Z + z


def strip_at(step):
    return lax.rem(lax.axis_index("strip") + step + STRIPS, STRIPS)


def column(values, lane):
    lanes = lax.broadcasted_iota(jnp.int32, values.shape, 1)
    return jnp.sum(jnp.where(lanes == lane, values, 0.0), axis=1, keepdims=True)


def one_hot(index, width):
    lanes = lax.broadcasted_iota(jnp.int32, (index.shape[0], width), 1).astype(F32)
    return jnp.where(lanes == index, 1.0, 0.0).astype(BF16)


def dot(a, b):
    return jnp.dot(a, b, preferred_element_type=F32)


def dot_nt(a, b):
    return lax.dot_general(a, b, (((1,), (1,)), ((), ())), preferred_element_type=F32)


def row_index(slot, row):
    offset = lax.shift_right_logical(slot, 11)
    base = FETCH * (lax.shift_right_logical(slot, 6) & (CELLS - 1))
    part = lax.shift_right_logical((row - base - offset) * 171, 9)
    return base + offset * PART + part


def envelope_of(distance):
    return 0.5 * (jnp.cos(jnp.pi * distance / CUTOFF) + 1.0)


def gate_of(distance, envelope, w_in, w_out):
    centers = lax.broadcasted_iota(jnp.int32, (1, COUNT), 1).astype(F32) * (CUTOFF / (COUNT - 1))
    scaled = (distance - centers) * (COUNT / (2.0 * CUTOFF))
    basis = (jnp.exp(-scaled * scaled) * envelope).astype(BF16)
    radial = silu(dot(basis, w_in)).astype(BF16)
    return dot(radial, w_out)


def main_kernel(
    feat_h, atom_h, prow_h, slot_h, dist_h, lists_h, w_left_h, w_right_h, w_rin_h, w_rout_h, w_mix_h, w_out_h,
    own, partner,
    feat, atom, prow, slot, dist, lists, w_left, w_right, w_rin, w_rout, w_mix, w_raw, w_out,
    feat_in, list_in, far_f, scal_out, scal_in, entry_out, entry_in, tables, left, rows_out, rows_in, gate_s, gate_o, blk_out, blk_in,
    slot_d, slot_e, slot_a, slot_m, pair_d, pair_e, pair_a, pair_r, list_t, list_s, list_n, turn_a, turn_b,
    square, w_own, w_flip,
    in_sem, feat_ss, feat_rs, list_ss, list_rs, hop_ss, hop_rs, side_ss, side_rs, near_ss, near_rs, scal_ss, scal_rs, entry_ss, entry_rs, rows_ss, rows_rs, blk_ss, blk_rs, local_sem,
):
    me = lax.axis_index("cell")
    sources = (feat_h, w_left_h, w_right_h, lists_h, slot_h, dist_h, atom_h, prow_h, w_out_h, w_rin_h, w_rout_h, w_mix_h)
    targets = (feat, w_left, w_right, lists, slot, dist, atom, prow, w_raw, w_rin, w_rout, w_mix)
    loads = [pltpu.make_async_copy(a, b, in_sem.at[n]) for n, (a, b) in enumerate(zip(sources, targets))]
    for load in loads:
        load.start()

    barrier = pltpu.get_barrier_semaphore()

    def greet(n, _):
        k = CELLS - 1 - n
        c = cell_at(k, 1)
        for step in (-1, 0, 1):
            if step:
                pl.semaphore_signal(barrier, inc=1, device_id=(strip_at(step), c), device_id_type=MESH)
            else:
                @pl.when(k > 0)
                def _():
                    pl.semaphore_signal(barrier, inc=1, device_id=(strip_at(0), c), device_id_type=MESH)
        return 0

    lax.fori_loop(0, CELLS, greet, 0)
    for load in loads:
        load.wait()

    left[...] = dot(feat[...], w_left[...]).astype(BF16)
    tables[1] = dot(feat[...], w_right[...]).astype(BF16)

    entry_out[...] = jnp.zeros_like(entry_out)
    for n in range(FAR_CELLS):
        entry_out[n, 0:1, 0:FETCH] = lists[pl.ds(cell_at(NEAR_CELLS + n, -1), 1), :].astype(F32)
    square[...] = jnp.zeros_like(square)
    square[0:32, 0:FETCH] = lists[...].astype(F32)
    list_t[...] = square[...].T
    for o in range(3):
        list_s[pl.ds(o * PART, PART), :] = list_t[pl.ds(o, PART, stride=3), :] - float(o * D)

    def pick(o, i):
        index = jnp.concatenate(
            [column(list_s[pl.ds(pl.multiple_of(o * PART, PART), PART), :], cell_at(8 * i + h, 1)) for h in range(8)], axis=0
        )
        picked = dot(one_hot(index, D), tables[o]).astype(BF16)
        rows_out[o, pl.ds(pl.multiple_of(i * 8 * PART, 128), 8 * PART), :] = picked

    def pick_own(i, _):
        pick(1, i)
        return 0

    lax.fori_loop(0, CELLS // 8, pick_own, 0)

    def place(j, total):
        left_parts, right_parts = [], []
        for h in range(2):
            at = pl.ds(2 * j + h, 1)
            t = slot[at, :]
            d = dist[at, :]
            d_hi = d.astype(BF16).astype(F32)
            d_mid = (d - d_hi).astype(BF16).astype(F32)
            d_lo = d - d_hi - d_mid
            index = row_index(t, prow[at, :]) - FETCH * (lax.shift_right_logical(t, 6) & (CELLS - 1))
            hit = lax.broadcasted_iota(jnp.int32, (SLOT, 128), 0) == (t & (SLOT - 1))
            parts = (d_hi, d_mid, d_lo, (atom[at, :] + 1).astype(F32), index.astype(F32))
            left_parts.append(jnp.concatenate([jnp.where(hit, v, 0.0) for v in parts], axis=0))
            group = lax.broadcasted_iota(jnp.int32, (128, 128), 0) == lax.shift_right_logical(t, 6)
            right_parts.append(jnp.where(group, 1.0, 0.0))
        return total + dot_nt(
            jnp.concatenate(left_parts, axis=1).astype(BF16), jnp.concatenate(right_parts, axis=1).astype(BF16)
        )

    total = lax.fori_loop(0, PAIRS // 256, place, jnp.zeros((5 * SLOT, 128), F32))
    d = total[0:SLOT] + total[SLOT:2 * SLOT] + total[2 * SLOT:3 * SLOT]
    slot_d[...] = d
    slot_e[...] = envelope_of(d)
    slot_a[...] = total[3 * SLOT:4 * SLOT] - 1.0
    slot_m[...] = total[4 * SLOT:5 * SLOT]
    turn_a[...] = jnp.concatenate([d, total[3 * SLOT:4 * SLOT] - 1.0], axis=0).T
    turn_b[...] = jnp.concatenate([total[4 * SLOT:5 * SLOT], jnp.zeros((SLOT, 128), F32)], axis=0).T

    def pack_scalars(n, _):
        c = cell_at(NEAR_CELLS + n, -1)
        for o in range(3):
            scal_out[3 * n + o, 0:1, :] = turn_a[pl.ds(o * CELLS + c, 1), :]
            scal_out[3 * n + o, 1:2, :] = turn_b[pl.ds(o * CELLS + c, 1), :]
        return 0

    lax.fori_loop(0, FAR_CELLS, pack_scalars, 0)

    pl.semaphore_wait(barrier, 3 * CELLS - 1)

    def feature_copy(which):
        return pltpu.make_async_remote_copy(
            src_ref=feat, dst_ref=feat_in.at[which], send_sem=feat_ss.at[which], recv_sem=feat_rs.at[which],
            device_id=(strip_at(1 - 2 * which), me), device_id_type=MESH,
        )

    def row_copy(k, o, sender):
        return pltpu.make_async_remote_copy(
            src_ref=rows_out.at[o, pl.ds(pl.multiple_of(k * PART, PART), PART)],
            dst_ref=rows_in.at[pl.ds(pl.multiple_of(me * FETCH + o * PART, PART), PART)],
            send_sem=rows_ss.at[o], recv_sem=rows_rs.at[sender, o],
            device_id=(strip_at(0), cell_at(k, 1)), device_id_type=MESH,
        )

    def own_rows(o):
        return pltpu.make_async_copy(
            rows_out.at[o, pl.ds(0, PART)], rows_in.at[pl.ds(pl.multiple_of(me * FETCH + o * PART, PART), PART)], local_sem.at[o]
        )

    def send_rows_of(o, i):
        for h in range(8):
            if h >= NEAR_CELLS % 8:
                @pl.when(i < CELLS // 8 - 1)
                def _():
                    row_copy(8 * i + h, o, me).start()
            elif h:
                row_copy(8 * i + h, o, me).start()
            else:
                @pl.when(i == 0)
                def _():
                    own_rows(o).start()

                @pl.when(i > 0)
                def _():
                    row_copy(8 * i, o, me).start()

    def list_copy(which):
        return pltpu.make_async_remote_copy(
            src_ref=lists, dst_ref=list_in.at[which], send_sem=list_ss.at[which], recv_sem=list_rs.at[which],
            device_id=(strip_at(1 - 2 * which), me), device_id_type=MESH,
        )

    def far_step(b, dx):
        return NEAR_CELLS + b * X + dx

    def hop_copy(b):
        return pltpu.make_async_remote_copy(
            src_ref=feat, dst_ref=far_f.at[1, b * X], send_sem=hop_ss.at[b], recv_sem=hop_rs.at[b],
            device_id=(strip_at(0), cell_at(far_step(b, 0), -1)), device_id_type=MESH,
        )

    def side_copy(b, dx):
        return pltpu.make_async_remote_copy(
            src_ref=far_f.at[1, b * X], dst_ref=far_f.at[1, b * X + dx],
            send_sem=side_ss.at[b, dx - 1], recv_sem=side_rs.at[b, dx - 1],
            device_id=(strip_at(0), cell_at(dx * NEAR, -1)), device_id_type=MESH,
        )

    def near_copy(n, which):
        return pltpu.make_async_remote_copy(
            src_ref=far_f.at[1, n], dst_ref=far_f.at[2 * which, n],
            send_sem=near_ss.at[which], recv_sem=near_rs.at[n, which],
            device_id=(strip_at(1 - 2 * which), me), device_id_type=MESH,
        )

    def scalar_copy(n, o):
        k = far_step(lax.div(n, X), lax.rem(n, X))
        return pltpu.make_async_remote_copy(
            src_ref=scal_out.at[3 * n + o], dst_ref=scal_in.at[3 * n + o],
            send_sem=scal_ss.at[0], recv_sem=scal_rs.at[n, o],
            device_id=(strip_at(o - 1), cell_at(k, -1)), device_id_type=MESH,
        )

    def entry_copy(n):
        return pltpu.make_async_remote_copy(
            src_ref=entry_out.at[n], dst_ref=entry_in.at[n], send_sem=entry_ss.at[n], recv_sem=entry_rs.at[n],
            device_id=(strip_at(0), cell_at(NEAR_CELLS + n, -1)), device_id_type=MESH,
        )

    for which in range(2):
        feature_copy(which).start()
        list_copy(which).start()
    for n in range(FAR_CELLS):
        entry_copy(n).start()
    for b in range(FAR):
        hop_copy(b).start()

    def send_own_part(i, _):
        send_rows_of(1, i)
        return 0

    lax.fori_loop(0, CELLS // 8, send_own_part, 0)

    def near_step(n):
        return n

    def slot_columns(source, i):
        cells = [cell_at(near_step(WIDE * i + h), -1) for h in range(WIDE)]
        return jnp.concatenate([column(source[...], o * CELLS + c) for o in range(3) for c in cells], axis=0)

    def slot_gates(i, _):
        gate_s[pl.ds(pl.multiple_of(i * SPAN, 128), SPAN), :] = gate_of(
            slot_columns(slot_d, i), slot_columns(slot_e, i), w_rin[...], w_rout[...]
        )
        return 0

    early = EARLY
    lax.fori_loop(0, early, slot_gates, 0)

    for which in range(2):
        feature_copy(which).wait()
        tables[2 * which] = dot(feat_in[which], w_right[...]).astype(BF16)

    def rest(i):
        return 2 * lax.rem(i, 2), lax.div(i, 2)

    def pick_rest(i, _):
        pick(*rest(i))

        @pl.when(i > 0)
        def _():
            send_rows_of(*rest(i - 1))
        return 0

    lax.fori_loop(0, CELLS // 4, pick_rest, 0)
    lax.fori_loop(early, early + 1, slot_gates, 0)
    send_rows_of(2, CELLS // 8 - 1)
    def send_scalars(n, _):
        for o in range(3):
            scalar_copy(n, o).start()
        return 0

    lax.fori_loop(0, FAR_CELLS, send_scalars, 0)
    for which in range(2):
        list_copy(which).wait()
        square[0:32, 0:FETCH] = list_in[which].astype(F32)
        list_t[...] = square[...].T
        list_n[which] = list_t[pl.ds(2 - 2 * which, PART, stride=3), :] - float((2 - 2 * which) * D)
    lax.fori_loop(early + 1, NEAR_CELLS // WIDE, slot_gates, 0)

    def block_copy(k, o, sender):
        return pltpu.make_async_remote_copy(
            src_ref=blk_out.at[k, o], dst_ref=blk_in.at[o * CELLS + me],
            send_sem=blk_ss.at[k, o], recv_sem=blk_rs.at[sender, o],
            device_id=(strip_at(o - 1), cell_at(k, -1)), device_id_type=MESH,
        )

    own_block = pltpu.make_async_copy(blk_out.at[0, 1], blk_in.at[CELLS + me], local_sem.at[3])

    def send_blocks_of(i):
        for h in range(WIDE):
            for o in range(3):
                if h or o != 1:
                    block_copy(near_step(WIDE * i + h), o, me).start()
                else:
                    @pl.when(i == 0)
                    def _():
                        own_block.start()

                    @pl.when(i > 0)
                    def _():
                        block_copy(near_step(WIDE * i), 1, me).start()

    low = lax.broadcasted_iota(jnp.int32, (HALF, 128), 1) < SLOT

    def halves(out, o, h):
        start = (o * WIDE + h) * SLOT
        top = out[0:HALF, start:start + 128]
        bottom = out[HALF:2 * HALF, start:start + 128]
        return (
            jnp.where(low, top, pltpu.roll(bottom, SLOT, 1)).astype(BF16),
            jnp.where(low, pltpu.roll(top, SLOT, 1), bottom).astype(BF16),
        )

    def slots(i, _):
        cells = [cell_at(near_step(WIDE * i + h), -1) for h in range(WIDE)]
        for o in range(3):
            @pl.when(i == 0)
            def _():
                own_rows(o).wait()

            @pl.when(i > 0)
            def _():
                row_copy(near_step(WIDE * i), o, cells[0]).wait_recv()
            for h in range(1, WIDE):
                row_copy(near_step(WIDE * i + h), o, cells[h]).wait_recv()
        rows = jnp.concatenate([rows_in[pl.ds(pl.multiple_of(c * FETCH, PART), FETCH), :] for c in cells], axis=0)
        second = lax.rem(lax.div(lax.broadcasted_iota(jnp.int32, (SPAN, 1), 0), SLOT), WIDE) * FETCH
        left_rows = dot(one_hot(slot_columns(slot_a, i), D), left[...])
        right_rows = dot(one_hot(slot_columns(slot_m, i) + second.astype(F32), WIDE * FETCH), rows)
        gate = gate_s[pl.ds(pl.multiple_of(i * SPAN, 128), SPAN), :]
        edge = (left_rows * right_rows * gate).astype(BF16)
        mixed = silu(dot(edge, w_mix[...])).astype(BF16)
        out = dot_nt(w_flip[...], mixed)
        for o in range(3):
            for h in range(0, WIDE, 2):
                first, second = halves(out, o, h)
                blk_out[near_step(WIDE * i + h), o] = first
                blk_out[near_step(WIDE * i + h + 1), o] = second

        @pl.when(i > 0)
        def _():
            send_blocks_of(i - 1)
        return 0

    entry = lax.broadcasted_iota(jnp.int32, (2 * HALF, D), 0)
    lane = lax.broadcasted_iota(jnp.int32, (2 * HALF, D), 1)
    quotient = lax.shift_right_logical(entry * 79, 10)
    flipped = (entry - quotient * ORB) * ORB + quotient
    w_out[...] = jnp.zeros_like(w_out)
    w_out[0:BLOCK, :] = w_raw[...]
    w_own[...] = w_out[0:2 * HALF, :]
    w_flip[...] = dot(jnp.where((entry < BLOCK) & (lane == flipped), 1.0, 0.0).astype(BF16), w_out[...]).astype(BF16)

    def to_sides(b):
        hop_copy(b).wait_recv()
        for dx in range(1, X):
            side_copy(b, dx).start()
        for which in range(2):
            near_copy(b * X, which).start()

    def to_strips(b):
        for dx in range(1, X):
            side_copy(b, dx).wait_recv()
            for which in range(2):
                near_copy(b * X + dx, which).start()


    for b in range(FAR):
        to_sides(b)
    lax.fori_loop(0, NEAR_CELLS // WIDE, slots, 0)

    index = row_index(slot[...], prow[...])
    for source, target in ((dist[...], pair_d), (envelope_of(dist[...]), pair_e), (atom[...].astype(F32), pair_a), (index.astype(F32), pair_r)):
        square[0:32, :] = source
        target[...] = square[...].T


    send_blocks_of(NEAR_CELLS // WIDE - 1)
    for b in range(FAR):
        to_strips(b)

    def pair_gates(j, _):
        d = jnp.concatenate([column(pair_d[...], 2 * j + h) for h in range(2)], axis=0)
        e = jnp.concatenate([column(pair_e[...], 2 * j + h) for h in range(2)], axis=0)
        gate_o[pl.ds(pl.multiple_of(j * 256, 256), 256), :] = gate_of(d, e, w_rin[...], w_rout[...])
        return 0

    lax.fori_loop(0, PAIRS // 256, pair_gates, 0, unroll=4)

    for n in range(FAR_CELLS):
        entry_copy(n).wait()
        square[n:n + 1, :] = entry_in[n, 0:1, :]
        for which in range(2):
            near_copy(n, which).wait_recv()
    list_t[...] = square[...].T
    spans = [list_t[pl.ds(o, PART, stride=3), :] - float(o * D) for o in range(3)]
    chosen = jnp.concatenate(
        [dot(one_hot(spans[o][:, n:n + 1], D), far_f[o, n]).astype(BF16) for n in range(FAR_CELLS) for o in range(3)], axis=0
    )
    chosen = dot(chosen, w_right[...]).astype(BF16)
    for n in range(FAR_CELLS):
        rows_in[pl.ds(pl.multiple_of(cell_at(NEAR_CELLS + n, 1) * FETCH, PART), FETCH), :] = chosen[n * FETCH:(n + 1) * FETCH]


    def pairs(j, _):
        index_l = jnp.concatenate([column(pair_a[...], 2 * j + h) for h in range(2)], axis=0)
        index_r = jnp.concatenate([column(pair_r[...], 2 * j + h) for h in range(2)], axis=0)
        left_rows = dot(one_hot(index_l, D), left[...])
        right_rows = dot(one_hot(index_r, CELLS * FETCH), rows_in[...])
        at = pl.ds(pl.multiple_of(j * 256, 256), 256)
        edge = (left_rows * right_rows * gate_o[at, :]).astype(BF16)
        mixed = silu(dot(edge, w_mix[...])).astype(BF16)
        own[:, at] = dot_nt(w_own[...], mixed)[0:BLOCK].astype(BF16)
        return 0

    def pairs_of(i, _):
        for h in range(4):
            pairs(4 * i + h, 0)

        return 0

    lax.fori_loop(0, PAIRS // 1024, pairs_of, 0)

    own_block.wait()
    block_copy(0, 0, me).wait()
    block_copy(0, 2, me).wait()
    parity = lax.rem(me, 2)

    def unpack(n, _):
        o = lax.rem(n, 3)
        x = lax.rem(lax.div(n, 12) + lax.div(me, Z), X)
        rank = lax.rem(lax.div(n, 3), X)
        middle = lax.div(rank + 2, 3) * (1 + 2 * lax.rem(rank + parity, 2))
        shift = lax.rem(middle * lax.div(3 - rank + 2, 3) + 2 * lax.div(rank, 3), 4)
        even = x * Z + 2 * lax.rem(lax.div(lax.rem(me, Z), 2) + shift, 4)
        for h in range(2):
            away = lax.rem(lax.rem(even, Z) + h - lax.rem(me, Z) + Z + NEAR // 2, Z)

            @pl.when((even + h != me) & (away < NEAR))
            def _():
                block_copy(0, o, even + h).wait_recv()
        base = o * CELLS + even
        first = blk_in[base].astype(F32)
        second = blk_in[base + 1].astype(F32)
        top = jnp.where(low, first, pltpu.roll(second, SLOT, 1))
        bottom = jnp.where(low, pltpu.roll(first, SLOT, 1), second)
        partner[:, pl.ds(pl.multiple_of(base * SLOT, 128), 128)] = jnp.concatenate([top, bottom], axis=0)[0:BLOCK].astype(BF16)
        return 0

    def far(b, _):
        groups = [(o, dx) for o in range(3) for dx in range(X)]
        cells = [cell_at(far_step(b, dx), 1) for dx in range(X)]
        for g, (o, dx) in enumerate(groups):
            scalar_copy(b * X + dx, o).wait_recv()
            turn_a[g:g + 1, :] = scal_in[3 * (b * X + dx) + o, 0:1, :]
            turn_b[g:g + 1, :] = scal_in[3 * (b * X + dx) + o, 1:2, :]
        square[0:16, :] = envelope_of(turn_a[0:16, :])
        values, places, envelopes = turn_a[...].T, turn_b[...].T, square[...].T
        d = jnp.concatenate([values[0:SLOT, g:g + 1] for g in range(12)], axis=0)
        e = jnp.concatenate([envelopes[0:SLOT, g:g + 1] for g in range(12)], axis=0)
        m = jnp.concatenate([places[0:SLOT, g:g + 1] + float((g - o) * PART) for g, (o, dx) in enumerate(groups)], axis=0)
        gate = gate_of(d, e, w_rin[...], w_rout[...])
        entries = (list_n[1], list_s[PART:2 * PART, :], list_n[0])
        index = jnp.concatenate([column(entries[o], cells[dx]) for o, dx in groups], axis=0)
        rows = dot(one_hot(index, D), tables[1]).astype(BF16)
        right_rows = dot(one_hot(m, 12 * PART), rows)
        picked = jnp.concatenate(
            [dot(one_hot(values[SLOT:2 * SLOT, g:g + 1], D), far_f[2 - o, b * X + dx]).astype(BF16) for g, (o, dx) in enumerate(groups)], axis=0
        )
        left_rows = dot(picked, w_left[...]).astype(BF16).astype(F32)
        edge = (left_rows * right_rows * gate).astype(BF16)
        mixed = silu(dot(edge, w_mix[...])).astype(BF16)
        out = dot_nt(w_flip[...], mixed)
        for o in range(3):
            for h in range(0, X, 2):
                first, second = halves(out, o, h)
                blk_in[o * CELLS + cells[h]] = first
                blk_in[o * CELLS + cells[h + 1]] = second
        return 0

    lax.fori_loop(0, FAR, far, 0)
    lax.fori_loop(0, GROUPS // 2, unpack, 0)

    sent = []
    for o in range(3):
        sent.append((rows_out.at[o, pl.ds(PART, (NEAR_CELLS - 1) * PART)], rows_in.at[pl.ds(0, (NEAR_CELLS - 1) * PART)], rows_ss.at[o], rows_rs.at[0, o]))
    for which in range(2):
        sent.append((far_f.at[1], far_f.at[2 * which], near_ss.at[which], near_rs.at[0, which]))
    sent.append((scal_out, scal_in, scal_ss.at[0], scal_rs.at[0, 0]))
    for source, target, send_sem, recv_sem in sent:
        pltpu.make_async_remote_copy(
            src_ref=source, dst_ref=target, send_sem=send_sem, recv_sem=recv_sem,
            device_id=(strip_at(1), me), device_id_type=MESH,
        ).wait_send()

    def finish_blocks(n, _):
        for o in range(3):
            block_copy(near_step(n), o, me).wait_send()
        return 0

    lax.fori_loop(1, NEAR_CELLS, finish_blocks, 0)

    for b in range(FAR):
        hop_copy(b).wait_send()
        for dx in range(1, X):
            side_copy(b, dx).wait_send()


def output_kernel(own_in, partner_in, own, partner, sem):
    copies = [pltpu.make_async_copy(own_in, own, sem.at[0]), pltpu.make_async_copy(partner_in, partner, sem.at[1])]
    for copy in copies:
        copy.start()
    for copy in copies:
        copy.wait()


def body(features, pair_atom, partner_row, transpose_slot, distance, send_rows, w_left, w_right, w_radial_in, w_radial_out, w_mix, w_out):
    vmem = pl.BlockSpec(memory_space=pltpu.VMEM)
    hbm = pl.BlockSpec(memory_space=pltpu.HBM)
    sem = pltpu.SemaphoreType.DMA
    outputs = (
        jax.ShapeDtypeStruct((BLOCK, PAIRS), BF16),
        jax.ShapeDtypeStruct((BLOCK, GROUPS * SLOT), BF16),
    )
    own, partner = pl.pallas_call(
        main_kernel,
        out_shape=outputs,
        in_specs=[hbm] * 12,
        out_specs=(vmem, vmem),
        scratch_shapes=[
            pltpu.VMEM((D, D), BF16),
            *[pltpu.VMEM((32, 128), jnp.int32)] * 3,
            pltpu.VMEM((32, 128), F32),
            pltpu.VMEM((CELLS, FETCH), jnp.int32),
            pltpu.VMEM((D, D), BF16),
            pltpu.VMEM((D, D), BF16),
            pltpu.VMEM((COUNT, D), BF16),
            pltpu.VMEM((D, D), BF16),
            pltpu.VMEM((D, D), BF16),
            pltpu.VMEM((BLOCK, D), BF16),
            pltpu.VMEM((D, D), BF16),
            pltpu.VMEM((2, D, D), BF16),
            pltpu.VMEM((2, CELLS, FETCH), jnp.int32),
            pltpu.VMEM((3, FAR_CELLS, D, D), BF16),
            pltpu.VMEM((3 * FAR_CELLS, 2, 128), F32),
            pltpu.VMEM((3 * FAR_CELLS, 2, 128), F32),
            pltpu.VMEM((FAR_CELLS, 2, 128), F32),
            pltpu.VMEM((FAR_CELLS, 2, 128), F32),
            pltpu.VMEM((3, D, D), BF16),
            pltpu.VMEM((D, D), BF16),
            pltpu.VMEM((3, CELLS * PART, D), BF16),
            pltpu.VMEM((CELLS * FETCH, D), BF16),
            pltpu.VMEM((GROUPS * SLOT, D), F32),
            pltpu.VMEM((PAIRS, D), F32),
            pltpu.VMEM((CELLS, 3, HALF, 128), BF16),
            pltpu.VMEM((GROUPS, HALF, 128), BF16),
            *[pltpu.VMEM((SLOT, 128), F32)] * 4,
            *[pltpu.VMEM((128, 128), F32)] * 5,
            pltpu.VMEM((FETCH, 128), F32),
            pltpu.VMEM((2, PART, 128), F32),
            *[pltpu.VMEM((128, 128), F32)] * 3,
            pltpu.VMEM((2 * HALF, D), BF16),
            pltpu.VMEM((2 * HALF, D), BF16),
            sem((12,)), *[sem((2,))] * 4, *[sem((FAR,))] * 2, *[sem((FAR, X - 1))] * 2,
            sem((2,)), sem((FAR_CELLS, 2)), sem((1,)), sem((FAR_CELLS, 3)), sem((FAR_CELLS,)), sem((FAR_CELLS,)), sem((3,)), sem((CELLS, 3)), sem((CELLS, 3)), sem((CELLS, 3)), sem((4,)),
        ],
        compiler_params=pltpu.CompilerParams(collective_id=0, has_side_effects=True, vmem_limit_bytes=48 << 20),
    )(*[pltpu.with_memory_space_constraint(a, pltpu.HBM) for a in (
        features,
        pair_atom.reshape(32, 128),
        partner_row.reshape(32, 128),
        transpose_slot.reshape(32, 128),
        distance.reshape(32, 128),
        send_rows, w_left, w_right, w_radial_in, w_radial_out, w_mix, w_out.T,
    )])
    return pl.pallas_call(
        output_kernel,
        out_shape=outputs,
        in_specs=[vmem, vmem],
        out_specs=(hbm, hbm),
        scratch_shapes=[sem((2,))],
        compiler_params=pltpu.CompilerParams(vmem_limit_bytes=16 << 20),
    )(own, partner)


def solution(mesh):
    both = P(("strip", "cell"))
    rows = P(("strip", "cell"), None)
    in_specs = (rows, both, both, both, both, rows, P(), P(), P(), P(), P(), P())
    out_specs = (P(None, ("strip", "cell")), P(None, ("strip", "cell")))
    return jax.shard_map(body, mesh=mesh, in_specs=in_specs, out_specs=out_specs, check_vma=False)
```

```python
import functools

import jax
import jax.numpy as jnp
import numpy as np
from jax import lax
from jax.experimental import pallas as pl
from jax.experimental.pallas import tpu as pltpu
from jax.sharding import PartitionSpec as P

MESH = pl.DeviceIdType.MESH
F32 = jnp.float32
BF16 = jnp.bfloat16
D = 256
BLOCK = 169
ORB = 13
HALF = 88
FETCH = 48
SLOT = 64
CELLS = 32
STRIPS = 8
Z = 8
X = 4
PAIRS = 4096
GROUPS = 96
CUTOFF = 8.0
COUNT = 128
PART = 16
EARLY = 4
WIDE = 4
SPAN = 3 * WIDE * SLOT
NEAR = 7
FAR = Z - NEAR
NEAR_CELLS = NEAR * X
FAR_CELLS = FAR * X


def silu(x):
    half = 0.5 * x
    return half + half * jnp.tanh(half)


def offset_of(k):
    late = lax.div(k, NEAR_CELLS)
    n = k - late * NEAR_CELLS
    j = (1 - late) * lax.rem(k, NEAR) + late * (NEAR + lax.div(n, X))
    hop = lax.div(j + 1, 2) * (2 * lax.rem(j, 2) - 1)
    return (1 - late) * lax.div(k, NEAR) + late * lax.rem(n, X), hop


def cell_at(k, sign):
    c = lax.axis_index("cell")
    dx, dz = offset_of(k)
    x = lax.rem(lax.div(c, Z) + sign * dx + X, X)
    z = lax.rem(lax.rem(c, Z) + sign * dz + Z, Z)
    return x * Z + z


def strip_at(step):
    return lax.rem(lax.axis_index("strip") + step + STRIPS, STRIPS)


def column(values, lane):
    lanes = lax.broadcasted_iota(jnp.int32, values.shape, 1)
    return jnp.sum(jnp.where(lanes == lane, values, 0.0), axis=1, keepdims=True)


def one_hot(index, width):
    lanes = lax.broadcasted_iota(jnp.int32, (index.shape[0], width), 1).astype(F32)
    return jnp.where(lanes == index, 1.0, 0.0).astype(BF16)


def dot(a, b):
    return jnp.dot(a, b, preferred_element_type=F32)


def dot_nt(a, b):
    return lax.dot_general(a, b, (((1,), (1,)), ((), ())), preferred_element_type=F32)


def row_index(slot, row):
    offset = lax.shift_right_logical(slot, 11)
    base = FETCH * (lax.shift_right_logical(slot, 6) & (CELLS - 1))
    part = lax.shift_right_logical((row - base - offset) * 171, 9)
    return base + offset * PART + part


def envelope_of(distance):
    return 0.5 * (jnp.cos(jnp.pi * distance / CUTOFF) + 1.0)


def gate_of(distance, envelope, w_in, w_out):
    centers = lax.broadcasted_iota(jnp.int32, (1, COUNT), 1).astype(F32) * (CUTOFF / (COUNT - 1))
    scaled = (distance - centers) * (COUNT / (2.0 * CUTOFF))
    basis = (jnp.exp(-scaled * scaled) * envelope).astype(BF16)
    radial = silu(dot(basis, w_in)).astype(BF16)
    return dot(radial, w_out)


def main_kernel(
    feat_h, atom_h, prow_h, slot_h, dist_h, lists_h, w_left_h, w_right_h, w_rin_h, w_rout_h, w_mix_h, w_out_h,
    own, partner,
    feat, atom, prow, slot, dist, lists, w_left, w_right, w_rin, w_rout, w_mix, w_raw, w_out,
    feat_in, list_in, far_f, scal_out, scal_in, entry_out, entry_in, tables, left, rows_out, rows_in, gate_s, gate_o, blk_out, blk_in,
    slot_d, slot_e, slot_a, slot_m, pair_d, pair_e, pair_a, pair_r, list_t, list_s, list_n, turn_a, turn_b,
    square, w_own, w_flip,
    in_sem, feat_ss, feat_rs, list_ss, list_rs, hop_ss, hop_rs, side_ss, side_rs, near_ss, near_rs, scal_ss, scal_rs, entry_ss, entry_rs, rows_ss, rows_rs, blk_ss, blk_rs, local_sem,
):
    me = lax.axis_index("cell")
    sources = (feat_h, w_left_h, w_right_h, lists_h, slot_h, dist_h, atom_h, prow_h, w_out_h, w_rin_h, w_rout_h, w_mix_h)
    targets = (feat, w_left, w_right, lists, slot, dist, atom, prow, w_raw, w_rin, w_rout, w_mix)
    loads = [pltpu.make_async_copy(a, b, in_sem.at[n]) for n, (a, b) in enumerate(zip(sources, targets))]
    for load in loads:
        load.start()

    barrier = pltpu.get_barrier_semaphore()

    def greet(n, _):
        k = CELLS - 1 - n
        c = cell_at(k, 1)
        for step in (-1, 0, 1):
            if step:
                pl.semaphore_signal(barrier, inc=1, device_id=(strip_at(step), c), device_id_type=MESH)
            else:
                @pl.when(k > 0)
                def _():
                    pl.semaphore_signal(barrier, inc=1, device_id=(strip_at(0), c), device_id_type=MESH)
        return 0

    lax.fori_loop(0, CELLS, greet, 0)
    for load in loads:
        load.wait()

    left[...] = dot(feat[...], w_left[...]).astype(BF16)
    tables[1] = dot(feat[...], w_right[...]).astype(BF16)

    entry_out[...] = jnp.zeros_like(entry_out)
    for n in range(FAR_CELLS):
        entry_out[n, 0:1, 0:FETCH] = lists[pl.ds(cell_at(NEAR_CELLS + n, -1), 1), :].astype(F32)
    square[...] = jnp.zeros_like(square)
    square[0:32, 0:FETCH] = lists[...].astype(F32)
    list_t[...] = square[...].T
    for o in range(3):
        list_s[pl.ds(o * PART, PART), :] = list_t[pl.ds(o, PART, stride=3), :] - float(o * D)

    def pick(o, i):
        index = jnp.concatenate(
            [column(list_s[pl.ds(pl.multiple_of(o * PART, PART), PART), :], cell_at(8 * i + h, 1)) for h in range(8)], axis=0
        )
        picked = dot(one_hot(index, D), tables[o]).astype(BF16)
        rows_out[o, pl.ds(pl.multiple_of(i * 8 * PART, 128), 8 * PART), :] = picked

    def pick_own(i, _):
        pick(1, i)
        return 0

    lax.fori_loop(0, CELLS // 8, pick_own, 0)

    def place(j, total):
        left_parts, right_parts = [], []
        for h in range(2):
            at = pl.ds(2 * j + h, 1)
            t = slot[at, :]
            d = dist[at, :]
            d_hi = d.astype(BF16).astype(F32)
            d_mid = (d - d_hi).astype(BF16).astype(F32)
            d_lo = d - d_hi - d_mid
            index = row_index(t, prow[at, :]) - FETCH * (lax.shift_right_logical(t, 6) & (CELLS - 1))
            hit = lax.broadcasted_iota(jnp.int32, (SLOT, 128), 0) == (t & (SLOT - 1))
            parts = (d_hi, d_mid, d_lo, (atom[at, :] + 1).astype(F32), index.astype(F32))
            left_parts.append(jnp.concatenate([jnp.where(hit, v, 0.0) for v in parts], axis=0))
            group = lax.broadcasted_iota(jnp.int32, (128, 128), 0) == lax.shift_right_logical(t, 6)
            right_parts.append(jnp.where(group, 1.0, 0.0))
        return total + dot_nt(
            jnp.concatenate(left_parts, axis=1).astype(BF16), jnp.concatenate(right_parts, axis=1).astype(BF16)
        )

    total = lax.fori_loop(0, PAIRS // 256, place, jnp.zeros((5 * SLOT, 128), F32))
    d = total[0:SLOT] + total[SLOT:2 * SLOT] + total[2 * SLOT:3 * SLOT]
    slot_d[...] = d
    slot_e[...] = envelope_of(d)
    slot_a[...] = total[3 * SLOT:4 * SLOT] - 1.0
    slot_m[...] = total[4 * SLOT:5 * SLOT]
    turn_a[...] = jnp.concatenate([d, total[3 * SLOT:4 * SLOT] - 1.0], axis=0).T
    turn_b[...] = jnp.concatenate([total[4 * SLOT:5 * SLOT], jnp.zeros((SLOT, 128), F32)], axis=0).T

    def pack_scalars(n, _):
        c = cell_at(NEAR_CELLS + n, -1)
        for o in range(3):
            scal_out[3 * n + o, 0:1, :] = turn_a[pl.ds(o * CELLS + c, 1), :]
            scal_out[3 * n + o, 1:2, :] = turn_b[pl.ds(o * CELLS + c, 1), :]
        return 0

    lax.fori_loop(0, FAR_CELLS, pack_scalars, 0)

    pl.semaphore_wait(barrier, 3 * CELLS - 1)

    def feature_copy(which):
        return pltpu.make_async_remote_copy(
            src_ref=feat, dst_ref=feat_in.at[which], send_sem=feat_ss.at[which], recv_sem=feat_rs.at[which],
            device_id=(strip_at(1 - 2 * which), me), device_id_type=MESH,
        )

    def row_copy(k, o, sender):
        return pltpu.make_async_remote_copy(
            src_ref=rows_out.at[o, pl.ds(pl.multiple_of(k * PART, PART), PART)],
            dst_ref=rows_in.at[pl.ds(pl.multiple_of(me * FETCH + o * PART, PART), PART)],
            send_sem=rows_ss.at[o], recv_sem=rows_rs.at[sender, o],
            device_id=(strip_at(0), cell_at(k, 1)), device_id_type=MESH,
        )

    def own_rows(o):
        return pltpu.make_async_copy(
            rows_out.at[o, pl.ds(0, PART)], rows_in.at[pl.ds(pl.multiple_of(me * FETCH + o * PART, PART), PART)], local_sem.at[o]
        )

    def send_rows_of(o, i):
        for h in range(8):
            if h >= NEAR_CELLS % 8:
                @pl.when(i < CELLS // 8 - 1)
                def _():
                    row_copy(8 * i + h, o, me).start()
            elif h:
                row_copy(8 * i + h, o, me).start()
            else:
                @pl.when(i == 0)
                def _():
                    own_rows(o).start()

                @pl.when(i > 0)
                def _():
                    row_copy(8 * i, o, me).start()

    def list_copy(which):
        return pltpu.make_async_remote_copy(
            src_ref=lists, dst_ref=list_in.at[which], send_sem=list_ss.at[which], recv_sem=list_rs.at[which],
            device_id=(strip_at(1 - 2 * which), me), device_id_type=MESH,
        )

    def far_step(b, dx):
        return NEAR_CELLS + b * X + dx

    def hop_copy(b):
        return pltpu.make_async_remote_copy(
            src_ref=feat, dst_ref=far_f.at[1, b * X], send_sem=hop_ss.at[b], recv_sem=hop_rs.at[b],
            device_id=(strip_at(0), cell_at(far_step(b, 0), -1)), device_id_type=MESH,
        )

    def side_copy(b, dx):
        return pltpu.make_async_remote_copy(
            src_ref=far_f.at[1, b * X], dst_ref=far_f.at[1, b * X + dx],
            send_sem=side_ss.at[b, dx - 1], recv_sem=side_rs.at[b, dx - 1],
            device_id=(strip_at(0), cell_at(dx * NEAR, -1)), device_id_type=MESH,
        )

    def near_copy(n, which):
        return pltpu.make_async_remote_copy(
            src_ref=far_f.at[1, n], dst_ref=far_f.at[2 * which, n],
            send_sem=near_ss.at[which], recv_sem=near_rs.at[n, which],
            device_id=(strip_at(1 - 2 * which), me), device_id_type=MESH,
        )

    def scalar_copy(n, o):
        k = far_step(lax.div(n, X), lax.rem(n, X))
        return pltpu.make_async_remote_copy(
            src_ref=scal_out.at[3 * n + o], dst_ref=scal_in.at[3 * n + o],
            send_sem=scal_ss.at[0], recv_sem=scal_rs.at[n, o],
            device_id=(strip_at(o - 1), cell_at(k, -1)), device_id_type=MESH,
        )

    def entry_copy(n):
        return pltpu.make_async_remote_copy(
            src_ref=entry_out.at[n], dst_ref=entry_in.at[n], send_sem=entry_ss.at[n], recv_sem=entry_rs.at[n],
            device_id=(strip_at(0), cell_at(NEAR_CELLS + n, -1)), device_id_type=MESH,
        )

    for which in range(2):
        feature_copy(which).start()
        list_copy(which).start()
    for n in range(FAR_CELLS):
        entry_copy(n).start()
    for b in range(FAR):
        hop_copy(b).start()

    def send_own_part(i, _):
        send_rows_of(1, i)
        return 0

    lax.fori_loop(0, CELLS // 8, send_own_part, 0)

    def near_step(n):
        return n

    def slot_columns(source, i):
        cells = [cell_at(near_step(WIDE * i + h), -1) for h in range(WIDE)]
        return jnp.concatenate([column(source[...], o * CELLS + c) for o in range(3) for c in cells], axis=0)

    def slot_gates(i, _):
        gate_s[pl.ds(pl.multiple_of(i * SPAN, 128), SPAN), :] = gate_of(
            slot_columns(slot_d, i), slot_columns(slot_e, i), w_rin[...], w_rout[...]
        )
        return 0

    early = EARLY
    lax.fori_loop(0, early, slot_gates, 0)

    for which in range(2):
        feature_copy(which).wait()
        tables[2 * which] = dot(feat_in[which], w_right[...]).astype(BF16)

    def rest(i):
        return 2 * lax.rem(i, 2), lax.div(i, 2)

    def pick_rest(i, _):
        pick(*rest(i))

        @pl.when(i > 0)
        def _():
            send_rows_of(*rest(i - 1))
        return 0

    lax.fori_loop(0, CELLS // 4, pick_rest, 0)
    lax.fori_loop(early, early + 1, slot_gates, 0)
    send_rows_of(2, CELLS // 8 - 1)
    def send_scalars(n, _):
        for o in range(3):
            scalar_copy(n, o).start()
        return 0

    lax.fori_loop(0, FAR_CELLS, send_scalars, 0)
    for which in range(2):
        list_copy(which).wait()
        square[0:32, 0:FETCH] = list_in[which].astype(F32)
        list_t[...] = square[...].T
        list_n[which] = list_t[pl.ds(2 - 2 * which, PART, stride=3), :] - float((2 - 2 * which) * D)
    lax.fori_loop(early + 1, NEAR_CELLS // WIDE, slot_gates, 0)

    def block_copy(k, o, sender):
        return pltpu.make_async_remote_copy(
            src_ref=blk_out.at[k, o], dst_ref=blk_in.at[o * CELLS + me],
            send_sem=blk_ss.at[k, o], recv_sem=blk_rs.at[sender, o],
            device_id=(strip_at(o - 1), cell_at(k, -1)), device_id_type=MESH,
        )

    own_block = pltpu.make_async_copy(blk_out.at[0, 1], blk_in.at[CELLS + me], local_sem.at[3])

    def send_blocks_of(i):
        for h in range(WIDE):
            for o in range(3):
                if h or o != 1:
                    block_copy(near_step(WIDE * i + h), o, me).start()
                else:
                    @pl.when(i == 0)
                    def _():
                        own_block.start()

                    @pl.when(i > 0)
                    def _():
                        block_copy(near_step(WIDE * i), 1, me).start()

    low = lax.broadcasted_iota(jnp.int32, (HALF, 128), 1) < SLOT

    def halves(out, o, h):
        start = (o * WIDE + h) * SLOT
        top = out[0:HALF, start:start + 128]
        bottom = out[HALF:2 * HALF, start:start + 128]
        return (
            jnp.where(low, top, pltpu.roll(bottom, SLOT, 1)).astype(BF16),
            jnp.where(low, pltpu.roll(top, SLOT, 1), bottom).astype(BF16),
        )

    def slots(i, _):
        cells = [cell_at(near_step(WIDE * i + h), -1) for h in range(WIDE)]
        for o in range(3):
            @pl.when(i == 0)
            def _():
                own_rows(o).wait()

            @pl.when(i > 0)
            def _():
                row_copy(near_step(WIDE * i), o, cells[0]).wait_recv()
            for h in range(1, WIDE):
                row_copy(near_step(WIDE * i + h), o, cells[h]).wait_recv()
        rows = jnp.concatenate([rows_in[pl.ds(pl.multiple_of(c * FETCH, PART), FETCH), :] for c in cells], axis=0)
        second = lax.rem(lax.div(lax.broadcasted_iota(jnp.int32, (SPAN, 1), 0), SLOT), WIDE) * FETCH
        left_rows = dot(one_hot(slot_columns(slot_a, i), D), left[...])
        right_rows = dot(one_hot(slot_columns(slot_m, i) + second.astype(F32), WIDE * FETCH), rows)
        gate = gate_s[pl.ds(pl.multiple_of(i * SPAN, 128), SPAN), :]
        edge = (left_rows * right_rows * gate).astype(BF16)
        mixed = silu(dot(edge, w_mix[...])).astype(BF16)
        out = dot_nt(w_flip[...], mixed)
        for o in range(3):
            for h in range(0, WIDE, 2):
                first, second = halves(out, o, h)
                blk_out[near_step(WIDE * i + h), o] = first
                blk_out[near_step(WIDE * i + h + 1), o] = second

        @pl.when(i > 0)
        def _():
            send_blocks_of(i - 1)
        return 0

    entry = lax.broadcasted_iota(jnp.int32, (2 * HALF, D), 0)
    lane = lax.broadcasted_iota(jnp.int32, (2 * HALF, D), 1)
    quotient = lax.shift_right_logical(entry * 79, 10)
    flipped = (entry - quotient * ORB) * ORB + quotient
    w_out[...] = jnp.zeros_like(w_out)
    w_out[0:BLOCK, :] = w_raw[...]
    w_own[...] = w_out[0:2 * HALF, :]
    w_flip[...] = dot(jnp.where((entry < BLOCK) & (lane == flipped), 1.0, 0.0).astype(BF16), w_out[...]).astype(BF16)

    def to_sides(b):
        hop_copy(b).wait_recv()
        for dx in range(1, X):
            side_copy(b, dx).start()
        for which in range(2):
            near_copy(b * X, which).start()

    def to_strips(b):
        for dx in range(1, X):
            side_copy(b, dx).wait_recv()
            for which in range(2):
                near_copy(b * X + dx, which).start()


    for b in range(FAR):
        to_sides(b)
    lax.fori_loop(0, NEAR_CELLS // WIDE, slots, 0)

    index = row_index(slot[...], prow[...])
    for source, target in ((dist[...], pair_d), (envelope_of(dist[...]), pair_e), (atom[...].astype(F32), pair_a), (index.astype(F32), pair_r)):
        square[0:32, :] = source
        target[...] = square[...].T


    send_blocks_of(NEAR_CELLS // WIDE - 1)
    for b in range(FAR):
        to_strips(b)

    def pair_gates(j, _):
        d = jnp.concatenate([column(pair_d[...], 2 * j + h) for h in range(2)], axis=0)
        e = jnp.concatenate([column(pair_e[...], 2 * j + h) for h in range(2)], axis=0)
        gate_o[pl.ds(pl.multiple_of(j * 256, 256), 256), :] = gate_of(d, e, w_rin[...], w_rout[...])
        return 0

    lax.fori_loop(0, PAIRS // 256, pair_gates, 0, unroll=4)

    for n in range(FAR_CELLS):
        entry_copy(n).wait()
        square[n:n + 1, :] = entry_in[n, 0:1, :]
        for which in range(2):
            near_copy(n, which).wait_recv()
    list_t[...] = square[...].T
    spans = [list_t[pl.ds(o, PART, stride=3), :] - float(o * D) for o in range(3)]
    chosen = jnp.concatenate(
        [dot(one_hot(spans[o][:, n:n + 1], D), far_f[o, n]).astype(BF16) for n in range(FAR_CELLS) for o in range(3)], axis=0
    )
    chosen = dot(chosen, w_right[...]).astype(BF16)
    for n in range(FAR_CELLS):
        rows_in[pl.ds(pl.multiple_of(cell_at(NEAR_CELLS + n, 1) * FETCH, PART), FETCH), :] = chosen[n * FETCH:(n + 1) * FETCH]


    def pairs(j, _):
        index_l = jnp.concatenate([column(pair_a[...], 2 * j + h) for h in range(2)], axis=0)
        index_r = jnp.concatenate([column(pair_r[...], 2 * j + h) for h in range(2)], axis=0)
        left_rows = dot(one_hot(index_l, D), left[...])
        right_rows = dot(one_hot(index_r, CELLS * FETCH), rows_in[...])
        at = pl.ds(pl.multiple_of(j * 256, 256), 256)
        edge = (left_rows * right_rows * gate_o[at, :]).astype(BF16)
        mixed = silu(dot(edge, w_mix[...])).astype(BF16)
        own[:, at] = dot_nt(w_own[...], mixed)[0:BLOCK].astype(BF16)
        return 0

    def pairs_of(i, _):
        for h in range(4):
            pairs(4 * i + h, 0)

        return 0

    lax.fori_loop(0, PAIRS // 1024, pairs_of, 0)

    own_block.wait()
    block_copy(0, 0, me).wait()
    block_copy(0, 2, me).wait()
    parity = lax.rem(me, 2)

    def unpack(n, _):
        o = lax.rem(n, 3)
        x = lax.rem(lax.div(n, 12) + lax.div(me, Z), X)
        rank = lax.rem(lax.div(n, 3), X)
        middle = lax.div(rank + 2, 3) * (1 + 2 * lax.rem(rank + parity, 2))
        shift = lax.rem(middle * lax.div(3 - rank + 2, 3) + 2 * lax.div(rank, 3), 4)
        even = x * Z + 2 * lax.rem(lax.div(lax.rem(me, Z), 2) + shift, 4)
        for h in range(2):
            away = lax.rem(lax.rem(even, Z) + h - lax.rem(me, Z) + Z + NEAR // 2, Z)

            @pl.when((even + h != me) & (away < NEAR))
            def _():
                block_copy(0, o, even + h).wait_recv()
        base = o * CELLS + even
        first = blk_in[base].astype(F32)
        second = blk_in[base + 1].astype(F32)
        top = jnp.where(low, first, pltpu.roll(second, SLOT, 1))
        bottom = jnp.where(low, pltpu.roll(first, SLOT, 1), second)
        partner[:, pl.ds(pl.multiple_of(base * SLOT, 128), 128)] = jnp.concatenate([top, bottom], axis=0)[0:BLOCK].astype(BF16)
        return 0

    def far(b, _):
        groups = [(o, dx) for o in range(3) for dx in range(X)]
        cells = [cell_at(far_step(b, dx), 1) for dx in range(X)]
        for g, (o, dx) in enumerate(groups):
            scalar_copy(b * X + dx, o).wait_recv()
            turn_a[g:g + 1, :] = scal_in[3 * (b * X + dx) + o, 0:1, :]
            turn_b[g:g + 1, :] = scal_in[3 * (b * X + dx) + o, 1:2, :]
        square[0:16, :] = envelope_of(turn_a[0:16, :])
        values, places, envelopes = turn_a[...].T, turn_b[...].T, square[...].T
        d = jnp.concatenate([values[0:SLOT, g:g + 1] for g in range(12)], axis=0)
        e = jnp.concatenate([envelopes[0:SLOT, g:g + 1] for g in range(12)], axis=0)
        m = jnp.concatenate([places[0:SLOT, g:g + 1] + float((g - o) * PART) for g, (o, dx) in enumerate(groups)], axis=0)
        gate = gate_of(d, e, w_rin[...], w_rout[...])
        entries = (list_n[1], list_s[PART:2 * PART, :], list_n[0])
        index = jnp.concatenate([column(entries[o], cells[dx]) for o, dx in groups], axis=0)
        rows = dot(one_hot(index, D), tables[1]).astype(BF16)
        right_rows = dot(one_hot(m, 12 * PART), rows)
        picked = jnp.concatenate(
            [dot(one_hot(values[SLOT:2 * SLOT, g:g + 1], D), far_f[2 - o, b * X + dx]).astype(BF16) for g, (o, dx) in enumerate(groups)], axis=0
        )
        left_rows = dot(picked, w_left[...]).astype(BF16).astype(F32)
        edge = (left_rows * right_rows * gate).astype(BF16)
        mixed = silu(dot(edge, w_mix[...])).astype(BF16)
        out = dot_nt(w_flip[...], mixed)
        for o in range(3):
            for h in range(0, X, 2):
                first, second = halves(out, o, h)
                blk_in[o * CELLS + cells[h]] = first
                blk_in[o * CELLS + cells[h + 1]] = second
        return 0

    lax.fori_loop(0, FAR, far, 0)
    lax.fori_loop(0, GROUPS // 2, unpack, 0, unroll=2)

    sent = []
    for o in range(3):
        sent.append((rows_out.at[o, pl.ds(PART, (NEAR_CELLS - 1) * PART)], rows_in.at[pl.ds(0, (NEAR_CELLS - 1) * PART)], rows_ss.at[o], rows_rs.at[0, o]))
    for which in range(2):
        sent.append((far_f.at[1], far_f.at[2 * which], near_ss.at[which], near_rs.at[0, which]))
    sent.append((scal_out, scal_in, scal_ss.at[0], scal_rs.at[0, 0]))
    for source, target, send_sem, recv_sem in sent:
        pltpu.make_async_remote_copy(
            src_ref=source, dst_ref=target, send_sem=send_sem, recv_sem=recv_sem,
            device_id=(strip_at(1), me), device_id_type=MESH,
        ).wait_send()

    def finish_blocks(n, _):
        for o in range(3):
            block_copy(near_step(n), o, me).wait_send()
        return 0

    lax.fori_loop(1, NEAR_CELLS, finish_blocks, 0)

    for b in range(FAR):
        hop_copy(b).wait_send()
        for dx in range(1, X):
            side_copy(b, dx).wait_send()


def output_kernel(own_in, partner_in, own, partner, sem):
    copies = [pltpu.make_async_copy(own_in, own, sem.at[0]), pltpu.make_async_copy(partner_in, partner, sem.at[1])]
    for copy in copies:
        copy.start()
    for copy in copies:
        copy.wait()


def body(features, pair_atom, partner_row, transpose_slot, distance, send_rows, w_left, w_right, w_radial_in, w_radial_out, w_mix, w_out):
    vmem = pl.BlockSpec(memory_space=pltpu.VMEM)
    hbm = pl.BlockSpec(memory_space=pltpu.HBM)
    sem = pltpu.SemaphoreType.DMA
    outputs = (
        jax.ShapeDtypeStruct((BLOCK, PAIRS), BF16),
        jax.ShapeDtypeStruct((BLOCK, GROUPS * SLOT), BF16),
    )
    own, partner = pl.pallas_call(
        main_kernel,
        out_shape=outputs,
        in_specs=[hbm] * 12,
        out_specs=(vmem, vmem),
        scratch_shapes=[
            pltpu.VMEM((D, D), BF16),
            *[pltpu.VMEM((32, 128), jnp.int32)] * 3,
            pltpu.VMEM((32, 128), F32),
            pltpu.VMEM((CELLS, FETCH), jnp.int32),
            pltpu.VMEM((D, D), BF16),
            pltpu.VMEM((D, D), BF16),
            pltpu.VMEM((COUNT, D), BF16),
            pltpu.VMEM((D, D), BF16),
            pltpu.VMEM((D, D), BF16),
            pltpu.VMEM((BLOCK, D), BF16),
            pltpu.VMEM((D, D), BF16),
            pltpu.VMEM((2, D, D), BF16),
            pltpu.VMEM((2, CELLS, FETCH), jnp.int32),
            pltpu.VMEM((3, FAR_CELLS, D, D), BF16),
            pltpu.VMEM((3 * FAR_CELLS, 2, 128), F32),
            pltpu.VMEM((3 * FAR_CELLS, 2, 128), F32),
            pltpu.VMEM((FAR_CELLS, 2, 128), F32),
            pltpu.VMEM((FAR_CELLS, 2, 128), F32),
            pltpu.VMEM((3, D, D), BF16),
            pltpu.VMEM((D, D), BF16),
            pltpu.VMEM((3, CELLS * PART, D), BF16),
            pltpu.VMEM((CELLS * FETCH, D), BF16),
            pltpu.VMEM((GROUPS * SLOT, D), F32),
            pltpu.VMEM((PAIRS, D), F32),
            pltpu.VMEM((CELLS, 3, HALF, 128), BF16),
            pltpu.VMEM((GROUPS, HALF, 128), BF16),
            *[pltpu.VMEM((SLOT, 128), F32)] * 4,
            *[pltpu.VMEM((128, 128), F32)] * 5,
            pltpu.VMEM((FETCH, 128), F32),
            pltpu.VMEM((2, PART, 128), F32),
            *[pltpu.VMEM((128, 128), F32)] * 3,
            pltpu.VMEM((2 * HALF, D), BF16),
            pltpu.VMEM((2 * HALF, D), BF16),
            sem((12,)), *[sem((2,))] * 4, *[sem((FAR,))] * 2, *[sem((FAR, X - 1))] * 2,
            sem((2,)), sem((FAR_CELLS, 2)), sem((1,)), sem((FAR_CELLS, 3)), sem((FAR_CELLS,)), sem((FAR_CELLS,)), sem((3,)), sem((CELLS, 3)), sem((CELLS, 3)), sem((CELLS, 3)), sem((4,)),
        ],
        compiler_params=pltpu.CompilerParams(collective_id=0, has_side_effects=True, vmem_limit_bytes=48 << 20),
    )(*[pltpu.with_memory_space_constraint(a, pltpu.HBM) for a in (
        features,
        pair_atom.reshape(32, 128),
        partner_row.reshape(32, 128),
        transpose_slot.reshape(32, 128),
        distance.reshape(32, 128),
        send_rows, w_left, w_right, w_radial_in, w_radial_out, w_mix, w_out.T,
    )])
    return pl.pallas_call(
        output_kernel,
        out_shape=outputs,
        in_specs=[vmem, vmem],
        out_specs=(hbm, hbm),
        scratch_shapes=[sem((2,))],
        compiler_params=pltpu.CompilerParams(vmem_limit_bytes=16 << 20),
    )(own, partner)


def solution(mesh):
    both = P(("strip", "cell"))
    rows = P(("strip", "cell"), None)
    in_specs = (rows, both, both, both, both, rows, P(), P(), P(), P(), P(), P())
    out_specs = (P(None, ("strip", "cell")), P(None, ("strip", "cell")))
    return jax.shard_map(body, mesh=mesh, in_specs=in_specs, out_specs=out_specs, check_vma=False)
```
